128 devices in a mesh: tm: 4 (over z), ent: 32 (over x, y, core).
Axes of the slice: x: 4, y: 4, z: 4, core: 2. Of those that a mesh axis runs over, the one named last changes fastest.
Arguments:
- states: bfloat16 [4, 32768, 512], P('tm', 'ent'), may hold values from -6 to 6
- cotangent: bfloat16 [4, 32768, 512], P('tm', 'ent'), may hold values from -6 to 6
- export_rows: int32 [4, 32768], P('tm', 'ent'), may hold values from 0 to 1023
- edge_src: int32 [4, 32768], P('tm', 'ent'), may hold values from 0 to 1023
- edge_dst: int32 [4, 32768], P('tm', 'ent'), may hold values from 0 to 1023
- edge_rel: int32 [4, 32768], P('tm', 'ent'), may hold values from 0 to 255
- tile_count: int32 [4, 32], P('tm', 'ent'), may hold values from 1 to 8, as said below
- basis: bfloat16 [512, 2048], replicated, may hold values from -0.25 to 0.25
- coef: float32 [256, 4], replicated, may hold values from -3 to 3
- rel_emb: bfloat16 [256, 512], replicated, may hold values from -3 to 3
- self_weight: bfloat16 [512, 512], replicated, may hold values from -0.25 to 0.25
- gate_weight: bfloat16 [512, 512], replicated, may hold values from -0.25 to 0.25
- gate_bias: float32 [512], replicated, may hold values from -2 to 1
Outputs:
- grad_states: float32 [4, 32768, 512], P('tm', 'ent')
- grad_basis: float32 [512, 2048], P('ent')
- grad_self: float32 [512, 512], P('ent')
- grad_gate: float32 [512, 512], P('ent')
- grad_gate_bias: float32 [512], P('ent')
- grad_coef: float32 [256, 4], P('ent')
- grad_rel_emb: float32 [256, 512], P('ent')
The draws below stay inside these ranges and needn't reach their ends.
Inputs may be any that keep to these rules, and one draw needn't show every extreme that they name: `tile_count`: some slab of some snapshot has 8 live tiles in every draw.
All inputs are finite; a program needn't handle non-finite values.
Results may differ from the reference program's by a relative error of at most 0.01.
Values may be sent and summed in bfloat16 or wider, within the bound.
A program may use at most 128 MiB of HBM per device.

```python
import math
import jax
import jax.numpy as jnp
import numpy as np

D = 512
NREL = 256
NB = 4
TILE = 128
ROWS_DEV = 1024
TILES = 8
CAP = 32
SNAPS = 4
ENTITIES = 32768
SLOTS = 1024
EDGES_DEV = 1024
N_ENT = 32


def draw_tile_count(key, part):
    key_first = jax.random.fold_in(key, 11)
    key_second = jax.random.fold_in(key, 12)
    key_third = jax.random.fold_in(key, 13)
    first_draw = jax.random.randint(key_first, (SNAPS * N_ENT,), 1, TILES + 1)
    second_draw = jax.random.randint(key_second, (SNAPS * N_ENT,), 1, TILES + 1)
    flat_counts = jnp.minimum(first_draw, second_draw)
    full_place = jax.random.randint(key_third, (), 0, SNAPS * N_ENT)
    flat_counts = jnp.where(jnp.arange(SNAPS * N_ENT) == full_place, TILES, flat_counts)
    return flat_counts.reshape(SNAPS, N_ENT).astype(jnp.int32)


def plant(array, own_key, smallest, high):
    longest = array.shape.index(max(array.shape))
    spots = []
    for shift in (0, 1):
        where = [jax.random.randint(jax.random.fold_in(own_key, axis), (), 0, length) for axis, length in enumerate(array.shape)]
        where[longest] = (where[longest] + shift) % array.shape[longest]
        spots.append(tuple(where))
    return array.at[spots[0]].set(smallest).at[spots[1]].set(high)


def shard_levels(stream_key, shape, shards, smallest, high):
    def one(axis_at, blocks):
        steps = jax.random.uniform(jax.random.fold_in(jax.random.fold_in(stream_key, 6), axis_at), (blocks,), jnp.float32, smallest / len(shards), high / len(shards))
        return jnp.repeat(jnp.exp(steps), shape[axis_at] // blocks).reshape((-1,) + (1,) * (len(shape) - axis_at - 1))

    factor_of = one(*shards[0])
    for cut in shards[1:]:
        factor_of = factor_of * one(*cut)
    return factor_of


def rank_bounds(number_of, skew):
    portions = [(1 << 20) // math.isqrt(standing ** skew) + 1 for standing in range(1, number_of + 1)]
    spread = 1 + sum(portions) // (1 << 30)
    return np.cumsum(np.array([max(1, weight // spread) for weight in portions]))


def ranked_ids(key, shape, amount, skew):
    table = rank_bounds(amount, skew)
    ticket = jax.random.randint(jax.random.fold_in(key, 1), shape, 0, int(table[amount - 1]))
    standing = jnp.searchsorted(jnp.asarray(table, jnp.int32), ticket, side="right")
    return jax.random.permutation(jax.random.fold_in(key, 2), amount)[standing].astype(jnp.int32)


def gaussian(stream_key, extent, scale, limit, split=(), kind=jnp.bfloat16):
    entries = jax.random.normal(stream_key, extent, jnp.float32) * scale
    if len(split) > 0:
        entries = shard_levels(stream_key, extent, split, -0.22, 0.18) * entries
    return jnp.clip(entries, min=-limit, max=limit).astype(kind)


def setup_inputs(seed: int = 0) -> dict:
    streams_of = jax.random.split(jax.random.key(seed), 14)
    return {
        "states": gaussian(streams_of[0], (SNAPS, ENTITIES, D), 1.0, 6.0, ((0, 4), (1, 32))),
        "cotangent": gaussian(streams_of[1], (SNAPS, ENTITIES, D), 1.0, 6.0, ((0, 4), (1, 32))),
        "export_rows": plant(jax.random.randint(streams_of[2], (SNAPS, N_ENT * SLOTS), 0, ROWS_DEV), jax.random.fold_in(streams_of[2], 1), 0, ROWS_DEV - 1).astype(jnp.int32),
        "edge_src": plant(jax.random.randint(streams_of[3], (SNAPS, N_ENT * EDGES_DEV), 0, SLOTS), jax.random.fold_in(streams_of[3], 1), 0, SLOTS - 1).astype(jnp.int32),
        "edge_dst": plant(jax.random.randint(streams_of[4], (SNAPS, N_ENT * EDGES_DEV), 0, ROWS_DEV), jax.random.fold_in(streams_of[4], 1), 0, ROWS_DEV - 1).astype(jnp.int32),
        "edge_rel": plant(ranked_ids(streams_of[5], (SNAPS, N_ENT * EDGES_DEV), NREL, 2), jax.random.fold_in(streams_of[5], 3), 0, NREL - 1).astype(jnp.int32),
        "tile_count": draw_tile_count(jax.random.fold_in(streams_of[13], 71), 0),
        "basis": gaussian(streams_of[7], (D, NB * D), D ** -0.5, 0.25),
        "coef": gaussian(streams_of[8], (NREL, NB), 0.5, 3.0, (), jnp.float32),
        "rel_emb": gaussian(streams_of[9], (NREL, D), 0.5, 3.0),
        "self_weight": gaussian(streams_of[10], (D, D), D ** -0.5, 0.25),
        "gate_weight": gaussian(streams_of[11], (D, D), D ** -0.5, 0.25),
        "gate_bias": jnp.clip(jax.random.uniform(streams_of[12], (D,), jnp.float32, -2.0, 1.0), -2.0, 1.0),
    }


def reference(states, cotangent, export_rows, edge_src, edge_dst, edge_rel, tile_count, basis, coef, rel_emb, self_weight, gate_weight, gate_bias):
    edge_total = N_ENT * EDGES_DEV
    positions = jnp.arange(edge_total, dtype=jnp.int32)
    device_of = (positions // EDGES_DEV).astype(jnp.int32)
    handed = jnp.zeros((ENTITIES, D), jnp.bfloat16)
    basis_sum = jnp.zeros((D, NB * D), jnp.float32)
    self_sum = jnp.zeros((D, D), jnp.float32)
    gate_sum = jnp.zeros((D, D), jnp.float32)
    bias_sum = jnp.zeros((D,), jnp.float32)
    coef_sum = jnp.zeros((NREL, NB), jnp.float32)
    relation_sum = jnp.zeros((NREL, D), jnp.float32)
    grad_list = []
    for snapshot in range(SNAPS - 1, -1, -1):
        own_state = states[snapshot]
        owner = (edge_src[snapshot] // CAP).astype(jnp.int32)
        entry_slot = (edge_src[snapshot] % CAP).astype(jnp.int32)
        local_row = export_rows[snapshot][owner * (N_ENT * CAP) + device_of * CAP + entry_slot]
        source = (owner * ROWS_DEV + local_row).astype(jnp.int32)
        target = (device_of * ROWS_DEV + edge_dst[snapshot]).astype(jnp.int32)
        live_mask = ((positions % EDGES_DEV) // TILE) < tile_count[snapshot][device_of]
        relation = edge_rel[snapshot]
        edge_input = (own_state[source].astype(jnp.float32) + rel_emb[relation].astype(jnp.float32)).astype(jnp.bfloat16)
        images = jnp.dot(edge_input, basis, preferred_element_type=jnp.float32).reshape(edge_total, NB, D)
        edge_coef = coef[relation].astype(jnp.float32)
        message = jnp.einsum("eb,ebd->ed", edge_coef, images)
        message = jnp.where(live_mask[:, None], message, jnp.zeros((), jnp.float32))
        degree = 1.0 + jax.ops.segment_sum(live_mask.astype(jnp.float32), target, ENTITIES)
        self_part = jnp.dot(own_state, self_weight, preferred_element_type=jnp.float32)
        summed = (jax.ops.segment_sum(message, target, ENTITIES) + self_part) / degree[:, None]
        aggregated = jnp.tanh(summed)
        gate_open = jax.nn.sigmoid(jnp.dot(own_state, gate_weight, preferred_element_type=jnp.float32) + gate_bias)
        upstream = cotangent[snapshot].astype(jnp.float32) + handed.astype(jnp.float32)
        row_grad = (upstream * gate_open * (1.0 - aggregated * aggregated) / degree[:, None]).astype(jnp.bfloat16)
        gate_grad = upstream * (aggregated - own_state.astype(jnp.float32)) * gate_open * (1.0 - gate_open)
        gate_row = gate_grad.astype(jnp.bfloat16)
        edge_grad = jnp.where(live_mask[:, None], row_grad[target], jnp.zeros((), jnp.bfloat16))
        image_grad = (edge_coef[:, :, None] * edge_grad.astype(jnp.float32)[:, None, :]).astype(jnp.bfloat16).reshape(edge_total, NB * D)
        input_grad = jnp.dot(image_grad, basis.T, preferred_element_type=jnp.float32)
        state_grad = upstream * (1.0 - gate_open)
        state_grad = state_grad + jnp.dot(row_grad, self_weight.T, preferred_element_type=jnp.float32)
        state_grad = state_grad + jnp.dot(gate_row, gate_weight.T, preferred_element_type=jnp.float32)
        state_grad = state_grad + jax.ops.segment_sum(input_grad, source, ENTITIES)
        grad_list.append(state_grad)
        handed = state_grad.astype(jnp.bfloat16)
        basis_sum = basis_sum + jnp.dot(edge_input.T, image_grad, preferred_element_type=jnp.float32)
        self_sum = self_sum + jnp.dot(own_state.T, row_grad, preferred_element_type=jnp.float32)
        gate_sum = gate_sum + jnp.dot(own_state.T, gate_row, preferred_element_type=jnp.float32)
        bias_sum = bias_sum + jnp.sum(gate_grad, axis=0)
        coef_edge = jnp.einsum("ed,ebd->eb", edge_grad.astype(jnp.float32), images)
        coef_sum = coef_sum + jax.ops.segment_sum(coef_edge, relation, NREL)
        relation_sum = relation_sum + jax.ops.segment_sum(input_grad, relation, NREL)
    grad_states = jnp.stack(grad_list[::-1], axis=0)
    return (grad_states, basis_sum, self_sum, gate_sum, bias_sum, coef_sum, relation_sum)
```

```python
import jax
import jax.numpy as jnp
from jax import lax
from jax.sharding import PartitionSpec as P

TILE = 128
LAST = (((1,), (1,)), ((), ()))
FIRST = (((0,), (0,)), ((), ()))


def shifted(block, axis, distance):
    devices = range(lax.axis_size(axis))
    route = [(i - distance, i) for i in devices if i - distance in devices]
    return lax.ppermute(block, axis, route)


def dot(a, b, dims=(((1,), (0,)), ((), ()))):
    return lax.dot_general(a, b, dims, preferred_element_type=jnp.float32)


def onehot(ids, count):
    return ids[:, None] == jnp.arange(count, dtype=jnp.int32)[None, :]


def split_dot(hot, value):
    high = value.astype(jnp.bfloat16)
    low = (value - high.astype(jnp.float32)).astype(jnp.bfloat16)
    return dot(hot, high, FIRST) + dot(hot, low, FIRST)


def per_device(
    states, cotangent, export_rows, edge_src, edge_dst, edge_rel, tile_count,
    basis, coef, rel_emb, self_weight, gate_weight, gate_bias,
):
    bf16, f32 = jnp.bfloat16, jnp.float32
    ent_count = lax.axis_size("ent")
    section_count = lax.axis_size("tm")
    state = states[0]
    rows, width = state.shape
    basis_count = basis.shape[1] // width
    relations = rel_emb.shape[0]
    edges = edge_src.shape[1]
    slots = export_rows.shape[1]
    live = jnp.arange(edges, dtype=jnp.int32) // TILE < tile_count[0, 0]
    source = onehot(edge_src[0], slots).astype(bf16)
    target = (onehot(edge_dst[0], rows) & live[:, None]).astype(bf16)
    exported = onehot(export_rows[0], rows).astype(bf16)
    relation = onehot(edge_rel[0], relations).astype(bf16)

    received = lax.all_to_all(
        dot(exported, state).astype(bf16), "ent", split_axis=0, concat_axis=0, tiled=True
    )
    edge_input = (dot(source, received) + dot(relation, rel_emb)).astype(bf16)
    coef_high = coef.astype(bf16)
    coef_rest = coef - coef_high.astype(f32)
    coef_mid = coef_rest.astype(bf16)
    coef_low = (coef_rest - coef_mid.astype(f32)).astype(bf16)
    edge_coef = dot(relation, coef_high) + dot(relation, coef_mid) + dot(relation, coef_low)
    images = [
        dot(edge_input, basis[:, b * width : (b + 1) * width]) for b in range(basis_count)
    ]
    message = sum(edge_coef[:, b : b + 1] * images[b] for b in range(basis_count))
    degree = 1.0 + jnp.sum(target.astype(f32), axis=0)
    self_part = dot(state, self_weight)
    summed = (split_dot(target, message) + self_part) / degree[:, None]
    aggregated = jnp.tanh(summed)
    gate_open = jax.nn.sigmoid(dot(state, gate_weight) + gate_bias)
    keep = 1.0 - gate_open
    row_factor = gate_open * (1.0 - aggregated * aggregated) / degree[:, None]
    gate_factor = (aggregated - state.astype(f32)) * gate_open * keep

    handed = jnp.zeros((rows, width), bf16)
    for step in range(section_count):
        upstream = cotangent[0].astype(f32) + handed.astype(f32)
        row_grad = (upstream * row_factor).astype(bf16)
        gate_grad = upstream * gate_factor
        gate_row = gate_grad.astype(bf16)
        edge_grad = dot(target, row_grad)
        image_grad = [
            (edge_coef[:, b : b + 1] * edge_grad).astype(bf16) for b in range(basis_count)
        ]
        input_grad = sum(
            dot(image_grad[b], basis[:, b * width : (b + 1) * width], LAST)
            for b in range(basis_count)
        )
        slot_grad = dot(source, input_grad.astype(bf16), FIRST).astype(bf16)
        returned = lax.all_to_all(slot_grad, "ent", split_axis=0, concat_axis=0, tiled=True)
        state_grad = (
            upstream * keep
            + dot(row_grad, self_weight, LAST)
            + dot(gate_row, gate_weight, LAST)
            + dot(exported, returned, FIRST)
        )
        if step + 1 < section_count:
            handed = shifted(state_grad.astype(bf16), "tm", -1)

    coef_edge = jnp.stack(
        [jnp.sum(edge_grad * images[b], axis=1) for b in range(basis_count)], axis=1
    )
    small = jnp.concatenate(
        [
            jnp.sum(gate_grad, axis=0).reshape(ent_count, 1, width // ent_count),
            split_dot(relation, coef_edge).reshape(ent_count, 1, -1),
        ],
        axis=2,
    )
    small_width = small.shape[2]
    terms = [dot(edge_input, image_grad[b], FIRST) for b in range(basis_count)]
    terms += [dot(state, row_grad, FIRST), dot(state, gate_row, FIRST)]
    terms += [split_dot(relation, input_grad)]
    packed = jnp.concatenate(
        [term.reshape(ent_count, -1, width) for term in terms]
        + [jnp.pad(small, ((0, 0), (0, 7), (0, width - small_width)))],
        axis=1,
    )
    share = lax.psum_scatter(packed, "ent", scatter_dimension=0, tiled=False)
    share = lax.psum(share, "tm")
    height = width // ent_count
    top = basis_count * height
    return (
        state_grad[None],
        jnp.concatenate([share[b * height : (b + 1) * height] for b in range(basis_count)], axis=1),
        share[top : top + height],
        share[top + height : top + 2 * height],
        share[-8, :height],
        share[-8, height:small_width].reshape(relations // ent_count, basis_count),
        share[top + 2 * height : -8],
    )


def solution(mesh):
    placed = (P("tm", "ent", None),) * 2 + (P("tm", "ent"),) * 5 + (P(),) * 6
    return jax.shard_map(
        per_device,
        mesh=mesh,
        in_specs=placed,
        out_specs=(
            P("tm", "ent", None),
            P("ent", None),
            P("ent", None),
            P("ent", None),
            P("ent"),
            P("ent", None),
            P("ent", None),
        ),
        check_vma=False,
    )
```

```python
import jax
import jax.numpy as jnp
from jax import lax
from jax.experimental import pallas as pl
from jax.experimental.pallas import tpu as pltpu
from jax.sharding import PartitionSpec as P

TILE = 128
MESH = pl.DeviceIdType.MESH
CHUNKS = 2
BLOCK = 256
LAST = (((1,), (1,)), ((), ()))
FIRST = (((0,), (0,)), ((), ()))


def dot(a, b, dims=(((1,), (0,)), ((), ()))):
    return lax.dot_general(a, b, dims, preferred_element_type=jnp.float32)


def onehot(ids, count):
    return ids[:, None] == jnp.arange(count, dtype=jnp.int32)[None, :]


def split_dot(hot, value):
    high = value.astype(jnp.bfloat16)
    low = (value - high.astype(jnp.float32)).astype(jnp.bfloat16)
    return dot(hot, high, FIRST) + dot(hot, low, FIRST)


def chain_kernel(
    cot, row_factor, gate_factor, keep, target, source_t, exported_t, edge_coef,
    basis_t, self_t, gate_t,
    state_grad, row_grad, gate_row, edge_grad, input_grad,
    handed, sending, total, slot_send, slot_recv,
    z_send_sem, z_recv_sem, a_send_sem, a_recv_sem,
):
    bf16, f32 = jnp.bfloat16, jnp.float32
    t, me = lax.axis_index("tm"), lax.axis_index("ent")
    sections, ents = lax.axis_size("tm"), lax.axis_size("ent")
    rows, width = cot.shape
    edges, slots = target.shape[0], source_t.shape[0]
    share = slots // ents
    part = width // CHUNKS
    above = lax.rem(t + 1, sections)
    below = lax.rem(t + sections - 1, sections)

    barrier = pltpu.get_barrier_semaphore()

    def greet(k, carry):
        peer = lax.rem(me + k, ents)
        pl.semaphore_signal(barrier, inc=1, device_id=(t, peer), device_id_type=MESH)
        return carry

    lax.fori_loop(1, ents, greet, 0)
    pl.semaphore_signal(barrier, inc=1, device_id=(above, me), device_id_type=MESH)
    pl.semaphore_signal(barrier, inc=1, device_id=(below, me), device_id_type=MESH)
    pl.semaphore_wait(barrier, ents + 1)

    def pass_down(c):
        return pltpu.make_async_remote_copy(
            src_ref=sending.at[c],
            dst_ref=handed.at[c],
            send_sem=z_send_sem.at[c],
            recv_sem=z_recv_sem.at[c],
            device_id=(below, me),
            device_id_type=MESH,
        )

    def blocks(count, body):
        def step(i, carry):
            body(pl.ds(pl.multiple_of(i * BLOCK, BLOCK), BLOCK))
            return carry

        lax.fori_loop(0, count // BLOCK, step, 0)

    for c in range(CHUNKS):
        cols = pl.ds(c * part, part)

        @pl.when(t < sections - 1)
        def _():
            pass_down(c).wait_recv()

        @pl.when(t == sections - 1)
        def _():
            handed[c] = jnp.zeros((rows, part), bf16)

        def elementwise(r):
            upstream = cot[r, cols].astype(f32) + handed[c, r, :].astype(f32)
            row_grad[r, cols] = (upstream * row_factor[r, cols]).astype(bf16)
            gate_row[r, cols] = (upstream * gate_factor[r, cols]).astype(bf16)
            state_grad[r, cols] = upstream * keep[r, cols]

        blocks(rows, elementwise)

        def through_basis(e):
            gathered = dot(target[e, :], row_grad[:, cols])
            edge_grad[e, cols] = gathered.astype(bf16)
            out = 0.0
            for b in range(edge_coef.shape[1]):
                image_grad = (edge_coef[e, b : b + 1] * gathered).astype(bf16)
                out = out + dot(image_grad, basis_t[b, cols, :])
            if c > 0:
                out = out + total[e, :]
            if c < CHUNKS - 1:
                total[e, :] = out
            else:
                input_grad[e, :] = out.astype(bf16)

        blocks(edges, through_basis)

    for c in range(CHUNKS):
        cols = pl.ds(c * part, part)

        def to_slots(r):
            slot_send[c, r, :] = dot(source_t[r, :], input_grad[:, cols]).astype(bf16)

        blocks(slots, to_slots)
        mine = pl.ds(pl.multiple_of(me * share, share), share)
        pltpu.make_async_copy(
            slot_send.at[c, mine], slot_recv.at[c, mine], a_recv_sem.at[c]
        ).start()

        def send(k, carry):
            peer = lax.rem(me + k, ents)
            pltpu.make_async_remote_copy(
                src_ref=slot_send.at[c, pl.ds(pl.multiple_of(peer * share, share), share)],
                dst_ref=slot_recv.at[c, mine],
                send_sem=a_send_sem.at[c],
                recv_sem=a_recv_sem.at[c],
                device_id=(t, peer),
                device_id_type=MESH,
            ).start()
            return carry

        lax.fori_loop(1, ents, send, 0)

    def local_part(r):
        state_grad[r, :] += dot(row_grad[r, :], self_t[...]) + dot(gate_row[r, :], gate_t[...])

    blocks(rows, local_part)

    for c in range(CHUNKS):
        cols = pl.ds(c * part, part)
        pltpu.make_async_copy(slot_recv.at[c], slot_recv.at[c], a_recv_sem.at[c]).wait()

        def to_rows(r):
            out = state_grad[r, cols] + dot(exported_t[r, :], slot_recv[c])
            state_grad[r, cols] = out
            sending[c, r, :] = out.astype(bf16)

        blocks(rows, to_rows)

        @pl.when(t > 0)
        def _():
            pass_down(c).start()

    for c in range(CHUNKS):
        rest = slot_send.at[c, pl.ds(0, slots - share)]
        pltpu.make_async_copy(rest, rest, a_send_sem.at[c]).wait()

        @pl.when(t > 0)
        def _():
            pass_down(c).wait_send()


def run_chain(*operands):
    bf16, f32 = jnp.bfloat16, jnp.float32
    rows, width = operands[0].shape
    edges, slots = operands[4].shape[0], operands[5].shape[0]
    part = width // CHUNKS
    shape = jax.ShapeDtypeStruct
    sem = pltpu.SemaphoreType.DMA((CHUNKS,))
    return pl.pallas_call(
        chain_kernel,
        out_shape=(
            shape((rows, width), f32),
            shape((rows, width), bf16),
            shape((rows, width), bf16),
            shape((edges, width), bf16),
            shape((edges, width), bf16),
        ),
        in_specs=[pl.BlockSpec(memory_space=pltpu.VMEM)] * len(operands),
        out_specs=(pl.BlockSpec(memory_space=pltpu.VMEM),) * 5,
        scratch_shapes=[
            pltpu.VMEM((CHUNKS, rows, part), bf16),
            pltpu.VMEM((CHUNKS, rows, part), bf16),
            pltpu.VMEM((edges, width), f32),
            pltpu.VMEM((CHUNKS, slots, part), bf16),
            pltpu.VMEM((CHUNKS, slots, part), bf16),
            sem, sem, sem, sem,
        ],
        compiler_params=pltpu.CompilerParams(
            collective_id=0, has_side_effects=True, vmem_limit_bytes=58 << 20
        ),
    )(*operands)


def per_device(
    states, cotangent, export_rows, edge_src, edge_dst, edge_rel, tile_count,
    basis, coef, rel_emb, self_weight, gate_weight, gate_bias,
):
    bf16, f32 = jnp.bfloat16, jnp.float32
    ent_count = lax.axis_size("ent")
    state = states[0]
    rows, width = state.shape
    basis_count = basis.shape[1] // width
    relations = rel_emb.shape[0]
    edges = edge_src.shape[1]
    slots = export_rows.shape[1]
    live = jnp.arange(edges, dtype=jnp.int32) // TILE < tile_count[0, 0]
    source = onehot(edge_src[0], slots).astype(bf16)
    target = (onehot(edge_dst[0], rows) & live[:, None]).astype(bf16)
    exported = onehot(export_rows[0], rows).astype(bf16)
    relation = onehot(edge_rel[0], relations).astype(bf16)

    received = lax.all_to_all(
        dot(exported, state).astype(bf16), "ent", split_axis=0, concat_axis=0, tiled=True
    )
    edge_input = (dot(source, received) + dot(relation, rel_emb)).astype(bf16)
    coef_high = coef.astype(bf16)
    coef_rest = coef - coef_high.astype(f32)
    coef_mid = coef_rest.astype(bf16)
    coef_low = (coef_rest - coef_mid.astype(f32)).astype(bf16)
    edge_coef = dot(relation, coef_high) + dot(relation, coef_mid) + dot(relation, coef_low)
    images = [
        dot(edge_input, basis[:, b * width : (b + 1) * width]) for b in range(basis_count)
    ]
    message = sum(edge_coef[:, b : b + 1] * images[b] for b in range(basis_count))
    degree = 1.0 + jnp.sum(target.astype(f32), axis=0)
    self_part = dot(state, self_weight)
    summed = (split_dot(target, message) + self_part) / degree[:, None]
    aggregated = jnp.tanh(summed)
    gate_open = jax.nn.sigmoid(dot(state, gate_weight) + gate_bias)
    keep = 1.0 - gate_open
    row_factor = gate_open * (1.0 - aggregated * aggregated) / degree[:, None]
    gate_factor = (aggregated - state.astype(f32)) * gate_open * keep

    basis_t = jnp.stack(
        [basis[:, b * width : (b + 1) * width].T for b in range(basis_count)], axis=0
    )
    state_grad, row_grad, gate_row, edge_grad, input_grad = run_chain(
        cotangent[0], row_factor, gate_factor, keep, target,
        (jnp.arange(slots, dtype=jnp.int32)[:, None] == edge_src[0][None, :]).astype(bf16),
        (jnp.arange(rows, dtype=jnp.int32)[:, None] == export_rows[0][None, :]).astype(bf16),
        edge_coef, basis_t, self_weight.T, gate_weight.T,
    )
    edge_grad = edge_grad.astype(f32)
    image_grad = [
        (edge_coef[:, b : b + 1] * edge_grad).astype(bf16) for b in range(basis_count)
    ]

    coef_edge = jnp.stack(
        [jnp.sum(edge_grad * images[b], axis=1) for b in range(basis_count)], axis=1
    )
    small = jnp.concatenate(
        [
            jnp.sum(gate_row.astype(f32), axis=0).reshape(ent_count, 1, width // ent_count),
            split_dot(relation, coef_edge).reshape(ent_count, 1, -1),
        ],
        axis=2,
    )
    small_width = small.shape[2]
    terms = [dot(edge_input, image_grad[b], FIRST) for b in range(basis_count)]
    terms += [dot(state, row_grad, FIRST), dot(state, gate_row, FIRST)]
    terms += [dot(relation, input_grad, FIRST)]
    packed = jnp.concatenate(
        [term.reshape(ent_count, -1, width) for term in terms]
        + [jnp.pad(small, ((0, 0), (0, 7), (0, width - small_width)))],
        axis=1,
    )
    share = lax.psum_scatter(packed, "ent", scatter_dimension=0, tiled=False)
    share = lax.psum(share, "tm")
    height = width // ent_count
    top = basis_count * height
    return (
        state_grad[None],
        jnp.concatenate([share[b * height : (b + 1) * height] for b in range(basis_count)], axis=1),
        share[top : top + height],
        share[top + height : top + 2 * height],
        share[-8, :height],
        share[-8, height:small_width].reshape(relations // ent_count, basis_count),
        share[top + 2 * height : -8],
    )


def solution(mesh):
    placed = (P("tm", "ent", None),) * 2 + (P("tm", "ent"),) * 5 + (P(),) * 6
    return jax.shard_map(
        per_device,
        mesh=mesh,
        in_specs=placed,
        out_specs=(
            P("tm", "ent", None),
            P("ent", None),
            P("ent", None),
            P("ent", None),
            P("ent"),
            P("ent", None),
            P("ent", None),
        ),
        check_vma=False,
    )
```

```python
import jax
import jax.numpy as jnp
from jax import lax
from jax.experimental import pallas as pl
from jax.experimental.pallas import tpu as pltpu
from jax.sharding import PartitionSpec as P

TILE = 128
MESH = pl.DeviceIdType.MESH
CHUNKS = 2
BLOCK = 256
SIDE = 4
GROUP = 16
LAST = (((1,), (1,)), ((), ()))
FIRST = (((0,), (0,)), ((), ()))


def dot(a, b, dims=(((1,), (0,)), ((), ()))):
    return lax.dot_general(a, b, dims, preferred_element_type=jnp.float32)


def onehot(ids, count):
    return ids[:, None] == jnp.arange(count, dtype=jnp.int32)[None, :]


def split_dot(hot, value):
    high = value.astype(jnp.bfloat16)
    low = (value - high.astype(jnp.float32)).astype(jnp.bfloat16)
    return dot(hot, high, FIRST) + dot(hot, low, FIRST)


def chain_kernel(
    cot, row_factor, gate_factor, keep, target, source_t, exported_t, edge_coef,
    basis_t, self_t, gate_t, images_hbm, input_t_hbm, state_t_hbm, relation_t_hbm,
    state_grad, basis_out, self_out, gate_out, rel_out, coef_out, bias_out,
    row_grad, gate_row, edge_grad, input_grad,
    handed, sending, total, slot_send, slot_recv,
    images, input_t, state_t, relation_t, scaled, coef_hi, coef_lo, small,
    packed, pair_recv, paired, first_recv, first_sum, second_recv, shares,
    z_send_sem, z_recv_sem, a_send_sem, a_recv_sem, load_sem,
    pair_sem, first_send_sem, first_recv_sem, second_send_sem, second_recv_sem, share_sem,
):
    bf16, f32 = jnp.bfloat16, jnp.float32
    t, me = lax.axis_index("tm"), lax.axis_index("ent")
    sections, ents = lax.axis_size("tm"), lax.axis_size("ent")
    rows, width = cot.shape
    edges, slots = target.shape[0], source_t.shape[0]
    share = slots // ents
    part = width // CHUNKS
    above = lax.rem(t + 1, sections)
    below = lax.rem(t + sections - 1, sections)

    barrier = pltpu.get_barrier_semaphore()

    def greet(k, carry):
        peer = lax.rem(me + k, ents)
        pl.semaphore_signal(barrier, inc=1, device_id=(t, peer), device_id_type=MESH)
        return carry

    lax.fori_loop(1, ents, greet, 0)
    pl.semaphore_signal(barrier, inc=1, device_id=(above, me), device_id_type=MESH)
    pl.semaphore_signal(barrier, inc=1, device_id=(below, me), device_id_type=MESH)
    opposite = lax.rem(t + 2, sections)
    pl.semaphore_signal(barrier, inc=1, device_id=(opposite, me), device_id_type=MESH)
    loads = [
        pltpu.make_async_copy(src, dst, load_sem.at[i])
        for i, (src, dst) in enumerate(
            [
                (images_hbm, images),
                (input_t_hbm, input_t),
                (state_t_hbm, state_t),
                (relation_t_hbm, relation_t),
            ]
        )
    ]
    for load in loads:
        load.start()
    pl.semaphore_wait(barrier, ents + 2)

    def pass_down(c):
        return pltpu.make_async_remote_copy(
            src_ref=sending.at[c],
            dst_ref=handed.at[c],
            send_sem=z_send_sem.at[c],
            recv_sem=z_recv_sem.at[c],
            device_id=(below, me),
            device_id_type=MESH,
        )

    def blocks(count, body):
        def step(i, carry):
            body(pl.ds(pl.multiple_of(i * BLOCK, BLOCK), BLOCK))
            return carry

        lax.fori_loop(0, count // BLOCK, step, 0)

    for c in range(CHUNKS):
        cols = pl.ds(c * part, part)

        @pl.when(t < sections - 1)
        def _():
            pass_down(c).wait_recv()

        @pl.when(t == sections - 1)
        def _():
            handed[c] = jnp.zeros((rows, part), bf16)

        def elementwise(r):
            upstream = cot[r, cols].astype(f32) + handed[c, r, :].astype(f32)
            row_grad[r, cols] = (upstream * row_factor[r, cols]).astype(bf16)
            gate_row[r, cols] = (upstream * gate_factor[r, cols]).astype(bf16)
            state_grad[r, cols] = upstream * keep[r, cols]

        blocks(rows, elementwise)

        def through_basis(e):
            gathered = dot(target[e, :], row_grad[:, cols])
            edge_grad[e, cols] = gathered.astype(bf16)
            out = 0.0
            for b in range(edge_coef.shape[1]):
                image_grad = (edge_coef[e, b : b + 1] * gathered).astype(bf16)
                out = out + dot(image_grad, basis_t[b, cols, :])
            if c > 0:
                out = out + total[e, :]
            if c < CHUNKS - 1:
                total[e, :] = out
            else:
                input_grad[e, :] = out.astype(bf16)

        blocks(edges, through_basis)

    for c in range(CHUNKS):
        cols = pl.ds(c * part, part)

        def to_slots(r):
            slot_send[c, r, :] = dot(source_t[r, :], input_grad[:, cols]).astype(bf16)

        blocks(slots, to_slots)
        mine = pl.ds(pl.multiple_of(me * share, share), share)
        pltpu.make_async_copy(
            slot_send.at[c, mine], slot_recv.at[c, mine], a_recv_sem.at[c]
        ).start()

        def send(k, carry):
            peer = lax.rem(me + k, ents)
            pltpu.make_async_remote_copy(
                src_ref=slot_send.at[c, pl.ds(pl.multiple_of(peer * share, share), share)],
                dst_ref=slot_recv.at[c, mine],
                send_sem=a_send_sem.at[c],
                recv_sem=a_recv_sem.at[c],
                device_id=(t, peer),
                device_id_type=MESH,
            ).start()
            return carry

        lax.fori_loop(1, ents, send, 0)

    def local_part(r):
        state_grad[r, :] += dot(row_grad[r, :], self_t[...]) + dot(gate_row[r, :], gate_t[...])

    blocks(rows, local_part)

    for c in range(CHUNKS):
        cols = pl.ds(c * part, part)
        pltpu.make_async_copy(slot_recv.at[c], slot_recv.at[c], a_recv_sem.at[c]).wait()

        def to_rows(r):
            out = state_grad[r, cols] + dot(exported_t[r, :], slot_recv[c])
            state_grad[r, cols] = out
            sending[c, r, :] = out.astype(bf16)

        blocks(rows, to_rows)

        @pl.when(t > 0)
        def _():
            pass_down(c).start()

    for load in loads:
        load.wait()
    core = lax.rem(me, 2)
    y = lax.rem(me // 2, SIDE)
    x = me // (2 * SIDE)
    sibling = me + 1 - 2 * core
    half = width // 2

    def to_pair(offset):
        piece = pl.ds(offset, GROUP)
        return pltpu.make_async_remote_copy(
            src_ref=packed.at[1 - core, :, :, piece, :],
            dst_ref=pair_recv.at[:, :, piece, :],
            send_sem=pair_sem.at[0],
            recv_sem=pair_sem.at[1],
            device_id=(t, sibling),
            device_id_type=MESH,
        )

    def pack(offset, i, value):
        value = value.astype(bf16).reshape(SIDE, 2, GROUP, width)
        rows_at = pl.ds(offset, GROUP)
        for core_to in range(2):
            for y_to in range(SIDE):
                one = value[y_to, core_to]
                packed[core_to, 0, i * SIDE + y_to, rows_at, :] = one[:, :half]
                packed[core_to, 1, y_to * SIDE + i, rows_at, :] = one[:, half:]

    def term(offset, left, right):
        def step(i, carry):
            r = pl.ds(pl.multiple_of(i * 128, 128), 128)
            pack(offset, i, dot(left[r, :], right[...]))
            return carry

        lax.fori_loop(0, SIDE, step, 0)
        to_pair(offset).start()

    basis_count = edge_coef.shape[1]
    for b in range(basis_count):

        def scale(e):
            scaled[e, :] = (edge_coef[e, b : b + 1] * edge_grad[e, :].astype(f32)).astype(bf16)

        blocks(edges, scale)
        term(b * GROUP, input_t, scaled)
    term(basis_count * GROUP, state_t, row_grad)
    term((basis_count + 1) * GROUP, state_t, gate_row)

    def inner(e):
        lane = lax.broadcasted_iota(jnp.int32, (BLOCK, 128), 1)
        out = jnp.zeros((BLOCK, 128), f32)
        gradient = edge_grad[e, :].astype(f32)
        for b in range(basis_count):
            product = gradient * images[e, b * width : (b + 1) * width].astype(f32)
            out = jnp.where(lane == b, jnp.sum(product, axis=1, keepdims=True), out)
        high = out.astype(bf16)
        coef_hi[e, :] = high
        coef_lo[e, :] = (out - high.astype(f32)).astype(bf16)

    blocks(edges, inner)
    relations = relation_t.shape[0]
    bias = jnp.zeros((1, width), f32)
    for i in range(rows // BLOCK):
        piece = gate_row[i * BLOCK : (i + 1) * BLOCK, :].astype(f32)
        bias = bias + jnp.sum(piece, axis=0, keepdims=True)
    line = lax.broadcasted_iota(jnp.int32, (8, width - 128), 0)
    wrapped = jnp.concatenate([bias[:, width - 128 :]] * (width // 128 - 1), axis=1)
    tile = jnp.where(line == 0, bias[:, : width - 128], jnp.where(line == 1, wrapped, 0.0))
    small[:, 0:8, :] = dot(relation_t[...], input_grad[...]).reshape(ents, 8, width)
    coef_rows = dot(relation_t[...], coef_hi[...]) + dot(relation_t[...], coef_lo[...])
    small[:, 8:16, 0:128] = coef_rows.reshape(ents, 8, 128)
    small[:, 8:16, 128:] = jnp.broadcast_to(tile[None], (ents, 8, width - 128))

    def pack_small(i, carry):
        pack((basis_count + 2) * GROUP, i, small[pl.ds(i * 2 * SIDE, 2 * SIDE)])
        return carry

    lax.fori_loop(0, SIDE, pack_small, 0)
    to_pair((basis_count + 2) * GROUP).start()

    pltpu.make_async_copy(pair_recv, pair_recv, pair_sem.at[1]).wait()

    def chip(px, py):
        return (t, px * (2 * SIDE) + py * 2 + core)

    def other(h, k):
        return lax.rem((x if h == 0 else y) + k, SIDE)

    for h in range(2):

        def add_pair(i, carry):
            total_pair = packed[core, h, i].astype(f32) + pair_recv[h, i].astype(f32)
            paired[h, i] = total_pair.astype(bf16)
            return carry

        lax.fori_loop(0, SIDE * SIDE, add_pair, 0)
        for k in range(1, SIDE):
            to = other(h, k)
            pltpu.make_async_remote_copy(
                src_ref=paired.at[h, pl.ds(to * SIDE, SIDE)],
                dst_ref=first_recv.at[h, k - 1],
                send_sem=first_send_sem.at[h],
                recv_sem=first_recv_sem.at[h],
                device_id=chip(to, y) if h == 0 else chip(x, to),
                device_id_type=MESH,
            ).start()

    for h in range(2):
        pltpu.make_async_copy(first_recv.at[h], first_recv.at[h], first_recv_sem.at[h]).wait()

        def add_first(j, carry):
            out = paired[h, other(h, 0) * SIDE + j].astype(f32)
            for k in range(SIDE - 1):
                out = out + first_recv[h, k, j].astype(f32)
            first_sum[h, j] = out.astype(bf16)
            return carry

        lax.fori_loop(0, SIDE, add_first, 0)
        for k in range(1, SIDE):
            to = other(1 - h, k)
            pltpu.make_async_remote_copy(
                src_ref=first_sum.at[h, to],
                dst_ref=second_recv.at[h, k - 1],
                send_sem=second_send_sem.at[h],
                recv_sem=second_recv_sem.at[h],
                device_id=chip(x, to) if h == 0 else chip(to, y),
                device_id_type=MESH,
            ).start()

    for h in range(2):
        pltpu.make_async_copy(second_recv.at[h], second_recv.at[h], second_recv_sem.at[h]).wait()
        out = first_sum[h, other(1 - h, 0)].astype(f32)
        for k in range(SIDE - 1):
            out = out + second_recv[h, k].astype(f32)
        shares[t, h] = out.astype(bf16)
    for k in range(1, SIDE):
        pltpu.make_async_remote_copy(
            src_ref=shares.at[t],
            dst_ref=shares.at[t],
            send_sem=share_sem.at[0],
            recv_sem=share_sem.at[1],
            device_id=(lax.rem(t + k, sections), me),
            device_id_type=MESH,
        ).start()
    others = shares.at[pl.ds(0, sections - 1)]
    pltpu.make_async_copy(others, others, share_sem.at[1]).wait()
    for h in range(2):
        at = pl.ds(h * half, half)
        out = shares[0, h].astype(f32)
        for p in range(1, SIDE):
            out = out + shares[p, h].astype(f32)
        for b in range(basis_count):
            basis_out[:, b * width + h * half : b * width + (h + 1) * half] = out[
                b * GROUP : (b + 1) * GROUP
            ]
        top = basis_count * GROUP
        self_out[:, at] = out[top : top + GROUP]
        gate_out[:, at] = out[top + GROUP : top + 2 * GROUP]
        rel_out[:, at] = out[top + 2 * GROUP : top + 2 * GROUP + 8]
        rest = out[top + 2 * GROUP + 8 : top + 3 * GROUP]
        if h == 0:
            coef_out[...] = rest[:, :128]
            bias_out[:, : half - 128] = rest[:, 128:]
        else:
            bias_out[:, half - 128 :] = rest

    pltpu.make_async_copy(pair_recv, pair_recv, pair_sem.at[0]).wait()
    pltpu.make_async_copy(others, others, share_sem.at[0]).wait()
    for h in range(2):
        pltpu.make_async_copy(first_recv.at[h], first_recv.at[h], first_send_sem.at[h]).wait()
        pltpu.make_async_copy(second_recv.at[h], second_recv.at[h], second_send_sem.at[h]).wait()

    for c in range(CHUNKS):
        rest = slot_send.at[c, pl.ds(0, slots - share)]
        pltpu.make_async_copy(rest, rest, a_send_sem.at[c]).wait()

        @pl.when(t > 0)
        def _():
            pass_down(c).wait_send()


def run_chain(*operands):
    bf16, f32 = jnp.bfloat16, jnp.float32
    rows, width = operands[0].shape
    edges, slots = operands[4].shape[0], operands[5].shape[0]
    basis_count = operands[7].shape[1]
    relations = operands[14].shape[0]
    ents = lax.axis_size("ent")
    part, half = width // CHUNKS, width // 2
    height = (basis_count + 3) * GROUP
    shape = jax.ShapeDtypeStruct
    chunk_sem = pltpu.SemaphoreType.DMA((CHUNKS,))
    two = pltpu.SemaphoreType.DMA((2,))
    whole = pl.BlockSpec(memory_space=pltpu.VMEM)
    return pl.pallas_call(
        chain_kernel,
        out_shape=(
            shape((rows, width), f32),
            shape((GROUP, basis_count * width), f32),
            shape((GROUP, width), f32),
            shape((GROUP, width), f32),
            shape((8, width), f32),
            shape((8, 128), f32),
            shape((8, width - 128), f32),
        ),
        in_specs=[whole] * 11 + [pl.BlockSpec(memory_space=pl.ANY)] * 4,
        out_specs=(whole,) * 7,
        scratch_shapes=[
            pltpu.VMEM((rows, width), bf16),
            pltpu.VMEM((rows, width), bf16),
            pltpu.VMEM((edges, width), bf16),
            pltpu.VMEM((edges, width), bf16),
            pltpu.VMEM((CHUNKS, rows, part), bf16),
            pltpu.VMEM((CHUNKS, rows, part), bf16),
            pltpu.VMEM((edges, width), f32),
            pltpu.VMEM((CHUNKS, slots, part), bf16),
            pltpu.VMEM((CHUNKS, slots, part), bf16),
            pltpu.VMEM((edges, basis_count * width), bf16),
            pltpu.VMEM((width, edges), bf16),
            pltpu.VMEM((width, rows), bf16),
            pltpu.VMEM((relations, edges), bf16),
            pltpu.VMEM((edges, width), bf16),
            pltpu.VMEM((edges, 128), bf16),
            pltpu.VMEM((edges, 128), bf16),
            pltpu.VMEM((ents, GROUP, width), f32),
            pltpu.VMEM((2, 2, SIDE * SIDE, height, half), bf16),
            pltpu.VMEM((2, SIDE * SIDE, height, half), bf16),
            pltpu.VMEM((2, SIDE * SIDE, height, half), bf16),
            pltpu.VMEM((2, SIDE - 1, SIDE, height, half), bf16),
            pltpu.VMEM((2, SIDE, height, half), bf16),
            pltpu.VMEM((2, SIDE - 1, height, half), bf16),
            pltpu.VMEM((SIDE, 2, height, half), bf16),
            chunk_sem, chunk_sem, chunk_sem, chunk_sem,
            pltpu.SemaphoreType.DMA((4,)),
            two, two, two, two, two, two,
        ],
        compiler_params=pltpu.CompilerParams(
            collective_id=0, has_side_effects=True, vmem_limit_bytes=60 << 20
        ),
    )(*operands)


def per_device(
    states, cotangent, export_rows, edge_src, edge_dst, edge_rel, tile_count,
    basis, coef, rel_emb, self_weight, gate_weight, gate_bias,
):
    bf16, f32 = jnp.bfloat16, jnp.float32
    ent_count = lax.axis_size("ent")
    state = states[0]
    rows, width = state.shape
    basis_count = basis.shape[1] // width
    relations = rel_emb.shape[0]
    edges = edge_src.shape[1]
    slots = export_rows.shape[1]
    live = jnp.arange(edges, dtype=jnp.int32) // TILE < tile_count[0, 0]
    source = onehot(edge_src[0], slots).astype(bf16)
    target = (onehot(edge_dst[0], rows) & live[:, None]).astype(bf16)
    exported = onehot(export_rows[0], rows).astype(bf16)
    relation = onehot(edge_rel[0], relations).astype(bf16)

    received = lax.all_to_all(
        dot(exported, state).astype(bf16), "ent", split_axis=0, concat_axis=0, tiled=True
    )
    edge_input = (dot(source, received) + dot(relation, rel_emb)).astype(bf16)
    coef_high = coef.astype(bf16)
    coef_rest = coef - coef_high.astype(f32)
    coef_mid = coef_rest.astype(bf16)
    coef_low = (coef_rest - coef_mid.astype(f32)).astype(bf16)
    edge_coef = dot(relation, coef_high) + dot(relation, coef_mid) + dot(relation, coef_low)
    images = [
        dot(edge_input, basis[:, b * width : (b + 1) * width]) for b in range(basis_count)
    ]
    message = sum(edge_coef[:, b : b + 1] * images[b] for b in range(basis_count))
    degree = 1.0 + jnp.sum(target.astype(f32), axis=0)
    self_part = dot(state, self_weight)
    summed = (split_dot(target, message) + self_part) / degree[:, None]
    aggregated = jnp.tanh(summed)
    gate_open = jax.nn.sigmoid(dot(state, gate_weight) + gate_bias)
    keep = 1.0 - gate_open
    row_factor = gate_open * (1.0 - aggregated * aggregated) / degree[:, None]
    gate_factor = (aggregated - state.astype(f32)) * gate_open * keep

    basis_t = jnp.stack(
        [basis[:, b * width : (b + 1) * width].T for b in range(basis_count)], axis=0
    )
    slot_ids = jnp.arange(slots, dtype=jnp.int32)[:, None]
    row_ids = jnp.arange(rows, dtype=jnp.int32)[:, None]
    relation_ids = jnp.arange(relations, dtype=jnp.int32)[:, None]
    state_grad, basis_sum, self_sum, gate_sum, rel_sum, coef_sum, bias_sum = run_chain(
        cotangent[0], row_factor, gate_factor, keep, target,
        (slot_ids == edge_src[0][None, :]).astype(bf16),
        (row_ids == export_rows[0][None, :]).astype(bf16),
        edge_coef, basis_t, self_weight.T, gate_weight.T,
        jnp.concatenate([image.astype(bf16) for image in images], axis=1),
        edge_input.T, state.T,
        (relation_ids == edge_rel[0][None, :]).astype(bf16),
    )
    height = width // ent_count
    bias = jnp.concatenate([bias_sum[0], bias_sum[1, :128]])
    return (
        state_grad[None],
        basis_sum,
        self_sum,
        gate_sum,
        lax.dynamic_slice_in_dim(bias, lax.axis_index("ent") * height, height, 0),
        coef_sum[:, :basis_count],
        rel_sum,
    )


def solution(mesh):
    placed = (P("tm", "ent", None),) * 2 + (P("tm", "ent"),) * 5 + (P(),) * 6
    return jax.shard_map(
        per_device,
        mesh=mesh,
        in_specs=placed,
        out_specs=(
            P("tm", "ent", None),
            P("ent", None),
            P("ent", None),
            P("ent", None),
            P("ent"),
            P("ent", None),
            P("ent", None),
        ),
        check_vma=False,
    )
```

```python
import jax
import jax.numpy as jnp
from jax import lax
from jax.experimental import pallas as pl
from jax.experimental.pallas import tpu as pltpu
from jax.sharding import PartitionSpec as P

TILE = 128
MESH = pl.DeviceIdType.MESH
CHUNKS = 2
BLOCK = 256
SIDE = 4
GROUP = 16
EXPORT, SOURCE, TARGET, RELATION = range(4)
LAST = (((1,), (1,)), ((), ()))


def dot(a, b, dims=(((1,), (0,)), ((), ()))):
    return lax.dot_general(a, b, dims, preferred_element_type=jnp.float32)


def chain_kernel(
    state, ids_row, ids_col, coef_parts, gate_bias,
    cot_hbm, basis_hbm, rel_emb_hbm, self_hbm, gate_hbm,
    state_grad, basis_out, self_out, gate_out, rel_out, coef_out, bias_out,
    cot, basis, rel_emb, self_weight, gate_weight,
    row_factor, gate_factor, keep, target, source_t, early, exported_t, edge_coef,
    export_send, export_recv, edge_input,
    row_grad, gate_row, edge_grad, input_grad,
    handed, sending, total, slot_send, slot_recv,
    images, input_t, state_t, relation_t, scaled, coef_hi, coef_lo, small,
    packed, pair_recv, first_recv, first_sum, second_recv, shares,
    z_send_sem, z_recv_sem, a_send_sem, a_recv_sem, load_sem, export_sem,
    pair_sem, first_send_sem, first_recv_sem, second_send_sem, second_recv_sem, share_sem,
):
    bf16, f32 = jnp.bfloat16, jnp.float32
    t, me = lax.axis_index("tm"), lax.axis_index("ent")
    sections, ents = lax.axis_size("tm"), lax.axis_size("ent")
    rows, width = state.shape
    edges = slots = ids_row.shape[1]
    relations = rel_emb.shape[0]
    basis_count = basis.shape[1] // width
    share = slots // ents
    part = width // CHUNKS
    above = lax.rem(t + 1, sections)
    below = lax.rem(t + sections - 1, sections)

    barrier = pltpu.get_barrier_semaphore()

    def greet(k, carry):
        peer = lax.rem(me + k, ents)
        pl.semaphore_signal(barrier, inc=1, device_id=(t, peer), device_id_type=MESH)
        return carry

    lax.fori_loop(1, ents, greet, 0)
    pl.semaphore_signal(barrier, inc=1, device_id=(above, me), device_id_type=MESH)
    pl.semaphore_signal(barrier, inc=1, device_id=(below, me), device_id_type=MESH)
    opposite = lax.rem(t + 2, sections)
    pl.semaphore_signal(barrier, inc=1, device_id=(opposite, me), device_id_type=MESH)
    loads = [
        pltpu.make_async_copy(src, dst, load_sem.at[i])
        for i, (src, dst) in enumerate(
            [
                (rel_emb_hbm, rel_emb),
                (self_hbm, self_weight),
                (gate_hbm, gate_weight),
                (basis_hbm, basis),
                (cot_hbm, cot),
            ]
        )
    ]
    for load in loads:
        load.start()

    def pass_down(c):
        return pltpu.make_async_remote_copy(
            src_ref=sending.at[c],
            dst_ref=handed.at[c],
            send_sem=z_send_sem.at[c],
            recv_sem=z_recv_sem.at[c],
            device_id=(below, me),
            device_id_type=MESH,
        )

    def blocks(count, body):
        def step(i, carry):
            body(pl.ds(pl.multiple_of(i * BLOCK, BLOCK), BLOCK))
            return carry

        lax.fori_loop(0, count // BLOCK, step, 0)

    def one(mask):
        return jnp.where(mask, 1.0, 0.0).astype(bf16)

    def by_row(kind, r, count):
        lane = lax.broadcasted_iota(jnp.int32, (BLOCK, count), 1)
        return one(ids_col[r, kind : kind + 1] == lane)

    def by_column(kind, r):
        line = lax.broadcasted_iota(jnp.int32, (BLOCK, edges), 0) + r.start
        return one(ids_row[kind : kind + 1, :] == line)

    mine = pl.ds(pl.multiple_of(me * share, share), share)

    def export(r):
        export_send[r, :] = dot(by_row(EXPORT, r, rows), state[...]).astype(bf16)

    blocks(slots, export)
    pltpu.make_async_copy(export_send.at[mine], export_recv.at[mine], export_sem.at[1]).start()
    pl.semaphore_wait(barrier, ents + 2)

    def send_export(k, carry):
        peer = lax.rem(me + k, ents)
        pltpu.make_async_remote_copy(
            src_ref=export_send.at[pl.ds(pl.multiple_of(peer * share, share), share)],
            dst_ref=export_recv.at[mine],
            send_sem=export_sem.at[0],
            recv_sem=export_sem.at[1],
            device_id=(t, peer),
            device_id_type=MESH,
        ).start()
        return carry

    lax.fori_loop(1, ents, send_export, 0)
    for load in loads[:3]:
        load.wait()

    def by_edge(e):
        early[e, :] = by_row(SOURCE, e, slots)
        target[e, :] = by_row(TARGET, e, rows)
        relation = by_row(RELATION, e, relations)
        total[e, :] = dot(relation, rel_emb[...])
        edge_coef[e, :] = sum(dot(relation, coef_parts[i]) for i in range(3))

    blocks(edges, by_edge)

    def forms(r):
        exported_t[r, :] = by_column(TARGET, r)
        source_t[r, :] = by_column(SOURCE, r)
        state_grad[r, :] = dot(state[r, :], self_weight[...])
        keep[r, :] = jax.nn.sigmoid(dot(state[r, :], gate_weight[...]) + gate_bias[...])

    blocks(rows, forms)
    loads[3].wait()
    pltpu.make_async_copy(export_recv, export_recv, export_sem.at[1]).wait()

    def forward(e):
        value = (dot(early[e, :], export_recv[...]) + total[e, :]).astype(bf16)
        edge_input[e, :] = value
        message = 0.0
        for b in range(basis_count):
            at = slice(b * width, (b + 1) * width)
            image = dot(value, basis[:, at])
            images[e, at] = image.astype(bf16)
            message = message + edge_coef[e, b : b + 1] * image
        edge_grad[e, :] = message.astype(bf16)

    blocks(edges, forward)

    def factors(r):
        hot = exported_t[r, :]
        degree = 1.0 + dot(hot, jnp.ones((edges, 128), bf16))[:, :1]
        scale = 1.0 / degree
        aggregated = jnp.tanh((dot(hot, edge_grad[...]) + state_grad[r, :]) * scale)
        gate_open = keep[r, :]
        closed = 1.0 - gate_open
        row_factor[r, :] = gate_open * (1.0 - aggregated * aggregated) * scale
        gate_factor[r, :] = (aggregated - state[r, :].astype(f32)) * gate_open * closed
        keep[r, :] = closed

    blocks(rows, factors)
    loads[4].wait()

    for c in range(CHUNKS):
        cols = pl.ds(c * part, part)

        @pl.when(t < sections - 1)
        def _():
            pass_down(c).wait_recv()

        @pl.when(t == sections - 1)
        def _():
            handed[c] = jnp.zeros((rows, part), bf16)

        def elementwise(r):
            upstream = cot[r, cols].astype(f32) + handed[c, r, :].astype(f32)
            row_grad[r, cols] = (upstream * row_factor[r, cols]).astype(bf16)
            gate_row[r, cols] = (upstream * gate_factor[r, cols]).astype(bf16)
            state_grad[r, cols] = upstream * keep[r, cols]

        blocks(rows, elementwise)

        def through_basis(e):
            gathered = dot(target[e, :], row_grad[:, cols])
            edge_grad[e, cols] = gathered.astype(bf16)
            out = 0.0
            for b in range(basis_count):
                image_grad = (edge_coef[e, b : b + 1] * gathered).astype(bf16)
                at = slice(b * width + c * part, b * width + (c + 1) * part)
                out = out + dot(image_grad, basis[:, at], LAST)
            if c > 0:
                out = out + total[e, :]
            if c < CHUNKS - 1:
                total[e, :] = out
            else:
                input_grad[e, :] = out.astype(bf16)

        blocks(edges, through_basis)

    for c in range(CHUNKS):
        cols = pl.ds(c * part, part)

        def to_slots(r):
            slot_send[c, r, :] = dot(source_t[r, :], input_grad[:, cols]).astype(bf16)

        blocks(slots, to_slots)
        pltpu.make_async_copy(
            slot_send.at[c, mine], slot_recv.at[c, mine], a_recv_sem.at[c]
        ).start()

        def send(k, carry):
            peer = lax.rem(me + k, ents)
            pltpu.make_async_remote_copy(
                src_ref=slot_send.at[c, pl.ds(pl.multiple_of(peer * share, share), share)],
                dst_ref=slot_recv.at[c, mine],
                send_sem=a_send_sem.at[c],
                recv_sem=a_recv_sem.at[c],
                device_id=(t, peer),
                device_id_type=MESH,
            ).start()
            return carry

        lax.fori_loop(1, ents, send, 0)

    def local_part(r):
        state_grad[r, :] += dot(row_grad[r, :], self_weight[...], LAST) + dot(
            gate_row[r, :], gate_weight[...], LAST
        )
        exported_t[r, :] = by_column(EXPORT, r)

    blocks(rows, local_part)

    for c in range(CHUNKS):
        cols = pl.ds(c * part, part)
        pltpu.make_async_copy(slot_recv.at[c], slot_recv.at[c], a_recv_sem.at[c]).wait()

        def to_rows(r):
            out = state_grad[r, cols] + dot(exported_t[r, :], slot_recv[c])
            state_grad[r, cols] = out
            sending[c, r, :] = out.astype(bf16)

        blocks(rows, to_rows)

        @pl.when(t > 0)
        def _():
            pass_down(c).start()

    def turn(r):
        input_t[:, r] = edge_input[r, :].T
        state_t[:, r] = state[r, :].T

    blocks(edges, turn)
    relation_line = lax.broadcasted_iota(jnp.int32, (relations, edges), 0)
    relation_t[...] = one(ids_row[RELATION : RELATION + 1, :] == relation_line)
    core = lax.rem(me, 2)
    y = lax.rem(me // 2, SIDE)
    x = me // (2 * SIDE)
    sibling = me + 1 - 2 * core
    half = width // 2

    def to_pair(offset):
        piece = pl.ds(offset, GROUP)
        return pltpu.make_async_remote_copy(
            src_ref=packed.at[1 - core, :, :, piece, :],
            dst_ref=pair_recv.at[:, :, piece, :],
            send_sem=pair_sem.at[0],
            recv_sem=pair_sem.at[1],
            device_id=(t, sibling),
            device_id_type=MESH,
        )

    def pack(offset, i, value):
        value = value.astype(bf16).reshape(SIDE, 2, GROUP, width)
        rows_at = pl.ds(offset, GROUP)
        for core_to in range(2):
            for y_to in range(SIDE):
                one = value[y_to, core_to]
                packed[core_to, 0, i * SIDE + y_to, rows_at, :] = one[:, :half]
                packed[core_to, 1, y_to * SIDE + i, rows_at, :] = one[:, half:]

    def term(offset, left, right):
        def step(i, carry):
            r = pl.ds(pl.multiple_of(i * 128, 128), 128)
            pack(offset, i, dot(left[r, :], right[...]))
            return carry

        lax.fori_loop(0, SIDE, step, 0)
        to_pair(offset).start()

    for b in range(basis_count):

        def scale(e):
            scaled[e, :] = (edge_coef[e, b : b + 1] * edge_grad[e, :].astype(f32)).astype(bf16)

        blocks(edges, scale)
        term(b * GROUP, input_t, scaled)
    term(basis_count * GROUP, state_t, row_grad)
    term((basis_count + 1) * GROUP, state_t, gate_row)

    def inner(e):
        lane = lax.broadcasted_iota(jnp.int32, (BLOCK, 128), 1)
        out = jnp.zeros((BLOCK, 128), f32)
        gradient = edge_grad[e, :].astype(f32)
        for b in range(basis_count):
            product = gradient * images[e, b * width : (b + 1) * width].astype(f32)
            out = jnp.where(lane == b, jnp.sum(product, axis=1, keepdims=True), out)
        high = out.astype(bf16)
        coef_hi[e, :] = high
        coef_lo[e, :] = (out - high.astype(f32)).astype(bf16)

    blocks(edges, inner)
    bias = jnp.zeros((1, width), f32)
    for i in range(rows // BLOCK):
        piece = gate_row[i * BLOCK : (i + 1) * BLOCK, :].astype(f32)
        bias = bias + jnp.sum(piece, axis=0, keepdims=True)
    line = lax.broadcasted_iota(jnp.int32, (8, width - 128), 0)
    wrapped = jnp.concatenate([bias[:, width - 128 :]] * (width // 128 - 1), axis=1)
    tile = jnp.where(line == 0, bias[:, : width - 128], jnp.where(line == 1, wrapped, 0.0))
    small[:, 0:8, :] = dot(relation_t[...], input_grad[...]).reshape(ents, 8, width)
    coef_rows = dot(relation_t[...], coef_hi[...]) + dot(relation_t[...], coef_lo[...])
    small[:, 8:16, 0:128] = coef_rows.reshape(ents, 8, 128)
    small[:, 8:16, 128:] = jnp.broadcast_to(tile[None], (ents, 8, width - 128))

    def pack_small(i, carry):
        pack((basis_count + 2) * GROUP, i, small[pl.ds(i * 2 * SIDE, 2 * SIDE)])
        return carry

    lax.fori_loop(0, SIDE, pack_small, 0)
    to_pair((basis_count + 2) * GROUP).start()

    pltpu.make_async_copy(pair_recv, pair_recv, pair_sem.at[1]).wait()

    def chip(px, py):
        return (t, px * (2 * SIDE) + py * 2 + core)

    def other(h, k):
        return lax.rem((x if h == 0 else y) + k, SIDE)

    for h in range(2):

        def add_pair(i, carry):
            total_pair = packed[core, h, i].astype(f32) + pair_recv[h, i].astype(f32)
            packed[core, h, i] = total_pair.astype(bf16)
            return carry

        lax.fori_loop(0, SIDE * SIDE, add_pair, 0)
        for k in range(1, SIDE):
            to = other(h, k)
            pltpu.make_async_remote_copy(
                src_ref=packed.at[core, h, pl.ds(to * SIDE, SIDE)],
                dst_ref=first_recv.at[h, k - 1],
                send_sem=first_send_sem.at[h],
                recv_sem=first_recv_sem.at[h],
                device_id=chip(to, y) if h == 0 else chip(x, to),
                device_id_type=MESH,
            ).start()

    for h in range(2):
        pltpu.make_async_copy(first_recv.at[h], first_recv.at[h], first_recv_sem.at[h]).wait()

        def add_first(j, carry):
            out = packed[core, h, other(h, 0) * SIDE + j].astype(f32)
            for k in range(SIDE - 1):
                out = out + first_recv[h, k, j].astype(f32)
            first_sum[h, j] = out.astype(bf16)
            return carry

        lax.fori_loop(0, SIDE, add_first, 0)
        for k in range(1, SIDE):
            to = other(1 - h, k)
            pltpu.make_async_remote_copy(
                src_ref=first_sum.at[h, to],
                dst_ref=second_recv.at[h, k - 1],
                send_sem=second_send_sem.at[h],
                recv_sem=second_recv_sem.at[h],
                device_id=chip(x, to) if h == 0 else chip(to, y),
                device_id_type=MESH,
            ).start()

    for h in range(2):
        pltpu.make_async_copy(second_recv.at[h], second_recv.at[h], second_recv_sem.at[h]).wait()
        out = first_sum[h, other(1 - h, 0)].astype(f32)
        for k in range(SIDE - 1):
            out = out + second_recv[h, k].astype(f32)
        shares[t, h] = out.astype(bf16)
    for k in range(1, SIDE):
        pltpu.make_async_remote_copy(
            src_ref=shares.at[t],
            dst_ref=shares.at[t],
            send_sem=share_sem.at[0],
            recv_sem=share_sem.at[1],
            device_id=(lax.rem(t + k, sections), me),
            device_id_type=MESH,
        ).start()
    others = shares.at[pl.ds(0, sections - 1)]
    pltpu.make_async_copy(others, others, share_sem.at[1]).wait()
    for h in range(2):
        at = pl.ds(h * half, half)
        out = shares[0, h].astype(f32)
        for p in range(1, SIDE):
            out = out + shares[p, h].astype(f32)
        for b in range(basis_count):
            basis_out[:, b * width + h * half : b * width + (h + 1) * half] = out[
                b * GROUP : (b + 1) * GROUP
            ]
        top = basis_count * GROUP
        self_out[:, at] = out[top : top + GROUP]
        gate_out[:, at] = out[top + GROUP : top + 2 * GROUP]
        rel_out[:, at] = out[top + 2 * GROUP : top + 2 * GROUP + 8]
        rest = out[top + 2 * GROUP + 8 : top + 3 * GROUP]
        if h == 0:
            coef_out[...] = rest[:, :128]
            bias_out[:, : half - 128] = rest[:, 128:]
        else:
            bias_out[:, half - 128 :] = rest

    pltpu.make_async_copy(pair_recv, pair_recv, pair_sem.at[0]).wait()
    pltpu.make_async_copy(others, others, share_sem.at[0]).wait()
    for h in range(2):
        pltpu.make_async_copy(first_recv.at[h], first_recv.at[h], first_send_sem.at[h]).wait()
        pltpu.make_async_copy(second_recv.at[h], second_recv.at[h], second_send_sem.at[h]).wait()

    for c in range(CHUNKS):
        if c == 0:
            rest = export_send.at[pl.ds(0, slots - share)]
            pltpu.make_async_copy(rest, rest, export_sem.at[0]).wait()
        rest = slot_send.at[c, pl.ds(0, slots - share)]
        pltpu.make_async_copy(rest, rest, a_send_sem.at[c]).wait()

        @pl.when(t > 0)
        def _():
            pass_down(c).wait_send()


def run_chain(*operands):
    bf16, f32 = jnp.bfloat16, jnp.float32
    rows, width = operands[0].shape
    edges = slots = operands[1].shape[1]
    basis_count = operands[6].shape[1] // width
    relations = operands[7].shape[0]
    ents = lax.axis_size("ent")
    part, half = width // CHUNKS, width // 2
    height = (basis_count + 3) * GROUP
    shape = jax.ShapeDtypeStruct
    chunk_sem = pltpu.SemaphoreType.DMA((CHUNKS,))
    two = pltpu.SemaphoreType.DMA((2,))
    whole = pl.BlockSpec(memory_space=pltpu.VMEM)
    wide, flat, narrow = (
        pltpu.VMEM((rows, width), f32),
        pltpu.VMEM((rows, width), bf16),
        pltpu.VMEM((edges, 128), bf16),
    )
    hot = pltpu.VMEM((rows, edges), bf16)
    return pl.pallas_call(
        chain_kernel,
        out_shape=(
            shape((rows, width), f32),
            shape((GROUP, basis_count * width), f32),
            shape((GROUP, width), f32),
            shape((GROUP, width), f32),
            shape((8, width), f32),
            shape((8, 128), f32),
            shape((8, width - 128), f32),
        ),
        in_specs=[whole] * 5 + [pl.BlockSpec(memory_space=pl.ANY)] * 5,
        out_specs=(whole,) * 7,
        scratch_shapes=[
            flat,
            pltpu.VMEM((width, basis_count * width), bf16),
            pltpu.VMEM((relations, width), bf16),
            pltpu.VMEM((width, width), bf16),
            pltpu.VMEM((width, width), bf16),
            wide, wide, wide, hot, hot, hot, hot,
            pltpu.VMEM((edges, 128), f32),
            flat, flat, flat,
            flat, flat, flat, flat,
            pltpu.VMEM((CHUNKS, rows, part), bf16),
            pltpu.VMEM((CHUNKS, rows, part), bf16),
            wide,
            pltpu.VMEM((CHUNKS, slots, part), bf16),
            pltpu.VMEM((CHUNKS, slots, part), bf16),
            pltpu.VMEM((edges, basis_count * width), bf16),
            pltpu.VMEM((width, edges), bf16),
            pltpu.VMEM((width, rows), bf16),
            pltpu.VMEM((relations, edges), bf16),
            flat, narrow, narrow,
            pltpu.VMEM((ents, GROUP, width), f32),
            pltpu.VMEM((2, 2, SIDE * SIDE, height, half), bf16),
            pltpu.VMEM((2, SIDE * SIDE, height, half), bf16),
            pltpu.VMEM((2, SIDE - 1, SIDE, height, half), bf16),
            pltpu.VMEM((2, SIDE, height, half), bf16),
            pltpu.VMEM((2, SIDE - 1, height, half), bf16),
            pltpu.VMEM((SIDE, 2, height, half), bf16),
            chunk_sem, chunk_sem, chunk_sem, chunk_sem,
            pltpu.SemaphoreType.DMA((5,)),
            two, two, two, two, two, two, two,
        ],
        compiler_params=pltpu.CompilerParams(
            collective_id=0, has_side_effects=True, vmem_limit_bytes=63 << 20
        ),
    )(*operands)


def per_device(
    states, cotangent, export_rows, edge_src, edge_dst, edge_rel, tile_count,
    basis, coef, rel_emb, self_weight, gate_weight, gate_bias,
):
    bf16, f32 = jnp.bfloat16, jnp.float32
    ent_count = lax.axis_size("ent")
    width = states.shape[2]
    basis_count = basis.shape[1] // width
    edges = edge_src.shape[1]
    live = jnp.arange(edges, dtype=jnp.int32) // TILE < tile_count[0, 0]
    ids = jnp.concatenate([export_rows, edge_src, jnp.where(live, edge_dst, -1), edge_rel], axis=0)
    padded = jnp.pad(coef, ((0, 0), (0, 128 - basis_count)))
    high = padded.astype(bf16)
    rest = padded - high.astype(f32)
    middle = rest.astype(bf16)
    low = (rest - middle.astype(f32)).astype(bf16)
    state_grad, basis_sum, self_sum, gate_sum, rel_sum, coef_sum, bias_sum = run_chain(
        states[0], ids, ids.T, jnp.stack([high, middle, low]), gate_bias[None],
        cotangent[0], basis, rel_emb, self_weight, gate_weight,
    )
    height = width // ent_count
    bias = jnp.concatenate([bias_sum[0], bias_sum[1, :128]])
    return (
        state_grad[None],
        basis_sum,
        self_sum,
        gate_sum,
        lax.dynamic_slice_in_dim(bias, lax.axis_index("ent") * height, height, 0),
        coef_sum[:, :basis_count],
        rel_sum,
    )


def solution(mesh):
    placed = (P("tm", "ent", None),) * 2 + (P("tm", "ent"),) * 5 + (P(),) * 6
    return jax.shard_map(
        per_device,
        mesh=mesh,
        in_specs=placed,
        out_specs=(
            P("tm", "ent", None),
            P("ent", None),
            P("ent", None),
            P("ent", None),
            P("ent"),
            P("ent", None),
            P("ent", None),
        ),
        check_vma=False,
    )
```

```python
import jax
import jax.numpy as jnp
from jax import lax
from jax.experimental import pallas as pl
from jax.experimental.pallas import tpu as pltpu
from jax.sharding import PartitionSpec as P

TILE = 128
MESH = pl.DeviceIdType.MESH
CHUNKS = 4
BLOCK = 256
SIDE = 4
GROUP = 16
PIECES = 4
EXPORT, SOURCE, TARGET, RELATION = range(4)
LAST = (((1,), (1,)), ((), ()))


def dot(a, b, dims=(((1,), (0,)), ((), ()))):
    return lax.dot_general(a, b, dims, preferred_element_type=jnp.float32)


def chain_kernel(
    state, ids_row, ids_col, coef_parts, gate_bias,
    cot_hbm, basis_hbm, rel_emb_hbm, self_hbm, gate_hbm,
    state_grad, basis_out, self_out, gate_out, rel_out, coef_out, bias_out,
    cot, basis, rel_emb, self_weight, gate_weight,
    row_factor, gate_factor, keep, target, source_t, early, exported_t, edge_coef,
    export_send, export_recv, edge_input,
    row_grad, gate_row, edge_grad, input_grad,
    handed, sending, total, slot_send, slot_recv,
    images, input_t, state_t, relation_t, scaled, coef_hi, coef_lo, small,
    packed, pair_recv, first_recv, first_sum, second_recv, shares,
    z_send_sem, z_recv_sem, a_send_sem, a_recv_sem, load_sem, export_sem,
    pair_sem, first_send_sem, first_recv_sem, second_send_sem, second_recv_sem, share_sem,
):
    bf16, f32 = jnp.bfloat16, jnp.float32
    t, me = lax.axis_index("tm"), lax.axis_index("ent")
    sections, ents = lax.axis_size("tm"), lax.axis_size("ent")
    rows, width = state.shape
    edges = slots = ids_row.shape[1]
    relations = rel_emb.shape[0]
    basis_count = basis.shape[1] // width
    share = slots // ents
    part = width // CHUNKS
    above = lax.rem(t + 1, sections)
    below = lax.rem(t + sections - 1, sections)

    barrier = pltpu.get_barrier_semaphore()

    def greet(k, carry):
        peer = lax.rem(me + k, ents)
        pl.semaphore_signal(barrier, inc=1, device_id=(t, peer), device_id_type=MESH)
        return carry

    lax.fori_loop(1, ents, greet, 0)
    pl.semaphore_signal(barrier, inc=1, device_id=(above, me), device_id_type=MESH)
    pl.semaphore_signal(barrier, inc=1, device_id=(below, me), device_id_type=MESH)
    opposite = lax.rem(t + 2, sections)
    pl.semaphore_signal(barrier, inc=1, device_id=(opposite, me), device_id_type=MESH)
    loads = [
        pltpu.make_async_copy(src, dst, load_sem.at[i])
        for i, (src, dst) in enumerate(
            [
                (rel_emb_hbm, rel_emb),
                (self_hbm, self_weight),
                (gate_hbm, gate_weight),
                (basis_hbm, basis),
                (cot_hbm, cot),
            ]
        )
    ]
    for load in loads:
        load.start()

    def pass_down(c):
        return pltpu.make_async_remote_copy(
            src_ref=sending.at[c],
            dst_ref=handed.at[c],
            send_sem=z_send_sem.at[c],
            recv_sem=z_recv_sem.at[c],
            device_id=(below, me),
            device_id_type=MESH,
        )

    def blocks(count, body):
        def step(i, carry):
            body(pl.ds(pl.multiple_of(i * BLOCK, BLOCK), BLOCK))
            return carry

        lax.fori_loop(0, count // BLOCK, step, 0)

    def one(mask):
        return jnp.where(mask, 1.0, 0.0).astype(bf16)

    def by_row(kind, r, count):
        lane = lax.broadcasted_iota(jnp.int32, (BLOCK, count), 1)
        return one(ids_col[r, kind : kind + 1] == lane)

    def by_column(kind, r):
        line = lax.broadcasted_iota(jnp.int32, (BLOCK, edges), 0) + r.start
        return one(ids_row[kind : kind + 1, :] == line)

    mine = pl.ds(pl.multiple_of(me * share, share), share)

    def export(r):
        export_send[r, :] = dot(by_row(EXPORT, r, rows), state[...]).astype(bf16)

    blocks(slots, export)
    pltpu.make_async_copy(export_send.at[mine], export_recv.at[mine], export_sem.at[1]).start()
    pl.semaphore_wait(barrier, ents + 2)

    def send_export(k, carry):
        peer = lax.rem(me + k, ents)
        pltpu.make_async_remote_copy(
            src_ref=export_send.at[pl.ds(pl.multiple_of(peer * share, share), share)],
            dst_ref=export_recv.at[mine],
            send_sem=export_sem.at[0],
            recv_sem=export_sem.at[1],
            device_id=(t, peer),
            device_id_type=MESH,
        ).start()
        return carry

    lax.fori_loop(1, ents, send_export, 0)
    for load in loads[:3]:
        load.wait()

    def by_edge(e):
        early[e, :] = by_row(SOURCE, e, slots)
        target[e, :] = by_row(TARGET, e, rows)
        relation = by_row(RELATION, e, relations)
        total[e, :] = dot(relation, rel_emb[...])
        edge_coef[e, :] = sum(dot(relation, coef_parts[i]) for i in range(3))

    blocks(edges, by_edge)

    def forms(r):
        exported_t[r, :] = by_column(TARGET, r)
        source_t[r, :] = by_column(SOURCE, r)
        state_grad[r, :] = dot(state[r, :], self_weight[...])
        keep[r, :] = jax.nn.sigmoid(dot(state[r, :], gate_weight[...]) + gate_bias[...])

    blocks(rows, forms)
    loads[3].wait()
    pltpu.make_async_copy(export_recv, export_recv, export_sem.at[1]).wait()

    def forward(e):
        value = (dot(early[e, :], export_recv[...]) + total[e, :]).astype(bf16)
        edge_input[e, :] = value
        message = 0.0
        for b in range(basis_count):
            at = slice(b * width, (b + 1) * width)
            image = dot(value, basis[:, at])
            images[e, at] = image.astype(bf16)
            message = message + edge_coef[e, b : b + 1] * image
        edge_grad[e, :] = message.astype(bf16)

    blocks(edges, forward)

    def factors(r):
        hot = exported_t[r, :]
        degree = 1.0 + dot(hot, jnp.ones((edges, 128), bf16))[:, :1]
        scale = 1.0 / degree
        aggregated = jnp.tanh((dot(hot, edge_grad[...]) + state_grad[r, :]) * scale)
        gate_open = keep[r, :]
        closed = 1.0 - gate_open
        row_factor[r, :] = gate_open * (1.0 - aggregated * aggregated) * scale
        gate_factor[r, :] = (aggregated - state[r, :].astype(f32)) * gate_open * closed
        keep[r, :] = closed

    blocks(rows, factors)
    loads[4].wait()

    for c in range(CHUNKS):
        cols = pl.ds(c * part, part)

        @pl.when(t < sections - 1)
        def _():
            pass_down(c).wait_recv()

        @pl.when(t == sections - 1)
        def _():
            handed[c] = jnp.zeros((rows, part), bf16)

        def elementwise(r):
            upstream = cot[r, cols].astype(f32) + handed[c, r, :].astype(f32)
            row_grad[r, cols] = (upstream * row_factor[r, cols]).astype(bf16)
            gate_row[r, cols] = (upstream * gate_factor[r, cols]).astype(bf16)
            state_grad[r, cols] = upstream * keep[r, cols]

        blocks(rows, elementwise)

        def through_basis(e):
            gathered = dot(target[e, :], row_grad[:, cols])
            edge_grad[e, cols] = gathered.astype(bf16)
            out = 0.0
            for b in range(basis_count):
                image_grad = (edge_coef[e, b : b + 1] * gathered).astype(bf16)
                at = slice(b * width + c * part, b * width + (c + 1) * part)
                out = out + dot(image_grad, basis[:, at], LAST)
            if c > 0:
                out = out + total[e, :]
            if c < CHUNKS - 1:
                total[e, :] = out
            else:
                input_grad[e, :] = out.astype(bf16)

        blocks(edges, through_basis)

    for c in range(CHUNKS):
        cols = pl.ds(c * part, part)

        def to_slots(r):
            slot_send[c, r, :] = dot(source_t[r, :], input_grad[:, cols]).astype(bf16)

        blocks(slots, to_slots)
        pltpu.make_async_copy(
            slot_send.at[c, mine], slot_recv.at[c, mine], a_recv_sem.at[c]
        ).start()

        def send(k, carry):
            peer = lax.rem(me + k, ents)
            pltpu.make_async_remote_copy(
                src_ref=slot_send.at[c, pl.ds(pl.multiple_of(peer * share, share), share)],
                dst_ref=slot_recv.at[c, mine],
                send_sem=a_send_sem.at[c],
                recv_sem=a_recv_sem.at[c],
                device_id=(t, peer),
                device_id_type=MESH,
            ).start()
            return carry

        lax.fori_loop(1, ents, send, 0)

    core = lax.rem(me, 2)
    y = lax.rem(me // 2, SIDE)
    x = me // (2 * SIDE)
    sibling = me + 1 - 2 * core
    half = width // 2

    def to_pair(offset):
        piece = pl.ds(offset, GROUP)
        return pltpu.make_async_remote_copy(
            src_ref=packed.at[1 - core, :, :, piece, :],
            dst_ref=pair_recv.at[:, :, piece, :],
            send_sem=pair_sem.at[0],
            recv_sem=pair_sem.at[1],
            device_id=(t, sibling),
            device_id_type=MESH,
        )

    def pack(offset, i, value):
        value = value.astype(bf16).reshape(SIDE, 2, GROUP, width)
        rows_at = pl.ds(offset, GROUP)
        for core_to in range(2):
            for y_to in range(SIDE):
                one = value[y_to, core_to]
                packed[core_to, 0, i * SIDE + y_to, rows_at, :] = one[:, :half]
                packed[core_to, 1, y_to * SIDE + i, rows_at, :] = one[:, half:]

    def term(offset, left, right):
        def step(i, carry):
            r = pl.ds(pl.multiple_of(i * 128, 128), 128)
            pack(offset, i, dot(left[r, :], right[...]))
            return carry

        lax.fori_loop(0, SIDE, step, 0)
        to_pair(offset).start()

    def weights():
        def turn(r):
            input_t[:, r] = edge_input[r, :].T
            state_t[:, r] = state[r, :].T

        blocks(edges, turn)
        relation_line = lax.broadcasted_iota(jnp.int32, (relations, edges), 0)
        relation_t[...] = one(ids_row[RELATION : RELATION + 1, :] == relation_line)
        for b in range(basis_count):

            def scale(e):
                scaled[e, :] = (edge_coef[e, b : b + 1] * edge_grad[e, :].astype(f32)).astype(bf16)

            blocks(edges, scale)
            term(b * GROUP, input_t, scaled)
        term(basis_count * GROUP, state_t, row_grad)
        term((basis_count + 1) * GROUP, state_t, gate_row)

        def inner(e):
            lane = lax.broadcasted_iota(jnp.int32, (BLOCK, 128), 1)
            out = jnp.zeros((BLOCK, 128), f32)
            gradient = edge_grad[e, :].astype(f32)
            for b in range(basis_count):
                product = gradient * images[e, b * width : (b + 1) * width].astype(f32)
                out = jnp.where(lane == b, jnp.sum(product, axis=1, keepdims=True), out)
            high = out.astype(bf16)
            coef_hi[e, :] = high
            coef_lo[e, :] = (out - high.astype(f32)).astype(bf16)

        blocks(edges, inner)
        bias = jnp.zeros((1, width), f32)
        for i in range(rows // BLOCK):
            piece = gate_row[i * BLOCK : (i + 1) * BLOCK, :].astype(f32)
            bias = bias + jnp.sum(piece, axis=0, keepdims=True)
        line = lax.broadcasted_iota(jnp.int32, (8, width - 128), 0)
        wrapped = jnp.concatenate([bias[:, width - 128 :]] * (width // 128 - 1), axis=1)
        tile = jnp.where(line == 0, bias[:, : width - 128], jnp.where(line == 1, wrapped, 0.0))
        small[:, 0:8, :] = dot(relation_t[...], input_grad[...]).reshape(ents, 8, width)
        coef_rows = dot(relation_t[...], coef_hi[...]) + dot(relation_t[...], coef_lo[...])
        small[:, 8:16, 0:128] = coef_rows.reshape(ents, 8, 128)
        small[:, 8:16, 128:] = jnp.broadcast_to(tile[None], (ents, 8, width - 128))

        def pack_small(i, carry):
            pack((basis_count + 2) * GROUP, i, small[pl.ds(i * 2 * SIDE, 2 * SIDE)])
            return carry

        lax.fori_loop(0, SIDE, pack_small, 0)
        to_pair((basis_count + 2) * GROUP).start()

    def local_part(r):
        state_grad[r, :] += dot(row_grad[r, :], self_weight[...], LAST) + dot(
            gate_row[r, :], gate_weight[...], LAST
        )
        exported_t[r, :] = by_column(EXPORT, r)

    blocks(rows, local_part)

    @pl.when(t == 0)
    def _():
        weights()

    for c in range(CHUNKS):
        cols = pl.ds(c * part, part)
        pltpu.make_async_copy(slot_recv.at[c], slot_recv.at[c], a_recv_sem.at[c]).wait()

        def to_rows(r):
            out = state_grad[r, cols] + dot(exported_t[r, :], slot_recv[c])
            state_grad[r, cols] = out
            sending[c, r, :] = out.astype(bf16)

        blocks(rows, to_rows)

        @pl.when(t > 0)
        def _():
            pass_down(c).start()

    @pl.when(t > 0)
    def _():
        weights()

    pltpu.make_async_copy(pair_recv, pair_recv, pair_sem.at[1]).wait()

    def chip(px, py):
        return (t, px * (2 * SIDE) + py * 2 + core)

    def other(h, k):
        return lax.rem((x if h == 0 else y) + k, SIDE)

    for h in range(2):

        def add_pair(i, carry):
            total_pair = packed[core, h, i].astype(f32) + pair_recv[h, i].astype(f32)
            packed[core, h, i] = total_pair.astype(bf16)
            return carry

        lax.fori_loop(0, SIDE * SIDE, add_pair, 0)
        for k in range(1, SIDE):
            to = other(h, k)
            pltpu.make_async_remote_copy(
                src_ref=packed.at[core, h, pl.ds(to * SIDE, SIDE)],
                dst_ref=first_recv.at[h, k - 1],
                send_sem=first_send_sem.at[h],
                recv_sem=first_recv_sem.at[h],
                device_id=chip(to, y) if h == 0 else chip(x, to),
                device_id_type=MESH,
            ).start()

    for h in range(2):
        pltpu.make_async_copy(first_recv.at[h], first_recv.at[h], first_recv_sem.at[h]).wait()

        def add_first(j, carry):
            out = packed[core, h, other(h, 0) * SIDE + j].astype(f32)
            for k in range(SIDE - 1):
                out = out + first_recv[h, k, j].astype(f32)
            first_sum[h, j] = out.astype(bf16)
            return carry

        lax.fori_loop(0, SIDE, add_first, 0)
        for k in range(1, SIDE):
            to = other(1 - h, k)
            pltpu.make_async_remote_copy(
                src_ref=first_sum.at[h, to],
                dst_ref=second_recv.at[h, k - 1],
                send_sem=second_send_sem.at[h],
                recv_sem=second_recv_sem.at[h],
                device_id=chip(x, to) if h == 0 else chip(to, y),
                device_id_type=MESH,
            ).start()

    for h in range(2):
        pltpu.make_async_copy(second_recv.at[h], second_recv.at[h], second_recv_sem.at[h]).wait()
        out = first_sum[h, other(1 - h, 0)].astype(f32)
        for k in range(SIDE - 1):
            out = out + second_recv[h, k].astype(f32)
        shares[t, h] = out.astype(bf16)
    for k in range(1, SIDE):
        pltpu.make_async_remote_copy(
            src_ref=shares.at[t],
            dst_ref=shares.at[t],
            send_sem=share_sem.at[0],
            recv_sem=share_sem.at[1],
            device_id=(lax.rem(t + k, sections), me),
            device_id_type=MESH,
        ).start()
    others = shares.at[pl.ds(0, sections - 1)]
    pltpu.make_async_copy(others, others, share_sem.at[1]).wait()
    for h in range(2):
        at = pl.ds(h * half, half)
        out = shares[0, h].astype(f32)
        for p in range(1, SIDE):
            out = out + shares[p, h].astype(f32)
        for b in range(basis_count):
            basis_out[:, b * width + h * half : b * width + (h + 1) * half] = out[
                b * GROUP : (b + 1) * GROUP
            ]
        top = basis_count * GROUP
        self_out[:, at] = out[top : top + GROUP]
        gate_out[:, at] = out[top + GROUP : top + 2 * GROUP]
        rel_out[:, at] = out[top + 2 * GROUP : top + 2 * GROUP + 8]
        rest = out[top + 2 * GROUP + 8 : top + 3 * GROUP]
        if h == 0:
            coef_out[...] = rest[:, :128]
            bias_out[:, : half - 128] = rest[:, 128:]
        else:
            bias_out[:, half - 128 :] = rest

    pltpu.make_async_copy(pair_recv, pair_recv, pair_sem.at[0]).wait()
    pltpu.make_async_copy(others, others, share_sem.at[0]).wait()
    for h in range(2):
        pltpu.make_async_copy(first_recv.at[h], first_recv.at[h], first_send_sem.at[h]).wait()
        pltpu.make_async_copy(second_recv.at[h], second_recv.at[h], second_send_sem.at[h]).wait()

    for c in range(CHUNKS):
        if c == 0:
            rest = export_send.at[pl.ds(0, slots - share)]
            pltpu.make_async_copy(rest, rest, export_sem.at[0]).wait()
        rest = slot_send.at[c, pl.ds(0, slots - share)]
        pltpu.make_async_copy(rest, rest, a_send_sem.at[c]).wait()

        @pl.when(t > 0)
        def _():
            pass_down(c).wait_send()


def run_chain(*operands):
    bf16, f32 = jnp.bfloat16, jnp.float32
    rows, width = operands[0].shape
    edges = slots = operands[1].shape[1]
    basis_count = operands[6].shape[1] // width
    relations = operands[7].shape[0]
    ents = lax.axis_size("ent")
    part, half = width // CHUNKS, width // 2
    height = (basis_count + 3) * GROUP
    shape = jax.ShapeDtypeStruct
    chunk_sem = pltpu.SemaphoreType.DMA((CHUNKS,))
    two = pltpu.SemaphoreType.DMA((2,))
    whole = pl.BlockSpec(memory_space=pltpu.VMEM)
    wide, flat, narrow = (
        pltpu.VMEM((rows, width), f32),
        pltpu.VMEM((rows, width), bf16),
        pltpu.VMEM((edges, 128), bf16),
    )
    hot = pltpu.VMEM((rows, edges), bf16)
    return pl.pallas_call(
        chain_kernel,
        out_shape=(
            shape((rows, width), f32),
            shape((GROUP, basis_count * width), f32),
            shape((GROUP, width), f32),
            shape((GROUP, width), f32),
            shape((8, width), f32),
            shape((8, 128), f32),
            shape((8, width - 128), f32),
        ),
        in_specs=[whole] * 5 + [pl.BlockSpec(memory_space=pl.ANY)] * 5,
        out_specs=(whole,) * 7,
        scratch_shapes=[
            flat,
            pltpu.VMEM((width, basis_count * width), bf16),
            pltpu.VMEM((relations, width), bf16),
            pltpu.VMEM((width, width), bf16),
            pltpu.VMEM((width, width), bf16),
            wide, wide, wide, hot, hot, hot, hot,
            pltpu.VMEM((edges, 128), f32),
            flat, flat, flat,
            flat, flat, flat, flat,
            pltpu.VMEM((CHUNKS, rows, part), bf16),
            pltpu.VMEM((CHUNKS, rows, part), bf16),
            wide,
            pltpu.VMEM((CHUNKS, slots, part), bf16),
            pltpu.VMEM((CHUNKS, slots, part), bf16),
            pltpu.VMEM((edges, basis_count * width), bf16),
            pltpu.VMEM((width, edges), bf16),
            pltpu.VMEM((width, rows), bf16),
            pltpu.VMEM((relations, edges), bf16),
            flat, narrow, narrow,
            pltpu.VMEM((ents, GROUP, width), f32),
            pltpu.VMEM((2, 2, SIDE * SIDE, height, half), bf16),
            pltpu.VMEM((2, SIDE * SIDE, height, half), bf16),
            pltpu.VMEM((2, SIDE - 1, SIDE, height, half), bf16),
            pltpu.VMEM((2, SIDE, height, half), bf16),
            pltpu.VMEM((2, SIDE - 1, height, half), bf16),
            pltpu.VMEM((SIDE, 2, height, half), bf16),
            chunk_sem, chunk_sem, chunk_sem, chunk_sem,
            pltpu.SemaphoreType.DMA((5,)),
            two, two, two, two, two, two, two,
        ],
        compiler_params=pltpu.CompilerParams(
            collective_id=0, has_side_effects=True, vmem_limit_bytes=63 << 20
        ),
    )(*operands)


def write_kernel(*refs):
    count = len(refs) // 2
    refs[count][...] = refs[0][...]

    @pl.when(pl.program_id(0) == 0)
    def _():
        for i in range(1, count):
            refs[count + i][...] = refs[i][...]


def write_out(*arrays):
    rows, width = arrays[0].shape
    specs = [pl.BlockSpec((rows // PIECES, width), lambda i: (i, 0))]
    specs += [pl.BlockSpec(array.shape, lambda i: (0, 0)) for array in arrays[1:]]
    return pl.pallas_call(
        write_kernel,
        grid=(PIECES,),
        out_shape=tuple(jax.ShapeDtypeStruct(array.shape, array.dtype) for array in arrays),
        in_specs=specs,
        out_specs=tuple(specs),
    )(*arrays)


def per_device(
    states, cotangent, export_rows, edge_src, edge_dst, edge_rel, tile_count,
    basis, coef, rel_emb, self_weight, gate_weight, gate_bias,
):
    bf16, f32 = jnp.bfloat16, jnp.float32
    ent_count = lax.axis_size("ent")
    width = states.shape[2]
    basis_count = basis.shape[1] // width
    edges = edge_src.shape[1]
    live = jnp.arange(edges, dtype=jnp.int32) // TILE < tile_count[0, 0]
    ids = jnp.concatenate([export_rows, edge_src, jnp.where(live, edge_dst, -1), edge_rel], axis=0)
    padded = jnp.pad(coef, ((0, 0), (0, 128 - basis_count)))
    high = padded.astype(bf16)
    rest = padded - high.astype(f32)
    middle = rest.astype(bf16)
    low = (rest - middle.astype(f32)).astype(bf16)
    state_grad, basis_sum, self_sum, gate_sum, rel_sum, coef_sum, bias_sum = run_chain(
        states[0], ids, ids.T, jnp.stack([high, middle, low]), gate_bias[None],
        cotangent[0], basis, rel_emb, self_weight, gate_weight,
    )
    state_grad, basis_sum, self_sum, gate_sum, rel_sum = write_out(
        state_grad, basis_sum, self_sum, gate_sum, rel_sum
    )
    height = width // ent_count
    bias = jnp.concatenate([bias_sum[0], bias_sum[1, :128]])
    return (
        state_grad[None],
        basis_sum,
        self_sum,
        gate_sum,
        lax.dynamic_slice_in_dim(bias, lax.axis_index("ent") * height, height, 0),
        coef_sum[:, :basis_count],
        rel_sum,
    )


def solution(mesh):
    placed = (P("tm", "ent", None),) * 2 + (P("tm", "ent"),) * 5 + (P(),) * 6
    return jax.shard_map(
        per_device,
        mesh=mesh,
        in_specs=placed,
        out_specs=(
            P("tm", "ent", None),
            P("ent", None),
            P("ent", None),
            P("ent", None),
            P("ent"),
            P("ent", None),
            P("ent", None),
        ),
        check_vma=False,
    )
```

```python
import jax
import jax.numpy as jnp
from jax import lax
from jax.experimental import pallas as pl
from jax.experimental.pallas import tpu as pltpu
from jax.sharding import PartitionSpec as P

TILE = 128
MESH = pl.DeviceIdType.MESH
CHUNKS = 4
BLOCK = 512
SIDE = 4
GROUP = 16
PIECES = 4
LONG_WAY = (256, 256, 256, 128)
EXPORT, SOURCE, TARGET, RELATION = range(4)
LAST = (((1,), (1,)), ((), ()))


def dot(a, b, dims=(((1,), (0,)), ((), ()))):
    return lax.dot_general(a, b, dims, preferred_element_type=jnp.float32)


def chain_kernel(
    state, ids_row, ids_col, coef_parts, gate_bias,
    cot_hbm, basis_hbm, rel_emb_hbm, self_hbm, gate_hbm,
    state_grad, basis_out, self_out, gate_out, rel_out, coef_out, bias_out,
    cot, basis, rel_emb, self_weight, gate_weight,
    row_factor, gate_factor, keep, target, source_t, early, exported_t, edge_coef,
    export_send, export_recv, edge_input,
    row_grad, gate_row, edge_grad, input_grad,
    handed, sending, relay, total, slot_send, slot_recv,
    images, input_t, state_t, relation_t, scaled, coef_hi, coef_lo, small,
    packed, pair_recv, first_recv, first_sum, second_recv, shares,
    z_send_sem, z_recv_sem, hop_send_sem, hop_recv_sem, a_send_sem, a_recv_sem, load_sem, export_sem,
    pair_sem, first_send_sem, first_recv_sem, second_send_sem, second_recv_sem, share_sem,
):
    bf16, f32 = jnp.bfloat16, jnp.float32
    t, me = lax.axis_index("tm"), lax.axis_index("ent")
    sections, ents = lax.axis_size("tm"), lax.axis_size("ent")
    rows, width = state.shape
    edges = slots = ids_row.shape[1]
    relations = rel_emb.shape[0]
    basis_count = basis.shape[1] // width
    share = slots // ents
    part = width // CHUNKS
    above = lax.rem(t + 1, sections)
    below = lax.rem(t + sections - 1, sections)

    barrier = pltpu.get_barrier_semaphore()

    def greet(k, carry):
        peer = lax.rem(me + k, ents)
        pl.semaphore_signal(barrier, inc=1, device_id=(t, peer), device_id_type=MESH)
        return carry

    lax.fori_loop(1, ents, greet, 0)
    pl.semaphore_signal(barrier, inc=1, device_id=(above, me), device_id_type=MESH)
    pl.semaphore_signal(barrier, inc=1, device_id=(below, me), device_id_type=MESH)
    opposite = lax.rem(t + 2, sections)
    pl.semaphore_signal(barrier, inc=1, device_id=(opposite, me), device_id_type=MESH)
    loads = [
        pltpu.make_async_copy(src, dst, load_sem.at[i])
        for i, (src, dst) in enumerate(
            [
                (rel_emb_hbm, rel_emb),
                (self_hbm, self_weight),
                (gate_hbm, gate_weight),
                (basis_hbm, basis),
                (cot_hbm, cot),
            ]
        )
    ]
    for load in loads:
        load.start()

    def pass_down(c):
        piece = pl.ds(0, rows - LONG_WAY[c])
        return pltpu.make_async_remote_copy(
            src_ref=sending.at[c, piece],
            dst_ref=handed.at[c, piece],
            send_sem=z_send_sem.at[c],
            recv_sem=z_recv_sem.at[c],
            device_id=(below, me),
            device_id_type=MESH,
        )

    def hop(c, leg):
        count = LONG_WAY[c]
        piece, held = pl.ds(rows - count, count), pl.ds(0, count)
        stops = [
            sending.at[c, piece], relay.at[0, c, held], relay.at[1, c, held], handed.at[c, piece]
        ]
        return pltpu.make_async_remote_copy(
            src_ref=stops[leg],
            dst_ref=stops[leg + 1],
            send_sem=hop_send_sem.at[leg, c],
            recv_sem=hop_recv_sem.at[leg, c],
            device_id=(above, me),
            device_id_type=MESH,
        )

    detours = [c for c in range(CHUNKS) if LONG_WAY[c] > 0]

    def pass_on(leg):
        for c in detours:
            hop(c, leg - 1).wait_recv()
            hop(c, leg).start()
        for c in detours:
            hop(c, leg).wait_send()

    def blocks(count, body):
        def step(i, carry):
            body(pl.ds(pl.multiple_of(i * BLOCK, BLOCK), BLOCK))
            return carry

        lax.fori_loop(0, count // BLOCK, step, 0)

    def one(mask):
        return jnp.where(mask, 1.0, 0.0).astype(bf16)

    def by_row(kind, r, count):
        lane = lax.broadcasted_iota(jnp.int32, (BLOCK, count), 1)
        return one(ids_col[r, kind : kind + 1] == lane)

    def by_column(kind, r):
        line = lax.broadcasted_iota(jnp.int32, (BLOCK, edges), 0) + r.start
        return one(ids_row[kind : kind + 1, :] == line)

    mine = pl.ds(pl.multiple_of(me * share, share), share)

    def export(r):
        export_send[r, :] = dot(by_row(EXPORT, r, rows), state[...]).astype(bf16)

    blocks(slots, export)
    pltpu.make_async_copy(export_send.at[mine], export_recv.at[mine], export_sem.at[1]).start()
    pl.semaphore_wait(barrier, ents + 2)

    def send_export(k, carry):
        peer = lax.rem(me + k, ents)
        pltpu.make_async_remote_copy(
            src_ref=export_send.at[pl.ds(pl.multiple_of(peer * share, share), share)],
            dst_ref=export_recv.at[mine],
            send_sem=export_sem.at[0],
            recv_sem=export_sem.at[1],
            device_id=(t, peer),
            device_id_type=MESH,
        ).start()
        return carry

    lax.fori_loop(1, ents, send_export, 0)
    for load in loads[:3]:
        load.wait()

    def by_edge(e):
        early[e, :] = by_row(SOURCE, e, slots)
        target[e, :] = by_row(TARGET, e, rows)
        relation = by_row(RELATION, e, relations)
        total[e, :] = dot(relation, rel_emb[...])
        edge_coef[e, :] = sum(dot(relation, coef_parts[i]) for i in range(3))

    blocks(edges, by_edge)

    def forms(r):
        exported_t[r, :] = by_column(TARGET, r)
        source_t[r, :] = by_column(SOURCE, r)
        state_grad[r, :] = dot(state[r, :], self_weight[...])
        keep[r, :] = jax.nn.sigmoid(dot(state[r, :], gate_weight[...]) + gate_bias[...])

    blocks(rows, forms)
    loads[3].wait()
    pltpu.make_async_copy(export_recv, export_recv, export_sem.at[1]).wait()

    def forward(e):
        value = (dot(early[e, :], export_recv[...]) + total[e, :]).astype(bf16)
        edge_input[e, :] = value
        message = 0.0
        for b in range(basis_count):
            at = slice(b * width, (b + 1) * width)
            image = dot(value, basis[:, at])
            images[e, at] = image.astype(bf16)
            message = message + edge_coef[e, b : b + 1] * image
        edge_grad[e, :] = message.astype(bf16)

    blocks(edges, forward)

    def factors(r):
        hot = exported_t[r, :]
        degree = 1.0 + dot(hot, jnp.ones((edges, 128), bf16))[:, :1]
        scale = 1.0 / degree
        aggregated = jnp.tanh((dot(hot, edge_grad[...]) + state_grad[r, :]) * scale)
        gate_open = keep[r, :]
        closed = 1.0 - gate_open
        row_factor[r, :] = gate_open * (1.0 - aggregated * aggregated) * scale
        gate_factor[r, :] = (aggregated - state[r, :].astype(f32)) * gate_open * closed
        keep[r, :] = closed

    blocks(rows, factors)
    loads[4].wait()

    @pl.when(t == 0)
    def _():
        pass_on(1)

    @pl.when(t <= 1)
    def _():
        pass_on(2)

    for c in range(CHUNKS):
        cols = pl.ds(c * part, part)

        @pl.when(t < sections - 1)
        def _():
            pass_down(c).wait_recv()
            if c in detours:
                hop(c, 2).wait_recv()

        @pl.when(t == sections - 1)
        def _():
            handed[c] = jnp.zeros((rows, part), bf16)

        def elementwise(r):
            upstream = cot[r, cols].astype(f32) + handed[c, r, :].astype(f32)
            row_grad[r, cols] = (upstream * row_factor[r, cols]).astype(bf16)
            gate_row[r, cols] = (upstream * gate_factor[r, cols]).astype(bf16)
            state_grad[r, cols] = upstream * keep[r, cols]

        blocks(rows, elementwise)

        def through_basis(e):
            gathered = dot(target[e, :], row_grad[:, cols])
            edge_grad[e, cols] = gathered.astype(bf16)
            out = 0.0
            for b in range(basis_count):
                image_grad = (edge_coef[e, b : b + 1] * gathered).astype(bf16)
                at = slice(b * width + c * part, b * width + (c + 1) * part)
                out = out + dot(image_grad, basis[:, at], LAST)
            if c > 0:
                out = out + total[e, :]
            if c < CHUNKS - 1:
                total[e, :] = out
            else:
                input_grad[e, :] = out.astype(bf16)

        blocks(edges, through_basis)

    for c in range(CHUNKS):
        cols = pl.ds(c * part, part)

        def to_slots(r):
            slot_send[c, r, :] = dot(source_t[r, :], input_grad[:, cols]).astype(bf16)

        blocks(slots, to_slots)
        pltpu.make_async_copy(
            slot_send.at[c, mine], slot_recv.at[c, mine], a_recv_sem.at[c]
        ).start()

        def send(k, carry):
            peer = lax.rem(me + k, ents)
            pltpu.make_async_remote_copy(
                src_ref=slot_send.at[c, pl.ds(pl.multiple_of(peer * share, share), share)],
                dst_ref=slot_recv.at[c, mine],
                send_sem=a_send_sem.at[c],
                recv_sem=a_recv_sem.at[c],
                device_id=(t, peer),
                device_id_type=MESH,
            ).start()
            return carry

        lax.fori_loop(1, ents, send, 0)

    core = lax.rem(me, 2)
    y = lax.rem(me // 2, SIDE)
    x = me // (2 * SIDE)
    sibling = me + 1 - 2 * core
    half = width // 2

    def to_pair(offset):
        piece = pl.ds(offset, GROUP)
        return pltpu.make_async_remote_copy(
            src_ref=packed.at[1 - core, :, :, piece, :],
            dst_ref=pair_recv.at[:, :, piece, :],
            send_sem=pair_sem.at[0],
            recv_sem=pair_sem.at[1],
            device_id=(t, sibling),
            device_id_type=MESH,
        )

    def pack(offset, i, value):
        value = value.astype(bf16).reshape(SIDE, 2, GROUP, width)
        rows_at = pl.ds(offset, GROUP)
        for core_to in range(2):
            for y_to in range(SIDE):
                one = value[y_to, core_to]
                packed[core_to, 0, i * SIDE + y_to, rows_at, :] = one[:, :half]
                packed[core_to, 1, y_to * SIDE + i, rows_at, :] = one[:, half:]

    def term(offset, left, right):
        def step(i, carry):
            r = pl.ds(pl.multiple_of(i * 128, 128), 128)
            pack(offset, i, dot(left[r, :], right[...]))
            return carry

        lax.fori_loop(0, SIDE, step, 0)
        to_pair(offset).start()

    def weights():
        def turn(r):
            input_t[:, r] = edge_input[r, :].T
            state_t[:, r] = state[r, :].T

        blocks(edges, turn)
        relation_line = lax.broadcasted_iota(jnp.int32, (relations, edges), 0)
        relation_t[...] = one(ids_row[RELATION : RELATION + 1, :] == relation_line)
        for b in range(basis_count):

            def scale(e):
                scaled[e, :] = (edge_coef[e, b : b + 1] * edge_grad[e, :].astype(f32)).astype(bf16)

            blocks(edges, scale)
            term(b * GROUP, input_t, scaled)
        term(basis_count * GROUP, state_t, row_grad)
        term((basis_count + 1) * GROUP, state_t, gate_row)

        def inner(e):
            lane = lax.broadcasted_iota(jnp.int32, (BLOCK, 128), 1)
            out = jnp.zeros((BLOCK, 128), f32)
            gradient = edge_grad[e, :].astype(f32)
            for b in range(basis_count):
                product = gradient * images[e, b * width : (b + 1) * width].astype(f32)
                out = jnp.where(lane == b, jnp.sum(product, axis=1, keepdims=True), out)
            high = out.astype(bf16)
            coef_hi[e, :] = high
            coef_lo[e, :] = (out - high.astype(f32)).astype(bf16)

        blocks(edges, inner)
        bias = jnp.zeros((1, width), f32)
        for i in range(rows // BLOCK):
            piece = gate_row[i * BLOCK : (i + 1) * BLOCK, :].astype(f32)
            bias = bias + jnp.sum(piece, axis=0, keepdims=True)
        line = lax.broadcasted_iota(jnp.int32, (8, width - 128), 0)
        wrapped = jnp.concatenate([bias[:, width - 128 :]] * (width // 128 - 1), axis=1)
        tile = jnp.where(line == 0, bias[:, : width - 128], jnp.where(line == 1, wrapped, 0.0))
        small[:, 0:8, :] = dot(relation_t[...], input_grad[...]).reshape(ents, 8, width)
        coef_rows = dot(relation_t[...], coef_hi[...]) + dot(relation_t[...], coef_lo[...])
        small[:, 8:16, 0:128] = coef_rows.reshape(ents, 8, 128)
        small[:, 8:16, 128:] = jnp.broadcast_to(tile[None], (ents, 8, width - 128))

        def pack_small(i, carry):
            pack((basis_count + 2) * GROUP, i, small[pl.ds(i * 2 * SIDE, 2 * SIDE)])
            return carry

        lax.fori_loop(0, SIDE, pack_small, 0)
        to_pair((basis_count + 2) * GROUP).start()

    def local_part(r):
        state_grad[r, :] += dot(row_grad[r, :], self_weight[...], LAST) + dot(
            gate_row[r, :], gate_weight[...], LAST
        )
        exported_t[r, :] = by_column(EXPORT, r)

    blocks(rows, local_part)

    def finish_rows(last):
        for c in range(CHUNKS):
            cols = pl.ds(c * part, part)
            pltpu.make_async_copy(slot_recv.at[c], slot_recv.at[c], a_recv_sem.at[c]).wait()

            def to_rows(r):
                out = state_grad[r, cols] + dot(exported_t[r, :], slot_recv[c])
                state_grad[r, cols] = out
                if not last:
                    sending[c, r, :] = out.astype(bf16)

            blocks(rows, to_rows)
            if not last:
                if c in detours:
                    hop(c, 0).start()
                pass_down(c).start()

    @pl.when(t == 0)
    def _():
        weights()

    @pl.when(t > 0)
    def _():
        finish_rows(False)
        weights()

    @pl.when(t >= 2)
    def _():
        pass_on(1)

    @pl.when(t == 3)
    def _():
        pass_on(2)

    pltpu.make_async_copy(pair_recv, pair_recv, pair_sem.at[1]).wait()

    def chip(px, py):
        return (t, px * (2 * SIDE) + py * 2 + core)

    def other(h, k):
        return lax.rem((x if h == 0 else y) + k, SIDE)

    for h in range(2):

        def add_pair(i, carry):
            total_pair = packed[core, h, i].astype(f32) + pair_recv[h, i].astype(f32)
            packed[core, h, i] = total_pair.astype(bf16)
            return carry

        lax.fori_loop(0, SIDE * SIDE, add_pair, 0)
        for k in range(1, SIDE):
            to = other(h, k)
            pltpu.make_async_remote_copy(
                src_ref=packed.at[core, h, pl.ds(to * SIDE, SIDE)],
                dst_ref=first_recv.at[h, k - 1],
                send_sem=first_send_sem.at[h],
                recv_sem=first_recv_sem.at[h],
                device_id=chip(to, y) if h == 0 else chip(x, to),
                device_id_type=MESH,
            ).start()

    @pl.when(t == 0)
    def _():
        finish_rows(True)

    for h in range(2):
        pltpu.make_async_copy(first_recv.at[h], first_recv.at[h], first_recv_sem.at[h]).wait()

        def add_first(j, carry):
            out = packed[core, h, other(h, 0) * SIDE + j].astype(f32)
            for k in range(SIDE - 1):
                out = out + first_recv[h, k, j].astype(f32)
            first_sum[h, j] = out.astype(bf16)
            return carry

        lax.fori_loop(0, SIDE, add_first, 0)
        for k in range(1, SIDE):
            to = other(1 - h, k)
            pltpu.make_async_remote_copy(
                src_ref=first_sum.at[h, to],
                dst_ref=second_recv.at[h, k - 1],
                send_sem=second_send_sem.at[h],
                recv_sem=second_recv_sem.at[h],
                device_id=chip(x, to) if h == 0 else chip(to, y),
                device_id_type=MESH,
            ).start()

    for h in range(2):
        pltpu.make_async_copy(second_recv.at[h], second_recv.at[h], second_recv_sem.at[h]).wait()
        out = first_sum[h, other(1 - h, 0)].astype(f32)
        for k in range(SIDE - 1):
            out = out + second_recv[h, k].astype(f32)
        shares[t, h] = out.astype(bf16)
    for k in range(1, SIDE):
        pltpu.make_async_remote_copy(
            src_ref=shares.at[t],
            dst_ref=shares.at[t],
            send_sem=share_sem.at[0],
            recv_sem=share_sem.at[1],
            device_id=(lax.rem(t + k, sections), me),
            device_id_type=MESH,
        ).start()
    others = shares.at[pl.ds(0, sections - 1)]
    pltpu.make_async_copy(others, others, share_sem.at[1]).wait()
    for h in range(2):
        at = pl.ds(h * half, half)
        out = shares[0, h].astype(f32)
        for p in range(1, SIDE):
            out = out + shares[p, h].astype(f32)
        for b in range(basis_count):
            basis_out[:, b * width + h * half : b * width + (h + 1) * half] = out[
                b * GROUP : (b + 1) * GROUP
            ]
        top = basis_count * GROUP
        self_out[:, at] = out[top : top + GROUP]
        gate_out[:, at] = out[top + GROUP : top + 2 * GROUP]
        rel_out[:, at] = out[top + 2 * GROUP : top + 2 * GROUP + 8]
        rest = out[top + 2 * GROUP + 8 : top + 3 * GROUP]
        if h == 0:
            coef_out[...] = rest[:, :128]
            bias_out[:, : half - 128] = rest[:, 128:]
        else:
            bias_out[:, half - 128 :] = rest

    pltpu.make_async_copy(pair_recv, pair_recv, pair_sem.at[0]).wait()
    pltpu.make_async_copy(others, others, share_sem.at[0]).wait()
    for h in range(2):
        pltpu.make_async_copy(first_recv.at[h], first_recv.at[h], first_send_sem.at[h]).wait()
        pltpu.make_async_copy(second_recv.at[h], second_recv.at[h], second_send_sem.at[h]).wait()

    for c in range(CHUNKS):
        if c == 0:
            rest = export_send.at[pl.ds(0, slots - share)]
            pltpu.make_async_copy(rest, rest, export_sem.at[0]).wait()
        rest = slot_send.at[c, pl.ds(0, slots - share)]
        pltpu.make_async_copy(rest, rest, a_send_sem.at[c]).wait()

        @pl.when(t > 0)
        def _():
            pass_down(c).wait_send()
            if c in detours:
                hop(c, 0).wait_send()


def run_chain(*operands):
    bf16, f32 = jnp.bfloat16, jnp.float32
    rows, width = operands[0].shape
    edges = slots = operands[1].shape[1]
    basis_count = operands[6].shape[1] // width
    relations = operands[7].shape[0]
    ents = lax.axis_size("ent")
    part, half = width // CHUNKS, width // 2
    height = (basis_count + 3) * GROUP
    shape = jax.ShapeDtypeStruct
    hop_sem = pltpu.SemaphoreType.DMA((3, CHUNKS))
    chunk_sem = pltpu.SemaphoreType.DMA((CHUNKS,))
    two = pltpu.SemaphoreType.DMA((2,))
    whole = pl.BlockSpec(memory_space=pltpu.VMEM)
    wide, flat, narrow = (
        pltpu.VMEM((rows, width), f32),
        pltpu.VMEM((rows, width), bf16),
        pltpu.VMEM((edges, 128), bf16),
    )
    hot = pltpu.VMEM((rows, edges), bf16)
    return pl.pallas_call(
        chain_kernel,
        out_shape=(
            shape((rows, width), f32),
            shape((GROUP, basis_count * width), f32),
            shape((GROUP, width), f32),
            shape((GROUP, width), f32),
            shape((8, width), f32),
            shape((8, 128), f32),
            shape((8, width - 128), f32),
        ),
        in_specs=[whole] * 5 + [pl.BlockSpec(memory_space=pl.ANY)] * 5,
        out_specs=(whole,) * 7,
        scratch_shapes=[
            flat,
            pltpu.VMEM((width, basis_count * width), bf16),
            pltpu.VMEM((relations, width), bf16),
            pltpu.VMEM((width, width), bf16),
            pltpu.VMEM((width, width), bf16),
            wide, wide, wide, hot, hot, hot, hot,
            pltpu.VMEM((edges, 128), f32),
            flat, flat, flat,
            flat, flat, flat, flat,
            pltpu.VMEM((CHUNKS, rows, part), bf16),
            pltpu.VMEM((CHUNKS, rows, part), bf16),
            pltpu.VMEM((2, CHUNKS, max(LONG_WAY), part), bf16),
            wide,
            pltpu.VMEM((CHUNKS, slots, part), bf16),
            pltpu.VMEM((CHUNKS, slots, part), bf16),
            pltpu.VMEM((edges, basis_count * width), bf16),
            pltpu.VMEM((width, edges), bf16),
            pltpu.VMEM((width, rows), bf16),
            pltpu.VMEM((relations, edges), bf16),
            flat, narrow, narrow,
            pltpu.VMEM((ents, GROUP, width), f32),
            pltpu.VMEM((2, 2, SIDE * SIDE, height, half), bf16),
            pltpu.VMEM((2, SIDE * SIDE, height, half), bf16),
            pltpu.VMEM((2, SIDE - 1, SIDE, height, half), bf16),
            pltpu.VMEM((2, SIDE, height, half), bf16),
            pltpu.VMEM((2, SIDE - 1, height, half), bf16),
            pltpu.VMEM((SIDE, 2, height, half), bf16),
            chunk_sem, chunk_sem, hop_sem, hop_sem, chunk_sem, chunk_sem,
            pltpu.SemaphoreType.DMA((5,)),
            two, two, two, two, two, two, two,
        ],
        compiler_params=pltpu.CompilerParams(
            collective_id=0, has_side_effects=True, vmem_limit_bytes=63 << 20
        ),
    )(*operands)


def write_kernel(*refs):
    count = len(refs) // 2
    refs[count][...] = refs[0][...]

    @pl.when(pl.program_id(0) == 0)
    def _():
        for i in range(1, count):
            refs[count + i][...] = refs[i][...]


def write_out(*arrays):
    rows, width = arrays[0].shape
    specs = [pl.BlockSpec((rows // PIECES, width), lambda i: (i, 0))]
    specs += [pl.BlockSpec(array.shape, lambda i: (0, 0)) for array in arrays[1:]]
    return pl.pallas_call(
        write_kernel,
        grid=(PIECES,),
        out_shape=tuple(jax.ShapeDtypeStruct(array.shape, array.dtype) for array in arrays),
        in_specs=specs,
        out_specs=tuple(specs),
    )(*arrays)


def per_device(
    states, cotangent, export_rows, edge_src, edge_dst, edge_rel, tile_count,
    basis, coef, rel_emb, self_weight, gate_weight, gate_bias,
):
    bf16, f32 = jnp.bfloat16, jnp.float32
    ent_count = lax.axis_size("ent")
    width = states.shape[2]
    basis_count = basis.shape[1] // width
    edges = edge_src.shape[1]
    live = jnp.arange(edges, dtype=jnp.int32) // TILE < tile_count[0, 0]
    ids = jnp.concatenate([export_rows, edge_src, jnp.where(live, edge_dst, -1), edge_rel], axis=0)
    padded = jnp.pad(coef, ((0, 0), (0, 128 - basis_count)))
    high = padded.astype(bf16)
    rest = padded - high.astype(f32)
    middle = rest.astype(bf16)
    low = (rest - middle.astype(f32)).astype(bf16)
    state_grad, basis_sum, self_sum, gate_sum, rel_sum, coef_sum, bias_sum = run_chain(
        states[0], ids, ids.T, jnp.stack([high, middle, low]), gate_bias[None],
        cotangent[0], basis, rel_emb, self_weight, gate_weight,
    )
    state_grad, basis_sum, self_sum, gate_sum, rel_sum = write_out(
        state_grad, basis_sum, self_sum, gate_sum, rel_sum
    )
    height = width // ent_count
    bias = jnp.concatenate([bias_sum[0], bias_sum[1, :128]])
    return (
        state_grad[None],
        basis_sum,
        self_sum,
        gate_sum,
        lax.dynamic_slice_in_dim(bias, lax.axis_index("ent") * height, height, 0),
        coef_sum[:, :basis_count],
        rel_sum,
    )


def solution(mesh):
    placed = (P("tm", "ent", None),) * 2 + (P("tm", "ent"),) * 5 + (P(),) * 6
    return jax.shard_map(
        per_device,
        mesh=mesh,
        in_specs=placed,
        out_specs=(
            P("tm", "ent", None),
            P("ent", None),
            P("ent", None),
            P("ent", None),
            P("ent"),
            P("ent", None),
            P("ent", None),
        ),
        check_vma=False,
    )
```

```python
import jax
import jax.numpy as jnp
from jax import lax
from jax.experimental import pallas as pl
from jax.experimental.pallas import tpu as pltpu
from jax.sharding import PartitionSpec as P

TILE = 128
MESH = pl.DeviceIdType.MESH
CHUNKS = 4
BLOCK = 512
SIDE = 4
GROUP = 16
PIECES = 4
LONG_WAY = (256, 256, 256, 128)
EXPORT, SOURCE, TARGET, RELATION = range(4)
LAST = (((1,), (1,)), ((), ()))


def dot(a, b, dims=(((1,), (0,)), ((), ()))):
    return lax.dot_general(a, b, dims, preferred_element_type=jnp.float32)


def chain_kernel(
    state, export_rows, edge_src, edge_dst, edge_rel, tile_count, coef_t, gate_bias,
    cot_hbm, basis_hbm, rel_emb_hbm, self_hbm, gate_hbm,
    state_grad, basis_out, self_out, gate_out, rel_out, coef_out, bias_out,
    cot, basis, rel_emb, self_weight, gate_weight,
    row_factor, gate_factor, keep, target, source_t, early, exported_t, edge_coef,
    export_send, export_recv, edge_input, ids_row, ids_col, coef_rows_in, coef_parts,
    row_grad, gate_row, edge_grad, input_grad,
    handed, sending, relay, total, slot_send, slot_recv,
    images, input_t, state_t, relation_t, scaled, coef_hi, coef_lo, small,
    packed, pair_recv, first_recv, first_sum, second_recv, shares,
    z_send_sem, z_recv_sem, hop_send_sem, hop_recv_sem, a_send_sem, a_recv_sem, load_sem, export_sem,
    pair_sem, first_send_sem, first_recv_sem, second_send_sem, second_recv_sem, share_sem,
):
    bf16, f32 = jnp.bfloat16, jnp.float32
    t, me = lax.axis_index("tm"), lax.axis_index("ent")
    sections, ents = lax.axis_size("tm"), lax.axis_size("ent")
    rows, width = state.shape
    edges = slots = export_rows.shape[1]
    relations = rel_emb.shape[0]
    basis_count = basis.shape[1] // width
    share = slots // ents
    part = width // CHUNKS
    above = lax.rem(t + 1, sections)
    below = lax.rem(t + sections - 1, sections)

    barrier = pltpu.get_barrier_semaphore()

    def greet(k, carry):
        peer = lax.rem(me + k, ents)
        pl.semaphore_signal(barrier, inc=1, device_id=(t, peer), device_id_type=MESH)
        return carry

    lax.fori_loop(1, ents, greet, 0)
    pl.semaphore_signal(barrier, inc=1, device_id=(above, me), device_id_type=MESH)
    pl.semaphore_signal(barrier, inc=1, device_id=(below, me), device_id_type=MESH)
    opposite = lax.rem(t + 2, sections)
    pl.semaphore_signal(barrier, inc=1, device_id=(opposite, me), device_id_type=MESH)
    loads = [
        pltpu.make_async_copy(src, dst, load_sem.at[i])
        for i, (src, dst) in enumerate(
            [
                (rel_emb_hbm, rel_emb),
                (self_hbm, self_weight),
                (gate_hbm, gate_weight),
                (basis_hbm, basis),
                (cot_hbm, cot),
            ]
        )
    ]
    for load in loads:
        load.start()

    def pass_down(c):
        piece = pl.ds(0, rows - LONG_WAY[c])
        return pltpu.make_async_remote_copy(
            src_ref=sending.at[c, piece],
            dst_ref=handed.at[c, piece],
            send_sem=z_send_sem.at[c],
            recv_sem=z_recv_sem.at[c],
            device_id=(below, me),
            device_id_type=MESH,
        )

    def hop(c, leg):
        count = LONG_WAY[c]
        piece, held = pl.ds(rows - count, count), pl.ds(0, count)
        stops = [
            sending.at[c, piece], relay.at[0, c, held], relay.at[1, c, held], handed.at[c, piece]
        ]
        return pltpu.make_async_remote_copy(
            src_ref=stops[leg],
            dst_ref=stops[leg + 1],
            send_sem=hop_send_sem.at[leg, c],
            recv_sem=hop_recv_sem.at[leg, c],
            device_id=(above, me),
            device_id_type=MESH,
        )

    detours = [c for c in range(CHUNKS) if LONG_WAY[c] > 0]

    def pass_on(leg):
        for c in detours:
            hop(c, leg - 1).wait_recv()
            hop(c, leg).start()
        for c in detours:
            hop(c, leg).wait_send()

    def blocks(count, body):
        def step(i, carry):
            body(pl.ds(pl.multiple_of(i * BLOCK, BLOCK), BLOCK))
            return carry

        lax.fori_loop(0, count // BLOCK, step, 0)

    ids_row[...] = jnp.zeros_like(ids_row)
    live = lax.broadcasted_iota(jnp.int32, (1, edges), 1) < tile_count[...] * TILE
    ids_row[EXPORT : EXPORT + 1, :] = export_rows[...]
    ids_row[SOURCE : SOURCE + 1, :] = edge_src[...]
    ids_row[TARGET : TARGET + 1, :] = jnp.where(live, edge_dst[...], -1)
    ids_row[RELATION : RELATION + 1, :] = edge_rel[...]
    ids_col[...] = ids_row[...].T

    def one(mask):
        return jnp.where(mask, 1.0, 0.0).astype(bf16)

    def by_row(kind, r, count):
        lane = lax.broadcasted_iota(jnp.int32, (BLOCK, count), 1)
        return one(ids_col[r, kind : kind + 1] == lane)

    def by_column(kind, r):
        line = lax.broadcasted_iota(jnp.int32, (BLOCK, edges), 0) + r.start
        return one(ids_row[kind : kind + 1, :] == line)

    mine = pl.ds(pl.multiple_of(me * share, share), share)

    def export(r):
        export_send[r, :] = dot(by_row(EXPORT, r, rows), state[...]).astype(bf16)

    blocks(slots, export)
    pltpu.make_async_copy(export_send.at[mine], export_recv.at[mine], export_sem.at[1]).start()
    pl.semaphore_wait(barrier, ents + 2)

    def send_export(k, carry):
        peer = lax.rem(me + k, ents)
        pltpu.make_async_remote_copy(
            src_ref=export_send.at[pl.ds(pl.multiple_of(peer * share, share), share)],
            dst_ref=export_recv.at[mine],
            send_sem=export_sem.at[0],
            recv_sem=export_sem.at[1],
            device_id=(t, peer),
            device_id_type=MESH,
        ).start()
        return carry

    lax.fori_loop(1, ents, send_export, 0)
    for load in loads[:3]:
        load.wait()
    coef_parts[...] = jnp.zeros_like(coef_parts)
    coef_rows_in[...] = jnp.zeros_like(coef_rows_in)
    coef_rows_in[:basis_count, :] = coef_t[...]
    left_over = coef_rows_in[...].T
    for i in range(3):
        kept = left_over.astype(bf16).astype(f32)
        coef_parts[i, :, :8] = kept
        left_over = left_over - kept

    def by_edge(e):
        early[e, :] = by_row(SOURCE, e, slots)
        target[e, :] = by_row(TARGET, e, rows)
        relation = by_row(RELATION, e, relations)
        total[e, :] = dot(relation, rel_emb[...])
        edge_coef[e, :] = sum(
            dot(relation, coef_parts[i].astype(bf16)) for i in range(3)
        )

    blocks(edges, by_edge)

    def forms(r):
        exported_t[r, :] = by_column(TARGET, r)
        source_t[r, :] = by_column(SOURCE, r)
        state_grad[r, :] = dot(state[r, :], self_weight[...])
        keep[r, :] = jax.nn.sigmoid(dot(state[r, :], gate_weight[...]) + gate_bias[...])

    blocks(rows, forms)
    loads[3].wait()
    pltpu.make_async_copy(export_recv, export_recv, export_sem.at[1]).wait()

    def forward(e):
        value = (dot(early[e, :], export_recv[...]) + total[e, :]).astype(bf16)
        edge_input[e, :] = value
        message = 0.0
        for b in range(basis_count):
            at = slice(b * width, (b + 1) * width)
            image = dot(value, basis[:, at])
            images[e, at] = image.astype(bf16)
            message = message + edge_coef[e, b : b + 1] * image
        edge_grad[e, :] = message.astype(bf16)

    blocks(edges, forward)

    def factors(r):
        hot = exported_t[r, :]
        degree = 1.0 + dot(hot, jnp.ones((edges, 128), bf16))[:, :1]
        scale = 1.0 / degree
        aggregated = jnp.tanh((dot(hot, edge_grad[...]) + state_grad[r, :]) * scale)
        gate_open = keep[r, :]
        closed = 1.0 - gate_open
        row_factor[r, :] = gate_open * (1.0 - aggregated * aggregated) * scale
        gate_factor[r, :] = (aggregated - state[r, :].astype(f32)) * gate_open * closed
        keep[r, :] = closed

    blocks(rows, factors)
    loads[4].wait()

    def turned():
        def turn(r):
            input_t[:, r] = edge_input[r, :].T
            state_t[:, r] = state[r, :].T

        blocks(edges, turn)
        relation_line = lax.broadcasted_iota(jnp.int32, (relations, edges), 0)
        relation_t[...] = one(ids_row[RELATION : RELATION + 1, :] == relation_line)

    @pl.when(t < sections - 1)
    def _():
        turned()

    @pl.when(t == 0)
    def _():
        pass_on(1)

    @pl.when(t <= 1)
    def _():
        pass_on(2)

    for c in range(CHUNKS):
        cols = pl.ds(c * part, part)

        @pl.when(t < sections - 1)
        def _():
            pass_down(c).wait_recv()
            if c in detours:
                hop(c, 2).wait_recv()

        @pl.when(t == sections - 1)
        def _():
            handed[c] = jnp.zeros((rows, part), bf16)

        def elementwise(r):
            upstream = cot[r, cols].astype(f32) + handed[c, r, :].astype(f32)
            row_grad[r, cols] = (upstream * row_factor[r, cols]).astype(bf16)
            gate_row[r, cols] = (upstream * gate_factor[r, cols]).astype(bf16)
            state_grad[r, cols] = upstream * keep[r, cols]

        blocks(rows, elementwise)

        def through_basis(e):
            gathered = dot(target[e, :], row_grad[:, cols])
            edge_grad[e, cols] = gathered.astype(bf16)
            out = 0.0
            for b in range(basis_count):
                image_grad = (edge_coef[e, b : b + 1] * gathered).astype(bf16)
                at = slice(b * width + c * part, b * width + (c + 1) * part)
                out = out + dot(image_grad, basis[:, at], LAST)
            if c > 0:
                out = out + total[e, :]
            if c < CHUNKS - 1:
                total[e, :] = out
            else:
                input_grad[e, :] = out.astype(bf16)

        blocks(edges, through_basis)

    for c in range(CHUNKS):
        cols = pl.ds(c * part, part)

        def to_slots(r):
            slot_send[c, r, :] = dot(source_t[r, :], input_grad[:, cols]).astype(bf16)

        blocks(slots, to_slots)
        pltpu.make_async_copy(
            slot_send.at[c, mine], slot_recv.at[c, mine], a_recv_sem.at[c]
        ).start()

        def send(k, carry):
            peer = lax.rem(me + k, ents)
            pltpu.make_async_remote_copy(
                src_ref=slot_send.at[c, pl.ds(pl.multiple_of(peer * share, share), share)],
                dst_ref=slot_recv.at[c, mine],
                send_sem=a_send_sem.at[c],
                recv_sem=a_recv_sem.at[c],
                device_id=(t, peer),
                device_id_type=MESH,
            ).start()
            return carry

        lax.fori_loop(1, ents, send, 0)

    core = lax.rem(me, 2)
    y = lax.rem(me // 2, SIDE)
    x = me // (2 * SIDE)
    sibling = me + 1 - 2 * core
    half = width // 2

    def to_pair(offset):
        piece = pl.ds(offset, GROUP)
        return pltpu.make_async_remote_copy(
            src_ref=packed.at[1 - core, :, :, piece, :],
            dst_ref=pair_recv.at[:, :, piece, :],
            send_sem=pair_sem.at[0],
            recv_sem=pair_sem.at[1],
            device_id=(t, sibling),
            device_id_type=MESH,
        )

    def pack(offset, i, value):
        value = value.astype(bf16).reshape(SIDE, 2, GROUP, width)
        rows_at = pl.ds(offset, GROUP)
        for core_to in range(2):
            for y_to in range(SIDE):
                one = value[y_to, core_to]
                packed[core_to, 0, i * SIDE + y_to, rows_at, :] = one[:, :half]
                packed[core_to, 1, y_to * SIDE + i, rows_at, :] = one[:, half:]

    def term(offset, left, right):
        value = dot(left[...], right[...])
        for i in range(SIDE):
            pack(offset, i, value[i * 128 : (i + 1) * 128])
        to_pair(offset).start()

    def weights():
        @pl.when(t == sections - 1)
        def _():
            turned()

        for b in range(basis_count):

            def scale(e):
                scaled[e, :] = (edge_coef[e, b : b + 1] * edge_grad[e, :].astype(f32)).astype(bf16)

            blocks(edges, scale)
            term(b * GROUP, input_t, scaled)
        term(basis_count * GROUP, state_t, row_grad)
        term((basis_count + 1) * GROUP, state_t, gate_row)

        def inner(e):
            lane = lax.broadcasted_iota(jnp.int32, (BLOCK, 128), 1)
            out = jnp.zeros((BLOCK, 128), f32)
            gradient = edge_grad[e, :].astype(f32)
            for b in range(basis_count):
                product = gradient * images[e, b * width : (b + 1) * width].astype(f32)
                out = jnp.where(lane == b, jnp.sum(product, axis=1, keepdims=True), out)
            high = out.astype(bf16)
            coef_hi[e, :] = high
            coef_lo[e, :] = (out - high.astype(f32)).astype(bf16)

        blocks(edges, inner)
        bias = jnp.zeros((1, width), f32)
        for i in range(rows // BLOCK):
            piece = gate_row[i * BLOCK : (i + 1) * BLOCK, :].astype(f32)
            bias = bias + jnp.sum(piece, axis=0, keepdims=True)
        line = lax.broadcasted_iota(jnp.int32, (8, width - 128), 0)
        wrapped = jnp.concatenate([bias[:, width - 128 :]] * (width // 128 - 1), axis=1)
        tile = jnp.where(line == 0, bias[:, : width - 128], jnp.where(line == 1, wrapped, 0.0))
        small[:, 0:8, :] = dot(relation_t[...], input_grad[...]).reshape(ents, 8, width)
        coef_rows = dot(relation_t[...], coef_hi[...]) + dot(relation_t[...], coef_lo[...])
        small[:, 8:16, 0:128] = coef_rows.reshape(ents, 8, 128)
        small[:, 8:16, 128:] = jnp.broadcast_to(tile[None], (ents, 8, width - 128))

        def pack_small(i, carry):
            pack((basis_count + 2) * GROUP, i, small[pl.ds(i * 2 * SIDE, 2 * SIDE)])
            return carry

        lax.fori_loop(0, SIDE, pack_small, 0)
        to_pair((basis_count + 2) * GROUP).start()

    def local_part(r):
        state_grad[r, :] += dot(row_grad[r, :], self_weight[...], LAST) + dot(
            gate_row[r, :], gate_weight[...], LAST
        )
        exported_t[r, :] = by_column(EXPORT, r)

    def finish_rows(last):
        blocks(rows, local_part)
        for c in range(CHUNKS):
            cols = pl.ds(c * part, part)
            pltpu.make_async_copy(slot_recv.at[c], slot_recv.at[c], a_recv_sem.at[c]).wait()

            def to_rows(r):
                out = state_grad[r, cols] + dot(exported_t[r, :], slot_recv[c])
                state_grad[r, cols] = out
                if not last:
                    sending[c, r, :] = out.astype(bf16)

            blocks(rows, to_rows)
            if not last:
                if c in detours:
                    hop(c, 0).start()
                pass_down(c).start()

    @pl.when(t == 0)
    def _():
        weights()

    @pl.when(t > 0)
    def _():
        finish_rows(False)
        weights()

    @pl.when(t >= 2)
    def _():
        pass_on(1)

    @pl.when(t == 3)
    def _():
        pass_on(2)

    pltpu.make_async_copy(pair_recv, pair_recv, pair_sem.at[1]).wait()

    def chip(px, py):
        return (t, px * (2 * SIDE) + py * 2 + core)

    def other(h, k):
        return lax.rem((x if h == 0 else y) + k, SIDE)

    for h in range(2):

        def add_pair(i, carry):
            total_pair = packed[core, h, i].astype(f32) + pair_recv[h, i].astype(f32)
            packed[core, h, i] = total_pair.astype(bf16)
            return carry

        lax.fori_loop(0, SIDE * SIDE, add_pair, 0)
        for k in range(1, SIDE):
            to = other(h, k)
            pltpu.make_async_remote_copy(
                src_ref=packed.at[core, h, pl.ds(to * SIDE, SIDE)],
                dst_ref=first_recv.at[h, k - 1],
                send_sem=first_send_sem.at[h],
                recv_sem=first_recv_sem.at[h],
                device_id=chip(to, y) if h == 0 else chip(x, to),
                device_id_type=MESH,
            ).start()

    @pl.when(t == 0)
    def _():
        finish_rows(True)

    for h in range(2):
        pltpu.make_async_copy(first_recv.at[h], first_recv.at[h], first_recv_sem.at[h]).wait()

        def add_first(j, carry):
            out = packed[core, h, other(h, 0) * SIDE + j].astype(f32)
            for k in range(SIDE - 1):
                out = out + first_recv[h, k, j].astype(f32)
            first_sum[h, j] = out.astype(bf16)
            return carry

        lax.fori_loop(0, SIDE, add_first, 0)
        for k in range(1, SIDE):
            to = other(1 - h, k)
            pltpu.make_async_remote_copy(
                src_ref=first_sum.at[h, to],
                dst_ref=second_recv.at[h, k - 1],
                send_sem=second_send_sem.at[h],
                recv_sem=second_recv_sem.at[h],
                device_id=chip(x, to) if h == 0 else chip(to, y),
                device_id_type=MESH,
            ).start()

    for h in range(2):
        pltpu.make_async_copy(second_recv.at[h], second_recv.at[h], second_recv_sem.at[h]).wait()
        out = first_sum[h, other(1 - h, 0)].astype(f32)
        for k in range(SIDE - 1):
            out = out + second_recv[h, k].astype(f32)
        shares[t, h] = out.astype(bf16)
    for k in range(1, SIDE):
        pltpu.make_async_remote_copy(
            src_ref=shares.at[t],
            dst_ref=shares.at[t],
            send_sem=share_sem.at[0],
            recv_sem=share_sem.at[1],
            device_id=(lax.rem(t + k, sections), me),
            device_id_type=MESH,
        ).start()
    others = shares.at[pl.ds(0, sections - 1)]
    pltpu.make_async_copy(others, others, share_sem.at[1]).wait()
    for h in range(2):
        at = pl.ds(h * half, half)
        out = shares[0, h].astype(f32)
        for p in range(1, SIDE):
            out = out + shares[p, h].astype(f32)
        for b in range(basis_count):
            basis_out[:, b * width + h * half : b * width + (h + 1) * half] = out[
                b * GROUP : (b + 1) * GROUP
            ]
        top = basis_count * GROUP
        self_out[:, at] = out[top : top + GROUP]
        gate_out[:, at] = out[top + GROUP : top + 2 * GROUP]
        rel_out[:, at] = out[top + 2 * GROUP : top + 2 * GROUP + 8]
        rest = out[top + 2 * GROUP + 8 : top + 3 * GROUP]
        if h == 0:
            coef_out[...] = rest[:, :128]
            bias_out[:, : half - 128] = rest[:, 128:]
        else:
            bias_out[:, half - 128 :] = rest

    pltpu.make_async_copy(pair_recv, pair_recv, pair_sem.at[0]).wait()
    pltpu.make_async_copy(others, others, share_sem.at[0]).wait()
    for h in range(2):
        pltpu.make_async_copy(first_recv.at[h], first_recv.at[h], first_send_sem.at[h]).wait()
        pltpu.make_async_copy(second_recv.at[h], second_recv.at[h], second_send_sem.at[h]).wait()

    for c in range(CHUNKS):
        if c == 0:
            rest = export_send.at[pl.ds(0, slots - share)]
            pltpu.make_async_copy(rest, rest, export_sem.at[0]).wait()
        rest = slot_send.at[c, pl.ds(0, slots - share)]
        pltpu.make_async_copy(rest, rest, a_send_sem.at[c]).wait()

        @pl.when(t > 0)
        def _():
            pass_down(c).wait_send()
            if c in detours:
                hop(c, 0).wait_send()


def run_chain(*operands):
    bf16, f32 = jnp.bfloat16, jnp.float32
    rows, width = operands[0].shape
    edges = slots = operands[1].shape[1]
    basis_count, relations = operands[6].shape
    ents = lax.axis_size("ent")
    part, half = width // CHUNKS, width // 2
    height = (basis_count + 3) * GROUP
    shape = jax.ShapeDtypeStruct
    hop_sem = pltpu.SemaphoreType.DMA((3, CHUNKS))
    chunk_sem = pltpu.SemaphoreType.DMA((CHUNKS,))
    two = pltpu.SemaphoreType.DMA((2,))
    whole = pl.BlockSpec(memory_space=pltpu.VMEM)
    wide, flat, narrow = (
        pltpu.VMEM((rows, width), f32),
        pltpu.VMEM((rows, width), bf16),
        pltpu.VMEM((edges, 128), bf16),
    )
    hot = pltpu.VMEM((rows, edges), bf16)
    return pl.pallas_call(
        chain_kernel,
        out_shape=(
            shape((rows, width), f32),
            shape((GROUP, basis_count * width), f32),
            shape((GROUP, width), f32),
            shape((GROUP, width), f32),
            shape((8, width), f32),
            shape((8, 128), f32),
            shape((8, width - 128), f32),
        ),
        in_specs=[whole] * 8 + [pl.BlockSpec(memory_space=pl.ANY)] * 5,
        out_specs=(whole,) * 7,
        scratch_shapes=[
            flat,
            pltpu.VMEM((width, basis_count * width), bf16),
            pltpu.VMEM((relations, width), bf16),
            pltpu.VMEM((width, width), bf16),
            pltpu.VMEM((width, width), bf16),
            wide, wide, wide, hot, hot, hot, hot,
            pltpu.VMEM((edges, 128), f32),
            flat, flat, flat,
            pltpu.VMEM((8, edges), jnp.int32),
            pltpu.VMEM((edges, 8), jnp.int32),
            pltpu.VMEM((8, relations), f32),
            pltpu.VMEM((3, relations, 128), f32),
            flat, flat, flat, flat,
            pltpu.VMEM((CHUNKS, rows, part), bf16),
            pltpu.VMEM((CHUNKS, rows, part), bf16),
            pltpu.VMEM((2, CHUNKS, max(LONG_WAY), part), bf16),
            wide,
            pltpu.VMEM((CHUNKS, slots, part), bf16),
            pltpu.VMEM((CHUNKS, slots, part), bf16),
            pltpu.VMEM((edges, basis_count * width), bf16),
            pltpu.VMEM((width, edges), bf16),
            pltpu.VMEM((width, rows), bf16),
            pltpu.VMEM((relations, edges), bf16),
            flat, narrow, narrow,
            pltpu.VMEM((ents, GROUP, width), f32),
            pltpu.VMEM((2, 2, SIDE * SIDE, height, half), bf16),
            pltpu.VMEM((2, SIDE * SIDE, height, half), bf16),
            pltpu.VMEM((2, SIDE - 1, SIDE, height, half), bf16),
            pltpu.VMEM((2, SIDE, height, half), bf16),
            pltpu.VMEM((2, SIDE - 1, height, half), bf16),
            pltpu.VMEM((SIDE, 2, height, half), bf16),
            chunk_sem, chunk_sem, hop_sem, hop_sem, chunk_sem, chunk_sem,
            pltpu.SemaphoreType.DMA((5,)),
            two, two, two, two, two, two, two,
        ],
        compiler_params=pltpu.CompilerParams(
            collective_id=0, has_side_effects=True, vmem_limit_bytes=63 << 20
        ),
    )(*operands)


def write_kernel(*refs):
    count = len(refs) // 2
    refs[count][...] = refs[0][...]

    @pl.when(pl.program_id(0) == 0)
    def _():
        for i in range(1, count - 2):
            refs[count + i][...] = refs[i][...]
        coef_in, bias_in, coef_out, bias_out = (refs[i] for i in (count - 2, count - 1, -2, -1))
        coef_out[...] = coef_in[...].T[: coef_out.shape[0]]
        bias = bias_in[...]
        bias = jnp.concatenate([bias, jnp.roll(bias[:, :128], -1, axis=0)], axis=1)
        width = bias.shape[1]
        share = bias_out.shape[1]
        shift = lax.rem(width - lax.axis_index("ent") * share, width)
        bias_out[...] = pltpu.roll(bias, shift, 1)[:1, :share]


def write_out(basis_count, *arrays):
    rows, width = arrays[0].shape
    shapes = [array.shape for array in arrays]
    results = shapes[:-2] + [(basis_count, 8), (1, width // lax.axis_size("ent"))]

    def specs(sizes):
        rest = [pl.BlockSpec(size, lambda i: (0, 0)) for size in sizes[1:]]
        return [pl.BlockSpec((rows // PIECES, width), lambda i: (i, 0))] + rest

    return pl.pallas_call(
        write_kernel,
        grid=(PIECES,),
        out_shape=tuple(jax.ShapeDtypeStruct(size, jnp.float32) for size in results),
        in_specs=specs(shapes),
        out_specs=tuple(specs(results)),
    )(*arrays)


def per_device(
    states, cotangent, export_rows, edge_src, edge_dst, edge_rel, tile_count,
    basis, coef, rel_emb, self_weight, gate_weight, gate_bias,
):
    basis_count = coef.shape[1]
    sums = run_chain(
        states[0], export_rows, edge_src, edge_dst, edge_rel, tile_count, coef.T, gate_bias[None],
        cotangent[0], basis, rel_emb, self_weight, gate_weight,
    )
    state_grad, basis_sum, self_sum, gate_sum, rel_sum, coef_t, bias = write_out(basis_count, *sums)
    return state_grad[None], basis_sum, self_sum, gate_sum, bias[0], coef_t.T, rel_sum


def solution(mesh):
    placed = (P("tm", "ent", None),) * 2 + (P("tm", "ent"),) * 5 + (P(),) * 6
    return jax.shard_map(
        per_device,
        mesh=mesh,
        in_specs=placed,
        out_specs=(
            P("tm", "ent", None),
            P("ent", None),
            P("ent", None),
            P("ent", None),
            P("ent"),
            P("ent", None),
            P("ent", None),
        ),
        check_vma=False,
    )
```

```python
import jax
import jax.numpy as jnp
from jax import lax
from jax.experimental import pallas as pl
from jax.experimental.pallas import tpu as pltpu
from jax.sharding import PartitionSpec as P

TILE = 128
MESH = pl.DeviceIdType.MESH
CHUNKS = 4
BLOCK = 512
SIDE = 4
GROUP = 16
PIECES = 2
LONG_WAY = (256, 256, 256, 128)
EXPORT, SOURCE, TARGET, RELATION = range(4)
LAST = (((1,), (1,)), ((), ()))


def dot(a, b, dims=(((1,), (0,)), ((), ()))):
    return lax.dot_general(a, b, dims, preferred_element_type=jnp.float32)


def chain_kernel(
    state, export_rows, edge_src, edge_dst, edge_rel, tile_count, coef_t, gate_bias,
    cot_hbm, basis_hbm, rel_emb_hbm, self_hbm, gate_hbm,
    state_grad, basis_out, self_out, gate_out, rel_out, coef_out, bias_out,
    cot, basis, rel_emb, self_weight, gate_weight,
    row_factor, gate_factor, keep, target, source_t, early, exported_t, edge_coef,
    export_send, export_recv, edge_input, ids_row, ids_col, coef_rows_in, coef_parts,
    row_grad, gate_row, edge_grad, input_grad,
    handed, sending, relay, total, slot_send, slot_recv,
    images, input_t, state_t, relation_t, scaled, coef_hi, coef_lo, small,
    packed, pair_recv, first_recv, first_sum, second_recv, shares,
    z_send_sem, z_recv_sem, hop_send_sem, hop_recv_sem, a_send_sem, a_recv_sem, load_sem, export_sem,
    pair_sem, first_send_sem, first_recv_sem, second_send_sem, second_recv_sem, share_sem,
):
    bf16, f32 = jnp.bfloat16, jnp.float32
    t, me = lax.axis_index("tm"), lax.axis_index("ent")
    sections, ents = lax.axis_size("tm"), lax.axis_size("ent")
    rows, width = state.shape
    edges = slots = export_rows.shape[1]
    relations = rel_emb.shape[0]
    basis_count = basis.shape[1] // width
    share = slots // ents
    part = width // CHUNKS
    above = lax.rem(t + 1, sections)
    below = lax.rem(t + sections - 1, sections)

    barrier = pltpu.get_barrier_semaphore()

    def greet(k, carry):
        peer = lax.rem(me + k, ents)
        pl.semaphore_signal(barrier, inc=1, device_id=(t, peer), device_id_type=MESH)
        return carry

    lax.fori_loop(1, ents, greet, 0)
    pl.semaphore_signal(barrier, inc=1, device_id=(above, me), device_id_type=MESH)
    pl.semaphore_signal(barrier, inc=1, device_id=(below, me), device_id_type=MESH)
    opposite = lax.rem(t + 2, sections)
    pl.semaphore_signal(barrier, inc=1, device_id=(opposite, me), device_id_type=MESH)
    loads = [
        pltpu.make_async_copy(src, dst, load_sem.at[i])
        for i, (src, dst) in enumerate(
            [
                (rel_emb_hbm, rel_emb),
                (self_hbm, self_weight),
                (gate_hbm, gate_weight),
                (basis_hbm, basis),
                (cot_hbm, cot),
            ]
        )
    ]
    for load in loads:
        load.start()

    def pass_down(c):
        piece = pl.ds(0, rows - LONG_WAY[c])
        return pltpu.make_async_remote_copy(
            src_ref=sending.at[c, piece],
            dst_ref=handed.at[c, piece],
            send_sem=z_send_sem.at[c],
            recv_sem=z_recv_sem.at[c],
            device_id=(below, me),
            device_id_type=MESH,
        )

    def hop(c, leg):
        count = LONG_WAY[c]
        piece, held = pl.ds(rows - count, count), pl.ds(0, count)
        stops = [
            sending.at[c, piece], relay.at[0, c, held], relay.at[1, c, held], handed.at[c, piece]
        ]
        return pltpu.make_async_remote_copy(
            src_ref=stops[leg],
            dst_ref=stops[leg + 1],
            send_sem=hop_send_sem.at[leg, c],
            recv_sem=hop_recv_sem.at[leg, c],
            device_id=(above, me),
            device_id_type=MESH,
        )

    detours = [c for c in range(CHUNKS) if LONG_WAY[c] > 0]

    def pass_on(leg):
        for c in detours:
            hop(c, leg - 1).wait_recv()
            hop(c, leg).start()
        for c in detours:
            hop(c, leg).wait_send()

    def blocks(count, body):
        def step(i, carry):
            body(pl.ds(pl.multiple_of(i * BLOCK, BLOCK), BLOCK))
            return carry

        lax.fori_loop(0, count // BLOCK, step, 0)

    ids_row[...] = jnp.zeros_like(ids_row)
    live = lax.broadcasted_iota(jnp.int32, (1, edges), 1) < tile_count[...] * TILE
    ids_row[EXPORT : EXPORT + 1, :] = export_rows[...]
    ids_row[SOURCE : SOURCE + 1, :] = edge_src[...]
    ids_row[TARGET : TARGET + 1, :] = jnp.where(live, edge_dst[...], -1)
    ids_row[RELATION : RELATION + 1, :] = edge_rel[...]
    ids_col[...] = ids_row[...].T

    def one(mask):
        return jnp.where(mask, 1.0, 0.0).astype(bf16)

    def by_row(kind, r, count):
        lane = lax.broadcasted_iota(jnp.int32, (BLOCK, count), 1)
        return one(ids_col[r, kind : kind + 1] == lane)

    def by_column(kind, r):
        line = lax.broadcasted_iota(jnp.int32, (BLOCK, edges), 0) + r.start
        return one(ids_row[kind : kind + 1, :] == line)

    mine = pl.ds(pl.multiple_of(me * share, share), share)

    def export(r):
        export_send[r, :] = dot(by_row(EXPORT, r, rows), state[...]).astype(bf16)

    blocks(slots, export)
    pltpu.make_async_copy(export_send.at[mine], export_recv.at[mine], export_sem.at[1]).start()
    pl.semaphore_wait(barrier, ents + 2)

    def send_export(k, carry):
        peer = lax.rem(me + k, ents)
        pltpu.make_async_remote_copy(
            src_ref=export_send.at[pl.ds(pl.multiple_of(peer * share, share), share)],
            dst_ref=export_recv.at[mine],
            send_sem=export_sem.at[0],
            recv_sem=export_sem.at[1],
            device_id=(t, peer),
            device_id_type=MESH,
        ).start()
        return carry

    lax.fori_loop(1, ents, send_export, 0)
    for load in loads[:3]:
        load.wait()
    coef_parts[...] = jnp.zeros_like(coef_parts)
    coef_rows_in[...] = jnp.zeros_like(coef_rows_in)
    coef_rows_in[:basis_count, :] = coef_t[...]
    left_over = coef_rows_in[...].T
    for i in range(3):
        kept = left_over.astype(bf16).astype(f32)
        coef_parts[i, :, :8] = kept
        left_over = left_over - kept

    def by_edge(e):
        early[e, :] = by_row(SOURCE, e, slots)
        target[e, :] = by_row(TARGET, e, rows)
        relation = by_row(RELATION, e, relations)
        total[e, :] = dot(relation, rel_emb[...])
        edge_coef[e, :] = sum(
            dot(relation, coef_parts[i].astype(bf16)) for i in range(3)
        )

    blocks(edges, by_edge)

    def forms(r):
        exported_t[r, :] = by_column(TARGET, r)
        source_t[r, :] = by_column(SOURCE, r)
        state_grad[r, :] = dot(state[r, :], self_weight[...])
        keep[r, :] = jax.nn.sigmoid(dot(state[r, :], gate_weight[...]) + gate_bias[...])

    blocks(rows, forms)
    loads[3].wait()
    pltpu.make_async_copy(export_recv, export_recv, export_sem.at[1]).wait()

    def forward(e):
        value = (dot(early[e, :], export_recv[...]) + total[e, :]).astype(bf16)
        edge_input[e, :] = value
        message = 0.0
        for b in range(basis_count):
            at = slice(b * width, (b + 1) * width)
            image = dot(value, basis[:, at])
            images[e, at] = image.astype(bf16)
            message = message + edge_coef[e, b : b + 1] * image
        edge_grad[e, :] = message.astype(bf16)

    blocks(edges, forward)

    def factors(r):
        hot = exported_t[r, :]
        degree = 1.0 + dot(hot, jnp.ones((edges, 128), bf16))[:, :1]
        scale = 1.0 / degree
        aggregated = jnp.tanh((dot(hot, edge_grad[...]) + state_grad[r, :]) * scale)
        gate_open = keep[r, :]
        closed = 1.0 - gate_open
        row_factor[r, :] = gate_open * (1.0 - aggregated * aggregated) * scale
        gate_factor[r, :] = (aggregated - state[r, :].astype(f32)) * gate_open * closed
        keep[r, :] = closed

    blocks(rows, factors)
    loads[4].wait()

    def turned():
        def turn(r):
            input_t[:, r] = edge_input[r, :].T
            state_t[:, r] = state[r, :].T

        blocks(edges, turn)
        relation_line = lax.broadcasted_iota(jnp.int32, (relations, edges), 0)
        relation_t[...] = one(ids_row[RELATION : RELATION + 1, :] == relation_line)

    @pl.when(t < sections - 1)
    def _():
        turned()

    @pl.when(t == 0)
    def _():
        pass_on(1)

    @pl.when(t <= 1)
    def _():
        pass_on(2)

    for c in range(CHUNKS):
        cols = pl.ds(c * part, part)

        @pl.when(t < sections - 1)
        def _():
            pass_down(c).wait_recv()
            if c in detours:
                hop(c, 2).wait_recv()

        @pl.when(t == sections - 1)
        def _():
            handed[c] = jnp.zeros((rows, part), bf16)

        def elementwise(r):
            upstream = cot[r, cols].astype(f32) + handed[c, r, :].astype(f32)
            row_grad[r, cols] = (upstream * row_factor[r, cols]).astype(bf16)
            gate_row[r, cols] = (upstream * gate_factor[r, cols]).astype(bf16)
            state_grad[r, cols] = upstream * keep[r, cols]

        blocks(rows, elementwise)

        def through_basis(e):
            gathered = dot(target[e, :], row_grad[:, cols])
            edge_grad[e, cols] = gathered.astype(bf16)
            scales = [edge_coef[e, b : b + 1] for b in range(basis_count)]
            image_grad = [(scale * gathered).astype(bf16) for scale in scales]
            starts = [b * width + c * part for b in range(basis_count)]
            columns = [basis[:, start : start + part] for start in starts]
            out = dot(
                jnp.concatenate(image_grad, axis=1), jnp.concatenate(columns, axis=1), LAST
            )
            if c > 0:
                out = out + total[e, :]
            if c < CHUNKS - 1:
                total[e, :] = out
            else:
                input_grad[e, :] = out.astype(bf16)

        blocks(edges, through_basis)

    for c in range(CHUNKS):
        cols = pl.ds(c * part, part)

        def to_slots(r):
            slot_send[c, r, :] = dot(source_t[r, :], input_grad[:, cols]).astype(bf16)

        blocks(slots, to_slots)
        pltpu.make_async_copy(
            slot_send.at[c, mine], slot_recv.at[c, mine], a_recv_sem.at[c]
        ).start()

        def send(k, carry):
            peer = lax.rem(me + k, ents)
            pltpu.make_async_remote_copy(
                src_ref=slot_send.at[c, pl.ds(pl.multiple_of(peer * share, share), share)],
                dst_ref=slot_recv.at[c, mine],
                send_sem=a_send_sem.at[c],
                recv_sem=a_recv_sem.at[c],
                device_id=(t, peer),
                device_id_type=MESH,
            ).start()
            return carry

        lax.fori_loop(1, ents, send, 0)

    core = lax.rem(me, 2)
    y = lax.rem(me // 2, SIDE)
    x = me // (2 * SIDE)
    sibling = me + 1 - 2 * core
    half = width // 2

    def to_pair(offset):
        piece = pl.ds(offset, GROUP)
        return pltpu.make_async_remote_copy(
            src_ref=packed.at[1 - core, :, :, piece, :],
            dst_ref=pair_recv.at[:, :, piece, :],
            send_sem=pair_sem.at[0],
            recv_sem=pair_sem.at[1],
            device_id=(t, sibling),
            device_id_type=MESH,
        )

    def pack(offset, i, value):
        value = value.astype(bf16).reshape(SIDE, 2, GROUP, width)
        rows_at = pl.ds(offset, GROUP)
        for core_to in range(2):
            for y_to in range(SIDE):
                one = value[y_to, core_to]
                packed[core_to, 0, i * SIDE + y_to, rows_at, :] = one[:, :half]
                packed[core_to, 1, y_to * SIDE + i, rows_at, :] = one[:, half:]

    def term(offset, left, right):
        value = dot(left[...], right[...])
        for i in range(SIDE):
            pack(offset, i, value[i * 128 : (i + 1) * 128])
        to_pair(offset).start()

    def weights():
        @pl.when(t == sections - 1)
        def _():
            turned()

        for b in range(basis_count):

            def scale(e):
                scaled[e, :] = (edge_coef[e, b : b + 1] * edge_grad[e, :].astype(f32)).astype(bf16)

            blocks(edges, scale)
            term(b * GROUP, input_t, scaled)
        term(basis_count * GROUP, state_t, row_grad)
        term((basis_count + 1) * GROUP, state_t, gate_row)

        def inner(e):
            lane = lax.broadcasted_iota(jnp.int32, (BLOCK, 128), 1)
            out = jnp.zeros((BLOCK, 128), f32)
            gradient = edge_grad[e, :].astype(f32)
            for b in range(basis_count):
                product = gradient * images[e, b * width : (b + 1) * width].astype(f32)
                out = jnp.where(lane == b, jnp.sum(product, axis=1, keepdims=True), out)
            high = out.astype(bf16)
            coef_hi[e, :] = high
            coef_lo[e, :] = (out - high.astype(f32)).astype(bf16)

        blocks(edges, inner)
        bias = jnp.zeros((1, width), f32)
        for i in range(rows // BLOCK):
            piece = gate_row[i * BLOCK : (i + 1) * BLOCK, :].astype(f32)
            bias = bias + jnp.sum(piece, axis=0, keepdims=True)
        line = lax.broadcasted_iota(jnp.int32, (8, width - 128), 0)
        wrapped = jnp.concatenate([bias[:, width - 128 :]] * (width // 128 - 1), axis=1)
        tile = jnp.where(line == 0, bias[:, : width - 128], jnp.where(line == 1, wrapped, 0.0))
        small[:, 0:8, :] = dot(relation_t[...], input_grad[...]).reshape(ents, 8, width)
        coef_rows = dot(relation_t[...], coef_hi[...]) + dot(relation_t[...], coef_lo[...])
        small[:, 8:16, 0:128] = coef_rows.reshape(ents, 8, 128)
        small[:, 8:16, 128:] = jnp.broadcast_to(tile[None], (ents, 8, width - 128))

        def pack_small(i, carry):
            pack((basis_count + 2) * GROUP, i, small[pl.ds(i * 2 * SIDE, 2 * SIDE)])
            return carry

        lax.fori_loop(0, SIDE, pack_small, 0)
        to_pair((basis_count + 2) * GROUP).start()

    def local_part(r):
        state_grad[r, :] += dot(row_grad[r, :], self_weight[...], LAST) + dot(
            gate_row[r, :], gate_weight[...], LAST
        )
        exported_t[r, :] = by_column(EXPORT, r)

    def finish_rows(last):
        blocks(rows, local_part)
        for c in range(CHUNKS):
            cols = pl.ds(c * part, part)
            pltpu.make_async_copy(slot_recv.at[c], slot_recv.at[c], a_recv_sem.at[c]).wait()

            def to_rows(r):
                out = state_grad[r, cols] + dot(exported_t[r, :], slot_recv[c])
                state_grad[r, cols] = out
                if not last:
                    sending[c, r, :] = out.astype(bf16)

            blocks(rows, to_rows)
            if not last:
                if c in detours:
                    hop(c, 0).start()
                pass_down(c).start()

    @pl.when(t == 0)
    def _():
        weights()

    @pl.when(t > 0)
    def _():
        finish_rows(False)
        weights()

    @pl.when(t >= 2)
    def _():
        pass_on(1)

    @pl.when(t == 3)
    def _():
        pass_on(2)

    pltpu.make_async_copy(pair_recv, pair_recv, pair_sem.at[1]).wait()

    def chip(px, py):
        return (t, px * (2 * SIDE) + py * 2 + core)

    def other(h, k):
        return lax.rem((x if h == 0 else y) + k, SIDE)

    for h in range(2):

        def add_pair(i, carry):
            total_pair = packed[core, h, i].astype(f32) + pair_recv[h, i].astype(f32)
            packed[core, h, i] = total_pair.astype(bf16)
            return carry

        lax.fori_loop(0, SIDE * SIDE, add_pair, 0)
        for k in range(1, SIDE):
            to = other(h, k)
            pltpu.make_async_remote_copy(
                src_ref=packed.at[core, h, pl.ds(to * SIDE, SIDE)],
                dst_ref=first_recv.at[h, k - 1],
                send_sem=first_send_sem.at[h],
                recv_sem=first_recv_sem.at[h],
                device_id=chip(to, y) if h == 0 else chip(x, to),
                device_id_type=MESH,
            ).start()

    @pl.when(t == 0)
    def _():
        finish_rows(True)

    for h in range(2):
        pltpu.make_async_copy(first_recv.at[h], first_recv.at[h], first_recv_sem.at[h]).wait()

        def add_first(j, carry):
            out = packed[core, h, other(h, 0) * SIDE + j].astype(f32)
            for k in range(SIDE - 1):
                out = out + first_recv[h, k, j].astype(f32)
            first_sum[h, j] = out.astype(bf16)
            return carry

        lax.fori_loop(0, SIDE, add_first, 0)
        for k in range(1, SIDE):
            to = other(1 - h, k)
            pltpu.make_async_remote_copy(
                src_ref=first_sum.at[h, to],
                dst_ref=second_recv.at[h, k - 1],
                send_sem=second_send_sem.at[h],
                recv_sem=second_recv_sem.at[h],
                device_id=chip(x, to) if h == 0 else chip(to, y),
                device_id_type=MESH,
            ).start()

    for h in range(2):
        pltpu.make_async_copy(second_recv.at[h], second_recv.at[h], second_recv_sem.at[h]).wait()
        out = first_sum[h, other(1 - h, 0)].astype(f32)
        for k in range(SIDE - 1):
            out = out + second_recv[h, k].astype(f32)
        shares[t, h] = out.astype(bf16)
    for k in range(1, SIDE):
        pltpu.make_async_remote_copy(
            src_ref=shares.at[t],
            dst_ref=shares.at[t],
            send_sem=share_sem.at[0],
            recv_sem=share_sem.at[1],
            device_id=(lax.rem(t + k, sections), me),
            device_id_type=MESH,
        ).start()
    others = shares.at[pl.ds(0, sections - 1)]
    pltpu.make_async_copy(others, others, share_sem.at[1]).wait()
    for h in range(2):
        at = pl.ds(h * half, half)
        out = shares[0, h].astype(f32)
        for p in range(1, SIDE):
            out = out + shares[p, h].astype(f32)
        for b in range(basis_count):
            basis_out[:, b * width + h * half : b * width + (h + 1) * half] = out[
                b * GROUP : (b + 1) * GROUP
            ]
        top = basis_count * GROUP
        self_out[:, at] = out[top : top + GROUP]
        gate_out[:, at] = out[top + GROUP : top + 2 * GROUP]
        rel_out[:, at] = out[top + 2 * GROUP : top + 2 * GROUP + 8]
        rest = out[top + 2 * GROUP + 8 : top + 3 * GROUP]
        if h == 0:
            coef_out[...] = rest[:, :128]
            bias_out[:, : half - 128] = rest[:, 128:]
        else:
            bias_out[:, half - 128 :] = rest

    pltpu.make_async_copy(pair_recv, pair_recv, pair_sem.at[0]).wait()
    pltpu.make_async_copy(others, others, share_sem.at[0]).wait()
    for h in range(2):
        pltpu.make_async_copy(first_recv.at[h], first_recv.at[h], first_send_sem.at[h]).wait()
        pltpu.make_async_copy(second_recv.at[h], second_recv.at[h], second_send_sem.at[h]).wait()

    for c in range(CHUNKS):
        if c == 0:
            rest = export_send.at[pl.ds(0, slots - share)]
            pltpu.make_async_copy(rest, rest, export_sem.at[0]).wait()
        rest = slot_send.at[c, pl.ds(0, slots - share)]
        pltpu.make_async_copy(rest, rest, a_send_sem.at[c]).wait()

        @pl.when(t > 0)
        def _():
            pass_down(c).wait_send()
            if c in detours:
                hop(c, 0).wait_send()


def run_chain(*operands):
    bf16, f32 = jnp.bfloat16, jnp.float32
    rows, width = operands[0].shape
    edges = slots = operands[1].shape[1]
    basis_count, relations = operands[6].shape
    ents = lax.axis_size("ent")
    part, half = width // CHUNKS, width // 2
    height = (basis_count + 3) * GROUP
    shape = jax.ShapeDtypeStruct
    hop_sem = pltpu.SemaphoreType.DMA((3, CHUNKS))
    chunk_sem = pltpu.SemaphoreType.DMA((CHUNKS,))
    two = pltpu.SemaphoreType.DMA((2,))
    whole = pl.BlockSpec(memory_space=pltpu.VMEM)
    wide, flat, narrow = (
        pltpu.VMEM((rows, width), f32),
        pltpu.VMEM((rows, width), bf16),
        pltpu.VMEM((edges, 128), bf16),
    )
    hot = pltpu.VMEM((rows, edges), bf16)
    return pl.pallas_call(
        chain_kernel,
        out_shape=(
            shape((rows, width), f32),
            shape((GROUP, basis_count * width), f32),
            shape((GROUP, width), f32),
            shape((GROUP, width), f32),
            shape((8, width), f32),
            shape((8, 128), f32),
            shape((8, width - 128), f32),
        ),
        in_specs=[whole] * 8 + [pl.BlockSpec(memory_space=pl.ANY)] * 5,
        out_specs=(whole,) * 7,
        scratch_shapes=[
            flat,
            pltpu.VMEM((width, basis_count * width), bf16),
            pltpu.VMEM((relations, width), bf16),
            pltpu.VMEM((width, width), bf16),
            pltpu.VMEM((width, width), bf16),
            wide, wide, wide, hot, hot, hot, hot,
            pltpu.VMEM((edges, 128), f32),
            flat, flat, flat,
            pltpu.VMEM((8, edges), jnp.int32),
            pltpu.VMEM((edges, 8), jnp.int32),
            pltpu.VMEM((8, relations), f32),
            pltpu.VMEM((3, relations, 128), f32),
            flat, flat, flat, flat,
            pltpu.VMEM((CHUNKS, rows, part), bf16),
            pltpu.VMEM((CHUNKS, rows, part), bf16),
            pltpu.VMEM((2, CHUNKS, max(LONG_WAY), part), bf16),
            wide,
            pltpu.VMEM((CHUNKS, slots, part), bf16),
            pltpu.VMEM((CHUNKS, slots, part), bf16),
            pltpu.VMEM((edges, basis_count * width), bf16),
            pltpu.VMEM((width, edges), bf16),
            pltpu.VMEM((width, rows), bf16),
            pltpu.VMEM((relations, edges), bf16),
            flat, narrow, narrow,
            pltpu.VMEM((ents, GROUP, width), f32),
            pltpu.VMEM((2, 2, SIDE * SIDE, height, half), bf16),
            pltpu.VMEM((2, SIDE * SIDE, height, half), bf16),
            pltpu.VMEM((2, SIDE - 1, SIDE, height, half), bf16),
            pltpu.VMEM((2, SIDE, height, half), bf16),
            pltpu.VMEM((2, SIDE - 1, height, half), bf16),
            pltpu.VMEM((SIDE, 2, height, half), bf16),
            chunk_sem, chunk_sem, hop_sem, hop_sem, chunk_sem, chunk_sem,
            pltpu.SemaphoreType.DMA((5,)),
            two, two, two, two, two, two, two,
        ],
        compiler_params=pltpu.CompilerParams(
            collective_id=0, has_side_effects=True, vmem_limit_bytes=63 << 20
        ),
    )(*operands)


def write_kernel(*refs):
    count = len(refs) // 2
    refs[count][...] = refs[0][...]

    @pl.when(pl.program_id(0) == 0)
    def _():
        for i in range(1, count - 2):
            refs[count + i][...] = refs[i][...]
        coef_in, bias_in, coef_out, bias_out = (refs[i] for i in (count - 2, count - 1, -2, -1))
        coef_out[...] = coef_in[...].T[: coef_out.shape[0]]
        bias = bias_in[...]
        bias = jnp.concatenate([bias, jnp.roll(bias[:, :128], -1, axis=0)], axis=1)
        width = bias.shape[1]
        share = bias_out.shape[1]
        shift = lax.rem(width - lax.axis_index("ent") * share, width)
        bias_out[...] = pltpu.roll(bias, shift, 1)[:1, :share]


def write_out(basis_count, *arrays):
    rows, width = arrays[0].shape
    shapes = [array.shape for array in arrays]
    results = shapes[:-2] + [(basis_count, 8), (1, width // lax.axis_size("ent"))]

    def specs(sizes):
        rest = [pl.BlockSpec(size, lambda i: (0, 0)) for size in sizes[1:]]
        return [pl.BlockSpec((rows // PIECES, width), lambda i: (i, 0))] + rest

    return pl.pallas_call(
        write_kernel,
        grid=(PIECES,),
        out_shape=tuple(jax.ShapeDtypeStruct(size, jnp.float32) for size in results),
        in_specs=specs(shapes),
        out_specs=tuple(specs(results)),
    )(*arrays)


def per_device(
    states, cotangent, export_rows, edge_src, edge_dst, edge_rel, tile_count,
    basis, coef, rel_emb, self_weight, gate_weight, gate_bias,
):
    basis_count = coef.shape[1]
    sums = run_chain(
        states[0], export_rows, edge_src, edge_dst, edge_rel, tile_count, coef.T, gate_bias[None],
        cotangent[0], basis, rel_emb, self_weight, gate_weight,
    )
    state_grad, basis_sum, self_sum, gate_sum, rel_sum, coef_t, bias = write_out(basis_count, *sums)
    return state_grad[None], basis_sum, self_sum, gate_sum, bias[0], coef_t.T, rel_sum


def solution(mesh):
    placed = (P("tm", "ent", None),) * 2 + (P("tm", "ent"),) * 5 + (P(),) * 6
    return jax.shard_map(
        per_device,
        mesh=mesh,
        in_specs=placed,
        out_specs=(
            P("tm", "ent", None),
            P("ent", None),
            P("ent", None),
            P("ent", None),
            P("ent"),
            P("ent", None),
            P("ent", None),
        ),
        check_vma=False,
    )
```

```python
import jax
import jax.numpy as jnp
from jax import lax
from jax.experimental import pallas as pl
from jax.experimental.pallas import tpu as pltpu
from jax.sharding import PartitionSpec as P

TILE = 128
MESH = pl.DeviceIdType.MESH
CHUNKS = 4
BLOCK = 512
SIDE = 4
GROUP = 16
PIECES = 2
LONG_WAY = (256, 256, 256, 128)
EXPORT, SOURCE, TARGET, RELATION = range(4)
LAST = (((1,), (1,)), ((), ()))


def dot(a, b, dims=(((1,), (0,)), ((), ()))):
    return lax.dot_general(a, b, dims, preferred_element_type=jnp.float32)


def chain_kernel(
    state, export_rows, edge_src, edge_dst, edge_rel, tile_count, coef_t, gate_bias,
    cot_hbm, basis_hbm, rel_emb_hbm, self_hbm, gate_hbm,
    state_grad, basis_out, self_out, gate_out, rel_out, coef_out, bias_out,
    cot, basis, rel_emb, self_weight, gate_weight,
    row_factor, gate_factor, keep, target, source_t, early, exported_t, edge_coef,
    export_send, export_recv, edge_input, ids_row, ids_col, coef_rows_in, coef_parts,
    row_grad, gate_row, edge_grad, input_grad,
    handed, sending, relay, total, slot_send, slot_recv,
    images, input_t, state_t, relation_t, scaled, coef_hi, coef_lo, small,
    packed, pair_recv, first_recv, first_sum, second_recv, shares,
    z_send_sem, z_recv_sem, hop_send_sem, hop_recv_sem, a_send_sem, a_recv_sem, load_sem, export_sem,
    pair_sem, first_send_sem, first_recv_sem, second_send_sem, second_recv_sem, share_sem,
):
    bf16, f32 = jnp.bfloat16, jnp.float32
    t, me = lax.axis_index("tm"), lax.axis_index("ent")
    sections, ents = lax.axis_size("tm"), lax.axis_size("ent")
    rows, width = state.shape
    edges = slots = export_rows.shape[1]
    relations = rel_emb.shape[0]
    basis_count = basis.shape[1] // width
    share = slots // ents
    part = width // CHUNKS
    above = lax.rem(t + 1, sections)
    below = lax.rem(t + sections - 1, sections)

    barrier = pltpu.get_barrier_semaphore()

    def greet(k, carry):
        peer = lax.rem(me + k, ents)
        pl.semaphore_signal(barrier, inc=1, device_id=(t, peer), device_id_type=MESH)
        return carry

    lax.fori_loop(1, ents, greet, 0)
    pl.semaphore_signal(barrier, inc=1, device_id=(above, me), device_id_type=MESH)
    pl.semaphore_signal(barrier, inc=1, device_id=(below, me), device_id_type=MESH)
    opposite = lax.rem(t + 2, sections)
    pl.semaphore_signal(barrier, inc=1, device_id=(opposite, me), device_id_type=MESH)
    loads = [
        pltpu.make_async_copy(src, dst, load_sem.at[i])
        for i, (src, dst) in enumerate(
            [
                (rel_emb_hbm, rel_emb),
                (self_hbm, self_weight),
                (gate_hbm, gate_weight),
                (basis_hbm, basis),
                (cot_hbm, cot),
            ]
        )
    ]
    for load in loads:
        load.start()

    def pass_down(c):
        piece = pl.ds(0, rows - LONG_WAY[c])
        return pltpu.make_async_remote_copy(
            src_ref=sending.at[c, piece],
            dst_ref=handed.at[c, piece],
            send_sem=z_send_sem.at[c],
            recv_sem=z_recv_sem.at[c],
            device_id=(below, me),
            device_id_type=MESH,
        )

    def hop(c, leg):
        count = LONG_WAY[c]
        piece, held = pl.ds(rows - count, count), pl.ds(0, count)
        stops = [
            sending.at[c, piece], relay.at[0, c, held], relay.at[1, c, held], handed.at[c, piece]
        ]
        return pltpu.make_async_remote_copy(
            src_ref=stops[leg],
            dst_ref=stops[leg + 1],
            send_sem=hop_send_sem.at[leg, c],
            recv_sem=hop_recv_sem.at[leg, c],
            device_id=(above, me),
            device_id_type=MESH,
        )

    detours = [c for c in range(CHUNKS) if LONG_WAY[c] > 0]

    def pass_on(leg):
        for c in detours:
            hop(c, leg - 1).wait_recv()
            hop(c, leg).start()
        for c in detours:
            hop(c, leg).wait_send()

    def blocks(count, body):
        def step(i, carry):
            body(pl.ds(pl.multiple_of(i * BLOCK, BLOCK), BLOCK))
            return carry

        lax.fori_loop(0, count // BLOCK, step, 0)

    ids_row[...] = jnp.zeros_like(ids_row)
    live = lax.broadcasted_iota(jnp.int32, (1, edges), 1) < tile_count[...] * TILE
    ids_row[EXPORT : EXPORT + 1, :] = export_rows[...]
    ids_row[SOURCE : SOURCE + 1, :] = edge_src[...]
    ids_row[TARGET : TARGET + 1, :] = jnp.where(live, edge_dst[...], -1)
    ids_row[RELATION : RELATION + 1, :] = edge_rel[...]
    ids_col[...] = ids_row[...].T

    def one(mask):
        return jnp.where(mask, 1.0, 0.0).astype(bf16)

    def by_row(kind, r, count):
        lane = lax.broadcasted_iota(jnp.int32, (BLOCK, count), 1)
        return one(ids_col[r, kind : kind + 1] == lane)

    def by_column(kind, r):
        line = lax.broadcasted_iota(jnp.int32, (BLOCK, edges), 0) + r.start
        return one(ids_row[kind : kind + 1, :] == line)

    mine = pl.ds(pl.multiple_of(me * share, share), share)

    def export(r):
        export_send[r, :] = dot(by_row(EXPORT, r, rows), state[...]).astype(bf16)

    blocks(slots, export)
    pltpu.make_async_copy(export_send.at[mine], export_recv.at[mine], export_sem.at[1]).start()
    pl.semaphore_wait(barrier, ents + 2)

    def send_export(k, carry):
        peer = lax.rem(me + k, ents)
        pltpu.make_async_remote_copy(
            src_ref=export_send.at[pl.ds(pl.multiple_of(peer * share, share), share)],
            dst_ref=export_recv.at[mine],
            send_sem=export_sem.at[0],
            recv_sem=export_sem.at[1],
            device_id=(t, peer),
            device_id_type=MESH,
        ).start()
        return carry

    lax.fori_loop(1, ents, send_export, 0)
    for load in loads[:3]:
        load.wait()
    coef_parts[...] = jnp.zeros_like(coef_parts)
    coef_rows_in[...] = jnp.zeros_like(coef_rows_in)
    coef_rows_in[:basis_count, :] = coef_t[...]
    left_over = coef_rows_in[...].T
    for i in range(3):
        kept = left_over.astype(bf16).astype(f32)
        coef_parts[i, :, :8] = kept
        left_over = left_over - kept

    def by_edge(e):
        early[e, :] = by_row(SOURCE, e, slots)
        target[e, :] = by_row(TARGET, e, rows)
        relation = by_row(RELATION, e, relations)
        total[e, :] = dot(relation, rel_emb[...])
        edge_coef[e, :] = sum(
            dot(relation, coef_parts[i].astype(bf16)) for i in range(3)
        )

    blocks(edges, by_edge)

    def forms(r):
        exported_t[r, :] = by_column(TARGET, r)
        source_t[r, :] = by_column(SOURCE, r)
        state_grad[r, :] = dot(state[r, :], self_weight[...])
        keep[r, :] = jax.nn.sigmoid(dot(state[r, :], gate_weight[...]) + gate_bias[...])

    blocks(rows, forms)
    loads[3].wait()
    pltpu.make_async_copy(export_recv, export_recv, export_sem.at[1]).wait()

    def forward(e):
        value = (dot(early[e, :], export_recv[...]) + total[e, :]).astype(bf16)
        edge_input[e, :] = value
        message = 0.0
        for b in range(basis_count):
            at = slice(b * width, (b + 1) * width)
            image = dot(value, basis[:, at])
            images[e, at] = image.astype(bf16)
            message = message + edge_coef[e, b : b + 1] * image
        edge_grad[e, :] = message.astype(bf16)

    blocks(edges, forward)

    def factors(r):
        hot = exported_t[r, :]
        degree = 1.0 + dot(hot, jnp.ones((edges, 128), bf16))[:, :1]
        scale = 1.0 / degree
        aggregated = jnp.tanh((dot(hot, edge_grad[...]) + state_grad[r, :]) * scale)
        gate_open = keep[r, :]
        closed = 1.0 - gate_open
        row_factor[r, :] = gate_open * (1.0 - aggregated * aggregated) * scale
        gate_factor[r, :] = (aggregated - state[r, :].astype(f32)) * gate_open * closed
        keep[r, :] = closed

    blocks(rows, factors)
    loads[4].wait()

    def turned():
        def turn(r):
            input_t[:, r] = edge_input[r, :].T
            state_t[:, r] = state[r, :].T

        blocks(edges, turn)
        relation_line = lax.broadcasted_iota(jnp.int32, (relations, edges), 0)
        relation_t[...] = one(ids_row[RELATION : RELATION + 1, :] == relation_line)

    @pl.when(t < sections - 1)
    def _():
        turned()

    @pl.when(t == 0)
    def _():
        pass_on(1)

    @pl.when(t <= 1)
    def _():
        pass_on(2)

    for c in range(CHUNKS):
        cols = pl.ds(c * part, part)

        @pl.when(t < sections - 1)
        def _():
            pass_down(c).wait_recv()
            if c in detours:
                hop(c, 2).wait_recv()

        @pl.when(t == sections - 1)
        def _():
            handed[c] = jnp.zeros((rows, part), bf16)

        def elementwise(r):
            upstream = cot[r, cols].astype(f32) + handed[c, r, :].astype(f32)
            row_grad[r, cols] = (upstream * row_factor[r, cols]).astype(bf16)
            gate_row[r, cols] = (upstream * gate_factor[r, cols]).astype(bf16)
            state_grad[r, cols] = upstream * keep[r, cols]

        blocks(rows, elementwise)

        def through_basis(e):
            gathered = dot(target[e, :], row_grad[:, cols])
            edge_grad[e, cols] = gathered.astype(bf16)
            scales = [edge_coef[e, b : b + 1] for b in range(basis_count)]
            image_grad = [(scale * gathered).astype(bf16) for scale in scales]
            starts = [b * width + c * part for b in range(basis_count)]
            columns = [basis[:, start : start + part] for start in starts]
            out = dot(
                jnp.concatenate(image_grad, axis=1), jnp.concatenate(columns, axis=1), LAST
            )
            if c > 0:
                out = out + total[e, :]
            if c < CHUNKS - 1:
                total[e, :] = out
            else:
                input_grad[e, :] = out.astype(bf16)

        blocks(edges, through_basis)

    for c in range(CHUNKS):
        cols = pl.ds(c * part, part)

        def to_slots(r):
            pair = dot(source_t[r, :], input_grad[:, c * part : (c + 2) * part]).astype(bf16)
            slot_send[c, r, :] = pair[:, :part]
            slot_send[c + 1, r, :] = pair[:, part:]

        if c % 2 == 0:
            blocks(slots, to_slots)
        pltpu.make_async_copy(
            slot_send.at[c, mine], slot_recv.at[c, mine], a_recv_sem.at[c]
        ).start()

        def send(k, carry):
            peer = lax.rem(me + k, ents)
            pltpu.make_async_remote_copy(
                src_ref=slot_send.at[c, pl.ds(pl.multiple_of(peer * share, share), share)],
                dst_ref=slot_recv.at[c, mine],
                send_sem=a_send_sem.at[c],
                recv_sem=a_recv_sem.at[c],
                device_id=(t, peer),
                device_id_type=MESH,
            ).start()
            return carry

        lax.fori_loop(1, ents, send, 0)

    core = lax.rem(me, 2)
    y = lax.rem(me // 2, SIDE)
    x = me // (2 * SIDE)
    sibling = me + 1 - 2 * core
    half = width // 2

    def to_pair(offset):
        piece = pl.ds(offset, GROUP)
        return pltpu.make_async_remote_copy(
            src_ref=packed.at[1 - core, :, :, piece, :],
            dst_ref=pair_recv.at[:, :, piece, :],
            send_sem=pair_sem.at[0],
            recv_sem=pair_sem.at[1],
            device_id=(t, sibling),
            device_id_type=MESH,
        )

    def pack(offset, i, value):
        value = value.astype(bf16).reshape(SIDE, 2, GROUP, width)
        rows_at = pl.ds(offset, GROUP)
        for core_to in range(2):
            for y_to in range(SIDE):
                one = value[y_to, core_to]
                packed[core_to, 0, i * SIDE + y_to, rows_at, :] = one[:, :half]
                packed[core_to, 1, y_to * SIDE + i, rows_at, :] = one[:, half:]

    def term(offset, left, right):
        value = dot(left[...], right[...])
        for i in range(SIDE):
            pack(offset, i, value[i * 128 : (i + 1) * 128])
        to_pair(offset).start()

    def weights():
        @pl.when(t == sections - 1)
        def _():
            turned()

        for b in range(basis_count):

            def scale(e):
                scaled[e, :] = (edge_coef[e, b : b + 1] * edge_grad[e, :].astype(f32)).astype(bf16)

            blocks(edges, scale)
            term(b * GROUP, input_t, scaled)
        term(basis_count * GROUP, state_t, row_grad)
        term((basis_count + 1) * GROUP, state_t, gate_row)

        def inner(e):
            lane = lax.broadcasted_iota(jnp.int32, (BLOCK, 128), 1)
            out = jnp.zeros((BLOCK, 128), f32)
            gradient = edge_grad[e, :].astype(f32)
            for b in range(basis_count):
                product = gradient * images[e, b * width : (b + 1) * width].astype(f32)
                out = jnp.where(lane == b, jnp.sum(product, axis=1, keepdims=True), out)
            high = out.astype(bf16)
            coef_hi[e, :] = high
            coef_lo[e, :] = (out - high.astype(f32)).astype(bf16)

        blocks(edges, inner)
        bias = jnp.zeros((1, width), f32)
        for i in range(rows // BLOCK):
            piece = gate_row[i * BLOCK : (i + 1) * BLOCK, :].astype(f32)
            bias = bias + jnp.sum(piece, axis=0, keepdims=True)
        line = lax.broadcasted_iota(jnp.int32, (8, width - 128), 0)
        wrapped = jnp.concatenate([bias[:, width - 128 :]] * (width // 128 - 1), axis=1)
        tile = jnp.where(line == 0, bias[:, : width - 128], jnp.where(line == 1, wrapped, 0.0))
        small[:, 0:8, :] = dot(relation_t[...], input_grad[...]).reshape(ents, 8, width)
        coef_rows = dot(relation_t[...], coef_hi[...]) + dot(relation_t[...], coef_lo[...])
        small[:, 8:16, 0:128] = coef_rows.reshape(ents, 8, 128)
        small[:, 8:16, 128:] = jnp.broadcast_to(tile[None], (ents, 8, width - 128))

        def pack_small(i, carry):
            pack((basis_count + 2) * GROUP, i, small[pl.ds(i * 2 * SIDE, 2 * SIDE)])
            return carry

        lax.fori_loop(0, SIDE, pack_small, 0)
        to_pair((basis_count + 2) * GROUP).start()

    def local_part(r):
        state_grad[r, :] += dot(row_grad[r, :], self_weight[...], LAST) + dot(
            gate_row[r, :], gate_weight[...], LAST
        )
        exported_t[r, :] = by_column(EXPORT, r)

    def finish_rows(last):
        blocks(rows, local_part)
        for c in range(CHUNKS):
            cols = pl.ds(c * part, part)
            pltpu.make_async_copy(slot_recv.at[c], slot_recv.at[c], a_recv_sem.at[c]).wait()

            def to_rows(r):
                out = state_grad[r, cols] + dot(exported_t[r, :], slot_recv[c])
                state_grad[r, cols] = out
                if not last:
                    sending[c, r, :] = out.astype(bf16)

            blocks(rows, to_rows)
            if not last:
                if c in detours:
                    hop(c, 0).start()
                pass_down(c).start()

    @pl.when(t == 0)
    def _():
        weights()

    @pl.when(t > 0)
    def _():
        finish_rows(False)
        weights()

    @pl.when(t >= 2)
    def _():
        pass_on(1)

    @pl.when(t == 3)
    def _():
        pass_on(2)

    pltpu.make_async_copy(pair_recv, pair_recv, pair_sem.at[1]).wait()

    def chip(px, py):
        return (t, px * (2 * SIDE) + py * 2 + core)

    def other(h, k):
        return lax.rem((x if h == 0 else y) + k, SIDE)

    for h in range(2):

        def add_pair(i, carry):
            total_pair = packed[core, h, i].astype(f32) + pair_recv[h, i].astype(f32)
            packed[core, h, i] = total_pair.astype(bf16)
            return carry

        lax.fori_loop(0, SIDE * SIDE, add_pair, 0)
        for k in range(1, SIDE):
            to = other(h, k)
            pltpu.make_async_remote_copy(
                src_ref=packed.at[core, h, pl.ds(to * SIDE, SIDE)],
                dst_ref=first_recv.at[h, k - 1],
                send_sem=first_send_sem.at[h],
                recv_sem=first_recv_sem.at[h],
                device_id=chip(to, y) if h == 0 else chip(x, to),
                device_id_type=MESH,
            ).start()

    @pl.when(t == 0)
    def _():
        finish_rows(True)

    for h in range(2):
        pltpu.make_async_copy(first_recv.at[h], first_recv.at[h], first_recv_sem.at[h]).wait()

        def add_first(j, carry):
            out = packed[core, h, other(h, 0) * SIDE + j].astype(f32)
            for k in range(SIDE - 1):
                out = out + first_recv[h, k, j].astype(f32)
            first_sum[h, j] = out.astype(bf16)
            return carry

        lax.fori_loop(0, SIDE, add_first, 0)
        for k in range(1, SIDE):
            to = other(1 - h, k)
            pltpu.make_async_remote_copy(
                src_ref=first_sum.at[h, to],
                dst_ref=second_recv.at[h, k - 1],
                send_sem=second_send_sem.at[h],
                recv_sem=second_recv_sem.at[h],
                device_id=chip(x, to) if h == 0 else chip(to, y),
                device_id_type=MESH,
            ).start()

    for h in range(2):
        pltpu.make_async_copy(second_recv.at[h], second_recv.at[h], second_recv_sem.at[h]).wait()
        out = first_sum[h, other(1 - h, 0)].astype(f32)
        for k in range(SIDE - 1):
            out = out + second_recv[h, k].astype(f32)
        shares[t, h] = out.astype(bf16)
    for k in range(1, SIDE):
        pltpu.make_async_remote_copy(
            src_ref=shares.at[t],
            dst_ref=shares.at[t],
            send_sem=share_sem.at[0],
            recv_sem=share_sem.at[1],
            device_id=(lax.rem(t + k, sections), me),
            device_id_type=MESH,
        ).start()
    others = shares.at[pl.ds(0, sections - 1)]
    pltpu.make_async_copy(others, others, share_sem.at[1]).wait()
    for h in range(2):
        at = pl.ds(h * half, half)
        out = shares[0, h].astype(f32)
        for p in range(1, SIDE):
            out = out + shares[p, h].astype(f32)
        for b in range(basis_count):
            basis_out[:, b * width + h * half : b * width + (h + 1) * half] = out[
                b * GROUP : (b + 1) * GROUP
            ]
        top = basis_count * GROUP
        self_out[:, at] = out[top : top + GROUP]
        gate_out[:, at] = out[top + GROUP : top + 2 * GROUP]
        rel_out[:, at] = out[top + 2 * GROUP : top + 2 * GROUP + 8]
        rest = out[top + 2 * GROUP + 8 : top + 3 * GROUP]
        if h == 0:
            coef_out[...] = rest[:, :128]
            bias_out[:, : half - 128] = rest[:, 128:]
        else:
            bias_out[:, half - 128 :] = rest

    pltpu.make_async_copy(pair_recv, pair_recv, pair_sem.at[0]).wait()
    pltpu.make_async_copy(others, others, share_sem.at[0]).wait()
    for h in range(2):
        pltpu.make_async_copy(first_recv.at[h], first_recv.at[h], first_send_sem.at[h]).wait()
        pltpu.make_async_copy(second_recv.at[h], second_recv.at[h], second_send_sem.at[h]).wait()

    for c in range(CHUNKS):
        if c == 0:
            rest = export_send.at[pl.ds(0, slots - share)]
            pltpu.make_async_copy(rest, rest, export_sem.at[0]).wait()
        rest = slot_send.at[c, pl.ds(0, slots - share)]
        pltpu.make_async_copy(rest, rest, a_send_sem.at[c]).wait()

        @pl.when(t > 0)
        def _():
            pass_down(c).wait_send()
            if c in detours:
                hop(c, 0).wait_send()


def run_chain(*operands):
    bf16, f32 = jnp.bfloat16, jnp.float32
    rows, width = operands[0].shape
    edges = slots = operands[1].shape[1]
    basis_count, relations = operands[6].shape
    ents = lax.axis_size("ent")
    part, half = width // CHUNKS, width // 2
    height = (basis_count + 3) * GROUP
    shape = jax.ShapeDtypeStruct
    hop_sem = pltpu.SemaphoreType.DMA((3, CHUNKS))
    chunk_sem = pltpu.SemaphoreType.DMA((CHUNKS,))
    two = pltpu.SemaphoreType.DMA((2,))
    whole = pl.BlockSpec(memory_space=pltpu.VMEM)
    wide, flat, narrow = (
        pltpu.VMEM((rows, width), f32),
        pltpu.VMEM((rows, width), bf16),
        pltpu.VMEM((edges, 128), bf16),
    )
    hot = pltpu.VMEM((rows, edges), bf16)
    return pl.pallas_call(
        chain_kernel,
        out_shape=(
            shape((rows, width), f32),
            shape((GROUP, basis_count * width), f32),
            shape((GROUP, width), f32),
            shape((GROUP, width), f32),
            shape((8, width), f32),
            shape((8, 128), f32),
            shape((8, width - 128), f32),
        ),
        in_specs=[whole] * 8 + [pl.BlockSpec(memory_space=pl.ANY)] * 5,
        out_specs=(whole,) * 7,
        scratch_shapes=[
            flat,
            pltpu.VMEM((width, basis_count * width), bf16),
            pltpu.VMEM((relations, width), bf16),
            pltpu.VMEM((width, width), bf16),
            pltpu.VMEM((width, width), bf16),
            wide, wide, wide, hot, hot, hot, hot,
            pltpu.VMEM((edges, 128), f32),
            flat, flat, flat,
            pltpu.VMEM((8, edges), jnp.int32),
            pltpu.VMEM((edges, 8), jnp.int32),
            pltpu.VMEM((8, relations), f32),
            pltpu.VMEM((3, relations, 128), f32),
            flat, flat, flat, flat,
            pltpu.VMEM((CHUNKS, rows, part), bf16),
            pltpu.VMEM((CHUNKS, rows, part), bf16),
            pltpu.VMEM((2, CHUNKS, max(LONG_WAY), part), bf16),
            wide,
            pltpu.VMEM((CHUNKS, slots, part), bf16),
            pltpu.VMEM((CHUNKS, slots, part), bf16),
            pltpu.VMEM((edges, basis_count * width), bf16),
            pltpu.VMEM((width, edges), bf16),
            pltpu.VMEM((width, rows), bf16),
            pltpu.VMEM((relations, edges), bf16),
            flat, narrow, narrow,
            pltpu.VMEM((ents, GROUP, width), f32),
            pltpu.VMEM((2, 2, SIDE * SIDE, height, half), bf16),
            pltpu.VMEM((2, SIDE * SIDE, height, half), bf16),
            pltpu.VMEM((2, SIDE - 1, SIDE, height, half), bf16),
            pltpu.VMEM((2, SIDE, height, half), bf16),
            pltpu.VMEM((2, SIDE - 1, height, half), bf16),
            pltpu.VMEM((SIDE, 2, height, half), bf16),
            chunk_sem, chunk_sem, hop_sem, hop_sem, chunk_sem, chunk_sem,
            pltpu.SemaphoreType.DMA((5,)),
            two, two, two, two, two, two, two,
        ],
        compiler_params=pltpu.CompilerParams(
            collective_id=0, has_side_effects=True, vmem_limit_bytes=63 << 20
        ),
    )(*operands)


def write_kernel(*refs):
    count = len(refs) // 2
    refs[count][...] = refs[0][...]

    @pl.when(pl.program_id(0) == 0)
    def _():
        for i in range(1, count - 2):
            refs[count + i][...] = refs[i][...]
        coef_in, bias_in, coef_out, bias_out = (refs[i] for i in (count - 2, count - 1, -2, -1))
        coef_out[...] = coef_in[...].T[: coef_out.shape[0]]
        bias = bias_in[...]
        bias = jnp.concatenate([bias, jnp.roll(bias[:, :128], -1, axis=0)], axis=1)
        width = bias.shape[1]
        share = bias_out.shape[1]
        shift = lax.rem(width - lax.axis_index("ent") * share, width)
        bias_out[...] = pltpu.roll(bias, shift, 1)[:1, :share]


def write_out(basis_count, *arrays):
    rows, width = arrays[0].shape
    shapes = [array.shape for array in arrays]
    results = shapes[:-2] + [(basis_count, 8), (1, width // lax.axis_size("ent"))]

    def specs(sizes):
        rest = [pl.BlockSpec(size, lambda i: (0, 0)) for size in sizes[1:]]
        return [pl.BlockSpec((rows // PIECES, width), lambda i: (i, 0))] + rest

    return pl.pallas_call(
        write_kernel,
        grid=(PIECES,),
        out_shape=tuple(jax.ShapeDtypeStruct(size, jnp.float32) for size in results),
        in_specs=specs(shapes),
        out_specs=tuple(specs(results)),
    )(*arrays)


def per_device(
    states, cotangent, export_rows, edge_src, edge_dst, edge_rel, tile_count,
    basis, coef, rel_emb, self_weight, gate_weight, gate_bias,
):
    basis_count = coef.shape[1]
    sums = run_chain(
        states[0], export_rows, edge_src, edge_dst, edge_rel, tile_count, coef.T, gate_bias[None],
        cotangent[0], basis, rel_emb, self_weight, gate_weight,
    )
    state_grad, basis_sum, self_sum, gate_sum, rel_sum, coef_t, bias = write_out(basis_count, *sums)
    return state_grad[None], basis_sum, self_sum, gate_sum, bias[0], coef_t.T, rel_sum


def solution(mesh):
    placed = (P("tm", "ent", None),) * 2 + (P("tm", "ent"),) * 5 + (P(),) * 6
    return jax.shard_map(
        per_device,
        mesh=mesh,
        in_specs=placed,
        out_specs=(
            P("tm", "ent", None),
            P("ent", None),
            P("ent", None),
            P("ent", None),
            P("ent"),
            P("ent", None),
            P("ent", None),
        ),
        check_vma=False,
    )
```
